256 devices in a mesh: row: 16 (over y, x), col: 16 (over z, core).
Axes of the slice: x: 4, y: 4, z: 8, core: 2. Of those that a mesh axis runs over, the one named last changes fastest.
Arguments:
- features: bfloat16 [512, 512, 128], P('col')
- diag_inverse: bfloat16 [512, 128, 128], P('col')
- precision_tiles: float32 [16, 16, 32, 128, 128], P('row', 'col'), may hold values from -3 to 3
- inverse_tiles: float32 [16, 16, 32, 128, 128], P('row', 'col'), may hold values from -0.3125 to 0.3125
- slot_rows: int32 [16, 16, 32], replicated, may hold values from 0 to 511, as said below
- slot_columns: int32 [16, 16, 32], replicated, may hold values from 0 to 1, as said below
- owned_columns: int32 [16, 16, 2], replicated, may hold values from 0 to 511, as said below
- live_counts: int32 [16, 16], replicated, may hold values from 1 to 32, as said below
Outputs:
- direction: float32 [16, 16, 32, 128, 128], P('row', 'col')
The draws below stay inside these ranges and needn't reach their ends.
Inputs may be any that keep to these rules, and one draw needn't show every extreme that they name: `slot_rows`: slot k of every owner names a block-row held by index k // 2 of col, that is one of feature blocks 32 * (k // 2) to 32 * (k // 2) + 31; no pair of block-row and block-column is named by two slots of the whole grid. `slot_columns`: some owner uses every entry of its list. `owned_columns`: an owner's 2 block-columns are distinct and lie among the feature blocks of its own index of col. The live slots of an owner are slots 0 to live_counts - 1; some owner has all 32 slots live.
All inputs are finite; a program needn't handle non-finite values.
Results may differ from the reference program's by a relative error of at most 0.0003.
Values may be sent and summed in bfloat16 or wider, within the bound.
No kernel may reach another device: no remote copies, remote signals or barrier semaphores. Data moves between devices by JAX's collectives and lax.ppermute only.
A program may use at most 128 MiB of HBM per device.

```python
import jax
import jax.numpy as jnp
from jax import lax

BS = 128
FB = 32
NSAMP = 512
CAPP = 2
JD = 2
SWEEPS = 4
CAP = 32
NB = 512
N_ROW = 16
N_COL = 16


module_count = 16


def permute_blocks(subkey):
    return jax.random.permutation(subkey, FB)


def index_tables(key):
    base = jax.random.fold_in(key, 29)
    subkeys = jax.random.split(base, 6)
    perm_keys = jax.random.split(subkeys[0], N_COL * N_COL)
    orders = jax.vmap(permute_blocks)(perm_keys).reshape(N_COL, N_COL, FB)
    orders = (orders - orders[:, :, :1] + FB - 1) % FB
    slot_index = jnp.arange(CAP)
    source = slot_index // CAPP
    within = slot_index % CAPP
    pick_index = jnp.arange(N_ROW)[:, None] * CAPP + within[None, :]
    offsets = orders[jnp.arange(N_COL)[None, :, None], source[None, None, :], pick_index[:, None, :]]
    block_rows = source[None, None, :] * FB + offsets
    own_keys = jax.random.split(subkeys[1], N_ROW * N_COL)
    owned_orders = jax.vmap(permute_blocks)(own_keys).reshape(N_ROW, N_COL, FB)
    rotated = (owned_orders - owned_orders[:, :, :1] + FB - 1) % FB
    first_row = (jnp.arange(N_ROW) == 0)[:, None, None]
    owned_orders = jnp.where(first_row, rotated, owned_orders)
    owned_cols = owned_orders[:, :, :JD] + jnp.arange(N_COL)[None, :, None] * FB
    list_index = jax.random.randint(subkeys[2], (N_ROW, N_COL, CAP), 0, JD)
    list_index = jnp.where(slot_index[None, None, :] < JD, slot_index[None, None, :], list_index)
    shifts = jax.random.randint(subkeys[3], (N_ROW, N_COL), 0, 4)
    base_counts = jnp.right_shift(jnp.full((N_ROW, N_COL), CAP, jnp.int32), shifts)
    trimmed = jax.random.randint(subkeys[4], (N_ROW, N_COL), 0, base_counts // 4 + 1)
    counts = base_counts - trimmed
    fullest = jax.random.randint(subkeys[5], (), 0, N_ROW * N_COL)
    counts = jnp.where(jnp.arange(N_ROW * N_COL).reshape(N_ROW, N_COL) == fullest, CAP, counts)
    return (block_rows.astype(jnp.int32), list_index.astype(jnp.int32), owned_cols.astype(jnp.int32), counts.astype(jnp.int32))


def draw_slot_rows(key, part):
    return index_tables(key)[0]


def draw_slot_columns(key, part):
    return index_tables(key)[1]


def draw_owned_columns(key, part):
    return index_tables(key)[2]


def draw_live_counts(key, part):
    return index_tables(key)[3]


def draw_features(key, part):
    subkeys = jax.random.split(jax.random.fold_in(key, 3), 4)
    factors = jax.random.normal(subkeys[0], (module_count, NSAMP), jnp.float32)
    module = jax.random.randint(subkeys[1], (NB, BS), 0, module_count)
    loading = jax.random.uniform(subkeys[2], (NB, BS), jnp.float32, -0.7, 0.7)
    noise_part = jax.random.normal(subkeys[3], (NB, NSAMP, BS), jnp.float32)
    shared = jnp.swapaxes(jnp.take(factors, module, axis=0), 1, 2)
    values = loading[:, None, :] * shared + jnp.sqrt(1.0 - loading * loading)[:, None, :] * noise_part
    return values.astype(jnp.bfloat16)


def draw_diag_inverse(key, part):
    subkeys = jax.random.split(jax.random.fold_in(key, 5), 2)
    identity = jnp.eye(BS, dtype=jnp.float32)
    diagonal = jax.random.uniform(subkeys[0], (NB, BS), jnp.float32, 0.7, 1.1)
    spread = 0.25 * jax.random.normal(subkeys[1], (NB, BS, BS), jnp.float32) / BS ** 0.5
    values = diagonal[:, :, None] * identity[None, :, :] + spread * (1.0 - identity[None, :, :])
    return values.astype(jnp.bfloat16)


def shard_levels(own_key, extent, cuts, least, top_value):
    factor_of = 1.0
    for dim, blocks in cuts:
        draws = jax.random.uniform(jax.random.fold_in(jax.random.fold_in(own_key, 6), dim), (blocks,), jnp.float32, least / len(cuts), top_value / len(cuts))
        factor_of = factor_of * jnp.repeat(jnp.exp(draws), extent[dim] // blocks).reshape((-1,) + (1,) * (len(extent) - 1 - dim))
    return factor_of


def normal_values(stream_key, dims, scale, most, cuts=(), kind=jnp.bfloat16):
    factor_of = shard_levels(stream_key, dims, cuts, -0.22, 0.18) if cuts else 1.0
    result = jax.random.normal(stream_key, dims, jnp.float32) * scale * factor_of
    return jnp.minimum(jnp.maximum(result, -most), most).astype(kind)


def setup_inputs(seed: int = 0) -> dict:
    key_list = jax.random.split(jax.random.key(seed), 9)
    return {
        "features": draw_features(jax.random.fold_in(key_list[8], 71), 0),
        "diag_inverse": draw_diag_inverse(jax.random.fold_in(key_list[8], 71), 0),
        "precision_tiles": normal_values(key_list[2], (N_ROW, N_COL, CAP, BS, BS), 0.5, 3.0, ((0, 16), (1, 16)), jnp.float32),
        "inverse_tiles": normal_values(key_list[3], (N_ROW, N_COL, CAP, BS, BS), (0.5 / (BS * (CAP / JD) ** 0.5) ** 0.5), 0.3125, ((0, 16), (1, 16)), jnp.float32),
        "slot_rows": draw_slot_rows(jax.random.fold_in(key_list[8], 71), 0),
        "slot_columns": draw_slot_columns(jax.random.fold_in(key_list[8], 71), 0),
        "owned_columns": draw_owned_columns(jax.random.fold_in(key_list[8], 71), 0),
        "live_counts": draw_live_counts(jax.random.fold_in(key_list[8], 71), 0),
    }


step_size = 0.3
penalty = 0.6
highest = lax.Precision.HIGHEST


def soft_update(precision_tile, direction, residual):
    shifted = precision_tile + direction - step_size * residual
    return jnp.sign(shifted) * jnp.maximum(jnp.abs(shifted) - step_size * penalty, 0.0) - precision_tile


def reference(features, diag_inverse, precision_tiles, inverse_tiles, slot_rows, slot_columns, owned_columns, live_counts):
    device_count = N_ROW * N_COL
    rows_flat = slot_rows.reshape(device_count, CAP)
    cols_flat = jnp.take_along_axis(owned_columns, slot_columns, axis=2).reshape(device_count, CAP)
    theta_flat = precision_tiles.reshape(device_count, CAP, BS, BS)
    tiles_flat = inverse_tiles.reshape(device_count, CAP, BS, BS)
    live_mask = (jnp.arange(CAP)[None, :] < live_counts.reshape(device_count, 1)).astype(jnp.float32)
    device_cols = jnp.arange(device_count) % N_COL
    local_cols = cols_flat - (device_cols * FB)[:, None]
    onehot = (local_cols[:, :, None] == jnp.arange(FB)[None, None, :]).astype(jnp.float32) * live_mask[:, :, None]
    onehot = onehot.reshape(N_ROW, N_COL, CAP, FB)
    devices_all = jnp.arange(device_count)

    def gradient_of(device):
        row_tiles = jnp.take(features, rows_flat[device], axis=0).astype(jnp.float32)
        col_tiles = jnp.take(features, cols_flat[device], axis=0).astype(jnp.float32)
        covariance = jnp.einsum("kna,knb->kab", row_tiles, col_tiles, precision=highest) / NSAMP
        return covariance - tiles_flat[device]

    gradient = lax.map(gradient_of, devices_all)
    direction = jnp.zeros_like(gradient)
    for sweep_index in range(SWEEPS):
        if sweep_index > 0:
            def product_of(device):
                return jnp.einsum("kba,kbc->kac", direction[device], tiles_flat[device], precision=highest)

            products = lax.map(product_of, devices_all).reshape(N_ROW, N_COL, CAP, BS, BS)
            column_sums = jnp.einsum("rckf,rckab->cfab", onehot, products, precision=highest)
        else:
            column_sums = jnp.zeros((N_COL, FB, BS, BS), jnp.float32)

        def update_of(device):
            residual = gradient[device]
            if sweep_index > 0:
                row_diag = jnp.take(diag_inverse, rows_flat[device], axis=0).astype(jnp.float32)
                col_diag = jnp.take(diag_inverse, cols_flat[device], axis=0).astype(jnp.float32)
                left_side = jnp.einsum("kab,kbc->kac", row_diag, direction[device], precision=highest)
                residual = residual + jnp.einsum("kac,kcd->kad", left_side, col_diag, precision=highest)
                own_sums = lax.dynamic_index_in_dim(column_sums, device % N_COL, 0, keepdims=False)
                wanted = jnp.take(own_sums, local_cols[device], axis=0)
                residual = residual + jnp.einsum("kab,kbc->kac", tiles_flat[device], wanted, precision=highest)
            return soft_update(theta_flat[device], direction[device], residual)

        direction = lax.map(update_of, devices_all)
    direction = direction * live_mask[:, :, None, None]
    return direction.reshape(N_ROW, N_COL, CAP, BS, BS)
```

```python
import functools

import jax
import jax.numpy as jnp
from jax import lax
from jax.experimental import pallas as pl
from jax.experimental.pallas import tpu as pltpu
from jax.sharding import PartitionSpec as P

SWEEPS = 4
STEP = 0.3
LAMBDA = 0.3 * 0.6
PER_STEP = 4

BF = jnp.bfloat16
F32 = jnp.float32
VMEM = pl.BlockSpec(memory_space=pltpu.VMEM)
SMEM = pl.BlockSpec(memory_space=pltpu.SMEM)
PARAMS = pltpu.CompilerParams(vmem_limit_bytes=20 * 1024 * 1024)


def split(x):
    high = x.astype(BF)
    low = (x - high.astype(F32)).astype(BF)
    return high, low


def dot(a, b):
    return jnp.dot(a, b, preferred_element_type=F32)


def shrink(x):
    return x - jnp.clip(x, -LAMBDA, LAMBDA)


def slice_kernel(group, features_ref, out_ref):
    r = lax.axis_index("row")
    variables = features_ref.shape[2]
    wanted = lax.broadcasted_iota(jnp.int32, (group, variables), 0) + r * group
    pick = (lax.broadcasted_iota(jnp.int32, (group, variables), 1) == wanted).astype(BF)
    for block in range(features_ref.shape[0]):
        rows = lax.dot_general(
            pick, features_ref[block], (((1,), (1,)), ((), ())), preferred_element_type=F32
        )
        out_ref[block] = rows.astype(BF)


def split_kernel(tiles_ref, out_ref):
    for s in range(tiles_ref.shape[0]):
        out_ref[s] = jnp.concatenate(split(tiles_ref[s]), axis=1)


def gather_kernel(wanted_ref, diag_ref, send_ref):
    for h in range(send_ref.shape[0]):
        for p in range(send_ref.shape[1]):
            send_ref[h, p] = diag_ref[wanted_ref[h, p]]


def covariance_kernel(
    rows_ref, lists_ref, owned_ref, slices_ref, features_ref, out_ref, left_ref,
):
    owners, slots = rows_ref.shape
    group = slices_ref.shape[1]
    samples = features_ref.shape[1]
    size = features_ref.shape[2]

    def owner_step(owner, carry):
        for k in range(slots):
            left_ref[k * group:(k + 1) * group, :] = slices_ref[rows_ref[owner, k]].astype(F32)
        left = left_ref[...].astype(BF)
        right = jnp.concatenate(
            [features_ref[owned_ref[owner, a]] for a in range(owned_ref.shape[1])], axis=1
        )
        both = dot(left, right) * (1.0 / samples)
        for k in range(slots):
            rows = both[k * group:(k + 1) * group]
            out_ref[owner, k] = jnp.where(
                lists_ref[owner, k] == 0, rows[:, :size], rows[:, size:]
            )
        return carry

    lax.fori_loop(0, owners, owner_step, 0)


def pair(x):
    size = x.shape[0]
    high = x[:, :size]
    return jnp.concatenate(
        [x, jnp.concatenate([high, jnp.zeros_like(high)], axis=1)], axis=0
    )


def add_product(s, d, column, tile, sums_ref):
    left = jnp.concatenate(split(d.T), axis=1)
    sums_ref[column] += dot(left, pair(tile))


def write_sums(sums_ref, out_ref):
    pieces, columns, group, size = out_ref.shape
    for a in range(columns):
        total = sums_ref[a][:, :size] + sums_ref[a][:, size:]
        out_ref[:, a] = total.reshape(pieces, group, size)


def first_kernel(
    list_ref, live_ref, cov_ref, theta_ref, tiles_ref, split_ref,
    base_ref, d_ref, out_ref, sums_ref,
):
    count, size, _ = theta_ref.shape
    step = pl.program_id(0)

    @pl.when(step == 0)
    def _():
        sums_ref[...] = jnp.zeros_like(sums_ref)

    for s in range(count):
        slot = step * count + s
        covariance = cov_ref[:, s].reshape(size, size)
        theta = theta_ref[s]
        base = theta - STEP * (covariance - tiles_ref[s])
        d = shrink(base) - theta
        d = jnp.where(slot < live_ref[0], d, 0.0)
        base_ref[s] = base
        d_ref[s] = d
        add_product(s, d, list_ref[slot], split_ref[s], sums_ref)

    @pl.when(step == pl.num_programs(0) - 1)
    def _():
        write_sums(sums_ref, out_ref)


def diagonal_kernel(list_ref, base_ref, d_ref, row_diag_ref, col_diag_ref, out_ref):
    count, size, _ = d_ref.shape
    step = pl.program_id(0)
    for s in range(count):
        d = d_ref[s]
        half = dot(row_diag_ref[s], jnp.concatenate(split(d), axis=1))
        half = half[:, :size] + half[:, size:]
        right = col_diag_ref[list_ref[step * count + s]]
        both = dot(
            jnp.concatenate(split(half), axis=1), jnp.concatenate([right, right], axis=0)
        )
        out_ref[s] = base_ref[s] + d - STEP * both


def sum_kernel(same_ref, in_ref, out_ref):
    same = same_ref[...].astype(BF)
    for g in range(in_ref.shape[1]):
        x = in_ref[:, g, :]
        x1, rest = x.astype(BF), x
        rest = rest - x1.astype(F32)
        x2 = rest.astype(BF)
        rest = rest - x2.astype(F32)
        x3 = rest.astype(BF)
        out_ref[:, g, :] = dot(
            jnp.concatenate([same, same, same], axis=1), jnp.concatenate([x1, x2, x3], axis=0)
        )


def sweep_kernel(last, list_ref, live_ref, t_ref, theta_ref, split_ref, q_ref, d_ref, *rest):
    count, size, _ = theta_ref.shape
    step = pl.program_id(0)
    if last:
        (right_ref,) = rest
    else:
        out_ref, right_ref, sums_ref = rest

    @pl.when(step == 0)
    def _():
        for a in range(q_ref.shape[1]):
            q = q_ref[:, a].reshape(size, size)
            right_ref[a] = pair(jnp.concatenate(split(q), axis=1))
        if not last:
            sums_ref[...] = jnp.zeros_like(sums_ref)

    for s in range(count):
        slot = step * count + s
        column = list_ref[slot]
        both = dot(split_ref[s], right_ref[column])
        product = both[:, :size] + both[:, size:]
        d = shrink(t_ref[s] - STEP * product) - theta_ref[s]
        d = jnp.where(slot < live_ref[0], d, 0.0)
        d_ref[s] = d
        if not last:
            add_product(s, d, column, split_ref[s], sums_ref)

    if not last:
        @pl.when(step == pl.num_programs(0) - 1)
        def _():
            write_sums(sums_ref, out_ref)


def shape(dims, dtype):
    return jax.ShapeDtypeStruct(dims, dtype)


def far(x):
    return pltpu.with_memory_space_constraint(x, pltpu.HBM)


def slot_blocks(*dims):
    return pl.BlockSpec((PER_STEP,) + dims, lambda i: (i,) + (0,) * len(dims))


def whole(*dims):
    return pl.BlockSpec(dims, lambda i: (0,) * len(dims))


def body(
    features,
    diag_inverse,
    precision_tiles,
    inverse_tiles,
    slot_rows,
    slot_columns,
    owned_columns,
    live_counts,
):
    row_count = lax.axis_size("row")
    col_count = lax.axis_size("col")
    r = lax.axis_index("row")
    c = lax.axis_index("col")
    blocks, samples, size = features.shape
    slots = precision_tiles.shape[2]
    columns = owned_columns.shape[2]
    per_source = slots // col_count
    group = size // row_count
    theta = precision_tiles[0, 0]
    tiles = inverse_tiles[0, 0]
    tile_shape = (slots, size, size)
    piece_shape = (row_count, columns, group, size)

    with jax.named_scope("slices"):
        per_step = 8
        mine = pl.pallas_call(
            functools.partial(slice_kernel, group),
            grid=(blocks // per_step,),
            in_specs=[pl.BlockSpec((per_step, samples, size), lambda i: (i, 0, 0))],
            out_specs=pl.BlockSpec((per_step, group, samples), lambda i: (i, 0, 0)),
            out_shape=shape((blocks, group, samples), BF),
        )(features)
        slices = lax.all_gather(mine, "col", axis=0, tiled=True)

    with jax.named_scope("tables"):
        rows_here = lax.dynamic_index_in_dim(slot_rows, c, 1, keepdims=False)
        lists_here = lax.dynamic_index_in_dim(slot_columns, c, 1, keepdims=False)
        owned_here = lax.dynamic_index_in_dim(owned_columns, c, 1, keepdims=False) - c * blocks
        my_list = lax.dynamic_index_in_dim(lists_here, r, 0, keepdims=False)
        live = lax.dynamic_slice(live_counts, (r, c), (1, 1)).reshape(1)
        wanted = lax.dynamic_slice(
            slot_rows, (r, 0, c * per_source), (1, col_count, per_source)
        ).reshape(col_count, per_source) - c * blocks
        flat = owned_here.reshape(-1)
        same = (flat[:, None] == flat[None, :]).astype(F32)
        my_owned = lax.dynamic_index_in_dim(owned_here, r, 0, keepdims=False)
        col_diag = jnp.take(diag_inverse, my_owned, axis=0)

    with jax.named_scope("diag"):
        send_diag = pl.pallas_call(
            gather_kernel,
            in_specs=[SMEM, VMEM],
            out_specs=VMEM,
            out_shape=shape((col_count, per_source, size, size), BF),
            compiler_params=PARAMS,
        )(wanted, diag_inverse)
        row_diag = lax.all_to_all(send_diag, "col", split_axis=0, concat_axis=0, tiled=True)
        row_diag = row_diag.reshape(tile_shape)

    steps = slots // PER_STEP
    tile_spec = slot_blocks(size, size)
    split_spec = slot_blocks(size, 2 * size)
    piece_spec = whole(*piece_shape)
    tile_out = pltpu.HBM(tile_shape, F32)
    sums = pltpu.VMEM((columns, size, 2 * size), F32)

    with jax.named_scope("split"):
        pairs = pl.pallas_call(
            split_kernel,
            grid=(steps,),
            in_specs=[tile_spec],
            out_specs=split_spec,
            out_shape=pltpu.HBM((slots, size, 2 * size), BF),
        )(tiles)

    with jax.named_scope("covariance"):
        partial = pl.pallas_call(
            covariance_kernel,
            in_specs=[SMEM, SMEM, SMEM, VMEM, VMEM],
            out_specs=VMEM,
            out_shape=shape((row_count, slots, group, size), F32),
            scratch_shapes=[pltpu.VMEM((slots * group, samples), F32)],
            compiler_params=PARAMS,
        )(rows_here, lists_here, owned_here, slices, features)
        partial, row_diag, pairs = lax.optimization_barrier((partial, row_diag, pairs))
        covariance = lax.all_to_all(partial, "row", split_axis=0, concat_axis=0, tiled=True)

    with jax.named_scope("first"):
        base, d, pieces = pl.pallas_call(
            first_kernel,
            grid=(steps,),
            in_specs=[
                SMEM,
                SMEM,
                pl.BlockSpec((row_count, PER_STEP, group, size), lambda i: (0, i, 0, 0)),
                tile_spec,
                tile_spec,
                split_spec,
            ],
            out_specs=[tile_spec, tile_spec, piece_spec],
            out_shape=[tile_out, tile_out, shape(piece_shape, F32)],
            scratch_shapes=[sums],
        )(my_list, live, covariance, far(theta), far(tiles), far(pairs))

    for sweep in range(1, SWEEPS):
        last = sweep == SWEEPS - 1
        with jax.named_scope("exchange"):
            got = lax.all_to_all(pieces, "row", split_axis=0, concat_axis=0, tiled=True)
            flat_shape = (row_count * columns, group, size)
            summed = pl.pallas_call(
                sum_kernel,
                in_specs=[VMEM, VMEM],
                out_specs=VMEM,
                out_shape=shape(flat_shape, F32),
            )(same, got.reshape(flat_shape))
            q = lax.all_to_all(
                summed.reshape(piece_shape), "row", split_axis=0, concat_axis=0, tiled=True
            )
        with jax.named_scope("diagonal"):
            t = pl.pallas_call(
                diagonal_kernel,
                grid=(steps,),
                in_specs=[
                    SMEM, tile_spec, tile_spec, tile_spec, whole(columns, size, size)
                ],
                out_specs=tile_spec,
                out_shape=tile_out,
            )(my_list, far(base), far(d), row_diag, col_diag)
        with jax.named_scope("sweep"):
            scratch = [pltpu.VMEM((columns, 2 * size, 2 * size), BF)]
            result = pl.pallas_call(
                functools.partial(sweep_kernel, last),
                grid=(steps,),
                in_specs=[SMEM, SMEM, tile_spec, tile_spec, split_spec, piece_spec],
                out_specs=[tile_spec] if last else [tile_spec, piece_spec],
                out_shape=[tile_out] if last else [tile_out, shape(piece_shape, F32)],
                scratch_shapes=scratch if last else scratch + [sums],
            )(my_list, live, far(t), far(theta), far(pairs), q)
            d = result[0]
            if not last:
                pieces = result[1]
    return d.reshape(precision_tiles.shape)


def solution(mesh):
    return jax.shard_map(
        body,
        mesh=mesh,
        in_specs=(
            P("col", None, None),
            P("col", None, None),
            P("row", "col", None, None, None),
            P("row", "col", None, None, None),
            P(),
            P(),
            P(),
            P(),
        ),
        out_specs=P("row", "col", None, None, None),
        check_vma=False,
    )
```

```python
import functools

import jax
import jax.numpy as jnp
from jax import lax
from jax.experimental import pallas as pl
from jax.experimental.pallas import tpu as pltpu
from jax.sharding import PartitionSpec as P

SWEEPS = 4
STEP = 0.3
LAMBDA = 0.3 * 0.6
PER_STEP = 8
CHUNK = 4

BF = jnp.bfloat16
F32 = jnp.float32
VMEM = pl.BlockSpec(memory_space=pltpu.VMEM)
HBM = pl.BlockSpec(memory_space=pltpu.HBM)
SMEM = pl.BlockSpec(memory_space=pltpu.SMEM)
PARAMS = pltpu.CompilerParams(vmem_limit_bytes=20 * 1024 * 1024)


def split(x):
    high = x.astype(BF)
    low = (x - high.astype(F32)).astype(BF)
    return high, low


def dot(a, b):
    return jnp.dot(a, b, preferred_element_type=F32)


def shrink(x):
    return x - jnp.clip(x, -LAMBDA, LAMBDA)


def slice_kernel(group, features_ref, out_ref):
    r = lax.axis_index("row")
    variables = features_ref.shape[2]
    wanted = lax.broadcasted_iota(jnp.int32, (group, variables), 0) + r * group
    pick = (lax.broadcasted_iota(jnp.int32, (group, variables), 1) == wanted).astype(BF)
    for block in range(features_ref.shape[0]):
        rows = lax.dot_general(
            pick, features_ref[block], (((1,), (1,)), ((), ())), preferred_element_type=F32
        )
        out_ref[block] = rows.astype(BF)


def split_kernel(tiles_ref, out_ref):
    for s in range(tiles_ref.shape[0]):
        out_ref[s] = jnp.concatenate(split(tiles_ref[s]), axis=1)


def gather_kernel(wanted_ref, diag_ref, *out_refs):
    c = lax.axis_index("col")
    for offset, out_ref in enumerate(out_refs):
        target = lax.rem(c + offset, len(out_refs))
        for p in range(out_ref.shape[0]):
            out_ref[p] = diag_ref[wanted_ref[target, p]]


class Tiles:
    def __init__(self, far_ref, near_ref, sem, back=False):
        self.refs = (near_ref, far_ref) if back else (far_ref, near_ref)
        self.near = near_ref
        self.sem = sem
        self.chunks = near_ref.shape[0] // CHUNK

    def copy(self, i):
        part = pl.ds(i * CHUNK, CHUNK)
        source, target = (ref.at[part] for ref in self.refs)
        return pltpu.make_async_copy(source, target, self.sem.at[i])

    def start(self, i):
        self.copy(i).start()

    def wait(self, i):
        self.copy(i).wait()


def start_all(arrays, chunks):
    for i in range(chunks):
        for array in arrays:
            array.start(i)


def each_slot(chunks, arrays, outs, slot_step):
    def step(i, carry):
        for array in arrays:
            array.wait(i)
        for s in range(CHUNK):
            slot_step(i * CHUNK + s)
        for out in outs:
            out.start(i)
        return carry

    lax.fori_loop(0, chunks, step, 0)
    for i in range(chunks):
        for out in outs:
            out.wait(i)


def covariance_kernel(
    rows_ref, lists_ref, owned_ref, far_slices, features, out_ref,
    slices_ref, right_ref, left_ref, slice_sem, right_sem,
):
    owners, slots = rows_ref.shape
    columns = owned_ref.shape[1]
    group = slices_ref.shape[1]
    samples = features.shape[1]
    size = features.shape[2]
    blocks = features.shape[0]
    parts = slices_ref.shape[0] // blocks

    def slice_copy(i):
        part = pl.ds(i * blocks, blocks)
        return pltpu.make_async_copy(far_slices.at[part], slices_ref.at[part], slice_sem.at[i])

    def right_copy(owner, a):
        return pltpu.make_async_copy(
            features.at[owned_ref[owner, a]], right_ref.at[owner, a], right_sem.at[owner, a]
        )

    for i in range(parts):
        slice_copy(i).start()
    for owner in range(owners):
        for a in range(columns):
            right_copy(owner, a).start()
    for i in range(parts):
        slice_copy(i).wait()

    def owner_step(owner, carry):
        for a in range(columns):
            right_copy(owner, a).wait()
        for k in range(slots):
            left_ref[k * group:(k + 1) * group, :] = slices_ref[rows_ref[owner, k]].astype(F32)
        left = left_ref[...].astype(BF)
        right = jnp.concatenate([right_ref[owner, a] for a in range(columns)], axis=1)
        both = dot(left, right) * (1.0 / samples)
        for k in range(slots):
            rows = both[k * group:(k + 1) * group]
            out_ref[owner, k] = jnp.where(
                lists_ref[owner, k] == 0, rows[:, :size], rows[:, size:]
            )
        return carry

    lax.fori_loop(0, owners, owner_step, 0)


def pair(x):
    size = x.shape[0]
    high = x[:, :size]
    return jnp.concatenate(
        [x, jnp.concatenate([high, jnp.zeros_like(high)], axis=1)], axis=0
    )


def add_product(d, column, tile, sums_ref):
    left = jnp.concatenate(split(d.T), axis=1)
    sums_ref[column] += dot(left, pair(tile))


def write_sums(sums_ref, out_ref):
    pieces, columns, group, size = out_ref.shape
    for a in range(columns):
        total = sums_ref[a][:, :size] + sums_ref[a][:, size:]
        out_ref[:, a] = total.reshape(pieces, group, size)


def first_kernel(
    list_ref, live_ref, cov_ref, far_theta, far_tiles, far_base, far_d, out_ref,
    theta_ref, tiles_ref, base_ref, d_ref, sums_ref, sems,
):
    slots, size, _ = theta_ref.shape
    chunks = slots // CHUNK
    arrays = [Tiles(far_theta, theta_ref, sems.at[0]), Tiles(far_tiles, tiles_ref, sems.at[1])]
    outs = [Tiles(far_base, base_ref, sems.at[2], True), Tiles(far_d, d_ref, sems.at[3], True)]
    start_all(arrays, chunks)
    sums_ref[...] = jnp.zeros_like(sums_ref)

    def slot_step(slot):
        covariance = cov_ref[:, slot].reshape(size, size)
        theta = theta_ref[slot]
        tile = tiles_ref[slot]
        base = theta - STEP * (covariance - tile)
        d = jnp.where(slot < live_ref[0], shrink(base) - theta, 0.0)
        base_ref[slot] = base
        d_ref[slot] = d
        halves = jnp.concatenate(split(tile), axis=1)
        add_product(d, list_ref[slot], halves, sums_ref)

    each_slot(chunks, arrays, outs, slot_step)
    write_sums(sums_ref, out_ref)


def diagonal_kernel(list_ref, far_base, far_d, col_diag_ref, *rest):
    far_diag = rest[:-7]
    far_out, base_ref, d_ref, diag_ref, out_ref, diag_sem, sems = rest[-7:]
    slots, size, _ = d_ref.shape
    chunks = slots // CHUNK
    c = lax.axis_index("col")
    per_source = slots // len(far_diag)
    arrays = [Tiles(far_base, base_ref, sems.at[0]), Tiles(far_d, d_ref, sems.at[1])]
    out = Tiles(far_out, out_ref, sems.at[2], True)

    def diag_copy(offset):
        source = lax.rem(c + len(far_diag) - offset, len(far_diag))
        return pltpu.make_async_copy(
            far_diag[offset], diag_ref.at[pl.ds(source * per_source, per_source)],
            diag_sem.at[offset],
        )

    for offset in range(len(far_diag)):
        diag_copy(offset).start()
    start_all(arrays, chunks)
    for offset in range(len(far_diag)):
        diag_copy(offset).wait()

    def slot_step(slot):
        d = d_ref[slot]
        half = dot(diag_ref[slot], jnp.concatenate(split(d), axis=1))
        half = half[:, :size] + half[:, size:]
        right = col_diag_ref[list_ref[slot]]
        both = dot(
            jnp.concatenate(split(half), axis=1), jnp.concatenate([right, right], axis=0)
        )
        out_ref[slot] = base_ref[slot] + d - STEP * both

    each_slot(chunks, arrays, [out], slot_step)


def sum_kernel(same_ref, in_ref, out_ref):
    same = same_ref[...].astype(BF)
    for g in range(in_ref.shape[1]):
        x = in_ref[:, g, :]
        x1, rest = x.astype(BF), x
        rest = rest - x1.astype(F32)
        x2 = rest.astype(BF)
        rest = rest - x2.astype(F32)
        x3 = rest.astype(BF)
        out_ref[:, g, :] = dot(
            jnp.concatenate([same, same, same], axis=1), jnp.concatenate([x1, x2, x3], axis=0)
        )


def sweep_kernel(
    last, list_ref, live_ref, far_t, far_theta, far_pairs, q_ref, far_d, *rest
):
    if last:
        t_ref, theta_ref, pairs_ref, d_ref, right_ref, sems = rest
    else:
        out_ref, t_ref, theta_ref, pairs_ref, d_ref, right_ref, sems, sums_ref = rest
    slots, size, _ = theta_ref.shape
    chunks = slots // CHUNK
    arrays = [
        Tiles(far_pairs, pairs_ref, sems.at[0]),
        Tiles(far_t, t_ref, sems.at[1]),
        Tiles(far_theta, theta_ref, sems.at[2]),
    ]
    out = Tiles(far_d, d_ref, sems.at[3], True)
    start_all(arrays, chunks)
    for a in range(q_ref.shape[1]):
        q = q_ref[:, a].reshape(size, size)
        right_ref[a] = pair(jnp.concatenate(split(q), axis=1))
    if not last:
        sums_ref[...] = jnp.zeros_like(sums_ref)

    def slot_step(slot):
        column = list_ref[slot]
        both = dot(pairs_ref[slot], right_ref[column])
        product = both[:, :size] + both[:, size:]
        d = shrink(t_ref[slot] - STEP * product) - theta_ref[slot]
        d = jnp.where(slot < live_ref[0], d, 0.0)
        d_ref[slot] = d
        if not last:
            add_product(d, column, pairs_ref[slot], sums_ref)

    each_slot(chunks, arrays, [out], slot_step)
    if not last:
        write_sums(sums_ref, out_ref)


def shape(dims, dtype):
    return jax.ShapeDtypeStruct(dims, dtype)


def far(x):
    return pltpu.with_memory_space_constraint(x, pltpu.HBM)


def slot_blocks(*dims):
    return pl.BlockSpec((PER_STEP,) + dims, lambda i: (i,) + (0,) * len(dims))


def body(
    features,
    diag_inverse,
    precision_tiles,
    inverse_tiles,
    slot_rows,
    slot_columns,
    owned_columns,
    live_counts,
):
    row_count = lax.axis_size("row")
    col_count = lax.axis_size("col")
    r = lax.axis_index("row")
    c = lax.axis_index("col")
    blocks, samples, size = features.shape
    slots = precision_tiles.shape[2]
    columns = owned_columns.shape[2]
    per_source = slots // col_count
    group = size // row_count
    theta = precision_tiles[0, 0]
    tiles = inverse_tiles[0, 0]
    tile_shape = (slots, size, size)
    piece_shape = (row_count, columns, group, size)

    with jax.named_scope("slices"):
        per_step = 8
        mine = pl.pallas_call(
            functools.partial(slice_kernel, group),
            grid=(blocks // per_step,),
            in_specs=[pl.BlockSpec((per_step, samples, size), lambda i: (i, 0, 0))],
            out_specs=pl.BlockSpec((per_step, group, samples), lambda i: (i, 0, 0)),
            out_shape=shape((blocks, group, samples), BF),
        )(features)
        slices = lax.all_gather(mine, "col", axis=0, tiled=True)

    with jax.named_scope("tables"):
        rows_here = lax.dynamic_index_in_dim(slot_rows, c, 1, keepdims=False)
        lists_here = lax.dynamic_index_in_dim(slot_columns, c, 1, keepdims=False)
        owned_here = lax.dynamic_index_in_dim(owned_columns, c, 1, keepdims=False) - c * blocks
        my_list = lax.dynamic_index_in_dim(lists_here, r, 0, keepdims=False)
        live = lax.dynamic_slice(live_counts, (r, c), (1, 1)).reshape(1)
        wanted = lax.dynamic_slice(
            slot_rows, (r, 0, c * per_source), (1, col_count, per_source)
        ).reshape(col_count, per_source) - c * blocks
        flat = owned_here.reshape(-1)
        same = (flat[:, None] == flat[None, :]).astype(F32)
        my_owned = lax.dynamic_index_in_dim(owned_here, r, 0, keepdims=False)
        col_diag = jnp.take(diag_inverse, my_owned, axis=0)

    tile_vmem = pltpu.VMEM(tile_shape, F32)
    tile_out = pltpu.HBM(tile_shape, F32)
    sums = pltpu.VMEM((columns, size, 2 * size), F32)
    chunks = slots // CHUNK

    def sems(*dims):
        return pltpu.SemaphoreType.DMA(dims)

    with jax.named_scope("split"):
        pairs = pl.pallas_call(
            split_kernel,
            grid=(slots // PER_STEP,),
            in_specs=[slot_blocks(size, size)],
            out_specs=slot_blocks(size, 2 * size),
            out_shape=pltpu.HBM((slots, size, 2 * size), BF),
        )(far(tiles))
        slices, pairs = lax.optimization_barrier((slices, pairs))

    with jax.named_scope("covariance"):
        partial = pl.pallas_call(
            covariance_kernel,
            in_specs=[SMEM, SMEM, SMEM, HBM, HBM],
            out_specs=VMEM,
            out_shape=pltpu.HBM((row_count, slots, group, size), F32),
            scratch_shapes=[
                pltpu.VMEM(slices.shape, BF),
                pltpu.VMEM((row_count, columns, samples, size), BF),
                pltpu.VMEM((slots * group, samples), F32),
                sems(col_count),
                sems(row_count, columns),
            ],
            compiler_params=PARAMS,
        )(rows_here, lists_here, owned_here, far(slices), far(features))
        covariance = lax.all_to_all(partial, "row", split_axis=0, concat_axis=0, tiled=True)

    with jax.named_scope("diag"):
        wanted, partial = lax.optimization_barrier((wanted, partial[0, 0]))
        send_diag = pl.pallas_call(
            gather_kernel,
            in_specs=[SMEM, VMEM],
            out_specs=[VMEM] * col_count,
            out_shape=[pltpu.HBM((per_source, size, size), BF)] * col_count,
            compiler_params=PARAMS,
        )(wanted, diag_inverse)
        row_diag = [
            lax.ppermute(
                block, "col", [(i, (i + offset) % col_count) for i in range(col_count)]
            ) if offset else block
            for offset, block in enumerate(send_diag)
        ]
        covariance, *row_diag = lax.optimization_barrier((covariance, *row_diag))

    with jax.named_scope("first"):
        base, d, pieces = pl.pallas_call(
            first_kernel,
            in_specs=[SMEM, SMEM, VMEM, HBM, HBM],
            out_specs=[HBM, HBM, VMEM],
            out_shape=[tile_out, tile_out, shape(piece_shape, F32)],
            scratch_shapes=[
                tile_vmem, tile_vmem, tile_vmem, tile_vmem, sums, sems(4, chunks),
            ],
            compiler_params=PARAMS,
        )(my_list, live, covariance, far(theta), far(tiles))

    for sweep in range(1, SWEEPS):
        last = sweep == SWEEPS - 1
        with jax.named_scope("exchange"):
            got = lax.all_to_all(pieces, "row", split_axis=0, concat_axis=0, tiled=True)
            flat_shape = (row_count * columns, group, size)
            summed = pl.pallas_call(
                sum_kernel,
                in_specs=[VMEM, VMEM],
                out_specs=VMEM,
                out_shape=shape(flat_shape, F32),
                compiler_params=PARAMS,
            )(same, got.reshape(flat_shape))
            q = lax.all_to_all(
                summed.reshape(piece_shape), "row", split_axis=0, concat_axis=0, tiled=True
            )
        with jax.named_scope("diagonal"):
            t = pl.pallas_call(
                diagonal_kernel,
                in_specs=[SMEM, HBM, HBM, VMEM] + [HBM] * col_count,
                out_specs=HBM,
                out_shape=tile_out,
                scratch_shapes=[
                    tile_vmem, tile_vmem, pltpu.VMEM(tile_shape, BF), tile_vmem,
                    sems(col_count), sems(3, chunks),
                ],
                compiler_params=PARAMS,
            )(my_list, far(base), far(d), col_diag, *[far(block) for block in row_diag])
        with jax.named_scope("sweep"):
            result = pl.pallas_call(
                functools.partial(sweep_kernel, last),
                in_specs=[SMEM, SMEM, HBM, HBM, HBM, VMEM],
                out_specs=[HBM] if last else [HBM, VMEM],
                out_shape=[tile_out] if last else [tile_out, shape(piece_shape, F32)],
                scratch_shapes=[
                    tile_vmem, tile_vmem, pltpu.VMEM((slots, size, 2 * size), BF), tile_vmem,
                    pltpu.VMEM((columns, 2 * size, 2 * size), BF), sems(4, chunks),
                ] + ([] if last else [sums]),
                compiler_params=PARAMS,
            )(my_list, live, far(t), far(theta), far(pairs), q)
            d = result[0]
            if not last:
                pieces = result[1]
    return d.reshape(precision_tiles.shape)


def solution(mesh):
    return jax.shard_map(
        body,
        mesh=mesh,
        in_specs=(
            P("col", None, None),
            P("col", None, None),
            P("row", "col", None, None, None),
            P("row", "col", None, None, None),
            P(),
            P(),
            P(),
            P(),
        ),
        out_specs=P("row", "col", None, None, None),
        check_vma=False,
    )
```

```python
import functools

import jax
import jax.numpy as jnp
from jax import lax
from jax.experimental import pallas as pl
from jax.experimental.pallas import tpu as pltpu
from jax.sharding import PartitionSpec as P

SWEEPS = 4
STEP = 0.3
LAMBDA = 0.3 * 0.6
PER_STEP = 8
CHUNK = 4
CORES = 2

BF = jnp.bfloat16
F32 = jnp.float32
VMEM = pl.BlockSpec(memory_space=pltpu.VMEM)
HBM = pl.BlockSpec(memory_space=pltpu.HBM)
SMEM = pl.BlockSpec(memory_space=pltpu.SMEM)
PARAMS = pltpu.CompilerParams(vmem_limit_bytes=20 * 1024 * 1024)


def split(x):
    high = x.astype(BF)
    low = (x - high.astype(F32)).astype(BF)
    return high, low


def dot(a, b):
    return jnp.dot(a, b, preferred_element_type=F32)


def shrink(x):
    return x - jnp.clip(x, -LAMBDA, LAMBDA)


def slice_kernel(group, features_ref, out_ref):
    r = lax.axis_index("row")
    variables = features_ref.shape[2]
    wanted = lax.broadcasted_iota(jnp.int32, (group, variables), 0) + r * group
    pick = (lax.broadcasted_iota(jnp.int32, (group, variables), 1) == wanted).astype(BF)
    for block in range(features_ref.shape[0]):
        rows = lax.dot_general(
            pick, features_ref[block], (((1,), (1,)), ((), ())), preferred_element_type=F32
        )
        out_ref[block] = rows.astype(BF)


def split_kernel(tiles_ref, out_ref):
    for s in range(tiles_ref.shape[0]):
        out_ref[s] = jnp.concatenate(split(tiles_ref[s]), axis=1)


def gather_kernel(steps, wanted_ref, features, diag, *rest):
    outs, sems = rest[:-1], rest[-1]
    c = lax.axis_index("col")
    samples = features.shape[1]
    copies = []
    for n, ((dz, dk), out) in enumerate(zip(steps, outs)):
        target = holder(c, -dz, dk, wanted_ref.shape[0])
        for p in range(out.shape[0]):
            block = wanted_ref[target, p]
            begin = 0
            if out.shape[1] > diag.shape[1]:
                copies.append(pltpu.make_async_copy(
                    features.at[block], out.at[p, pl.ds(0, samples)], sems.at[n, p, 0]
                ))
                begin = samples
            copies.append(pltpu.make_async_copy(
                diag.at[block], out.at[p, pl.ds(begin, diag.shape[1])], sems.at[n, p, 1]
            ))
    for copy in copies:
        copy.start()
    for copy in copies:
        copy.wait()


def holder(c, dz, dk, col_count):
    chips = col_count // CORES
    z = lax.rem(c // CORES + dz + chips, chips)
    return z * CORES + lax.rem(c + dk, CORES)


def chip_at(dz, col_count):
    return lax.rem(lax.axis_index("col") // CORES + dz, col_count // CORES)


class Tiles:
    def __init__(self, far_ref, near_ref, sem, back=False):
        self.refs = (near_ref, far_ref) if back else (far_ref, near_ref)
        self.near = near_ref
        self.sem = sem
        self.chunks = near_ref.shape[0] // CHUNK

    def copy(self, i):
        part = pl.ds(i * CHUNK, CHUNK)
        source, target = (ref.at[part] for ref in self.refs)
        return pltpu.make_async_copy(source, target, self.sem.at[i])

    def start(self, i):
        self.copy(i).start()

    def wait(self, i):
        self.copy(i).wait()


def start_all(arrays, chunks):
    for i in range(chunks):
        for array in arrays:
            array.start(i)


def each_slot(chunks, arrays, outs, slot_step):
    def step(i, carry):
        for array in arrays:
            array.wait(i)
        for s in range(CHUNK):
            slot_step(i * CHUNK + s)
        for out in outs:
            out.start(i)
        return carry

    lax.fori_loop(0, chunks, step, 0)
    for i in range(chunks):
        for out in outs:
            out.wait(i)


def covariance_kernel(
    far, col_count, rows_ref, lists_ref, owned_ref, far_slices, features, out_ref,
    slices_ref, right_ref, left_ref, slice_sem, right_sem,
):
    owners = rows_ref.shape[0]
    columns = owned_ref.shape[1]
    group = slices_ref.shape[1]
    samples = features.shape[1]
    size = features.shape[2]
    part = far_slices.shape[0] * CORES // col_count

    def slice_copy(n):
        here = pl.ds(chip_at(far[n], col_count) * part, part)
        return pltpu.make_async_copy(
            far_slices.at[here], slices_ref.at[here], slice_sem.at[n]
        )

    def right_copy(owner, a):
        return pltpu.make_async_copy(
            features.at[owned_ref[owner, a]], right_ref.at[owner, a], right_sem.at[owner, a]
        )

    for n in range(len(far)):
        slice_copy(n).start()
    for owner in range(owners):
        for a in range(columns):
            right_copy(owner, a).start()
    for n in range(len(far)):
        slice_copy(n).wait()

    def owner_step(owner, carry):
        for a in range(columns):
            right_copy(owner, a).wait()
        for n, dz in enumerate(far):
            first = chip_at(dz, col_count) * CHUNK
            for s in range(CHUNK):
                k = n * CHUNK + s
                left_ref[k * group:(k + 1) * group, :] = slices_ref[
                    rows_ref[owner, first + s]
                ].astype(F32)
        left = left_ref[...].astype(BF)
        right = jnp.concatenate([right_ref[owner, a] for a in range(columns)], axis=1)
        both = dot(left, right) * (1.0 / samples)
        for n, dz in enumerate(far):
            first = chip_at(dz, col_count) * CHUNK
            for s in range(CHUNK):
                k = n * CHUNK + s
                rows = both[k * group:(k + 1) * group]
                out_ref[owner, k] = jnp.where(
                    lists_ref[owner, first + s] == 0, rows[:, :size], rows[:, size:]
                )
        return carry

    lax.fori_loop(0, owners, owner_step, 0)


def pair(x):
    size = x.shape[0]
    high = x[:, :size]
    return jnp.concatenate(
        [x, jnp.concatenate([high, jnp.zeros_like(high)], axis=1)], axis=0
    )


def add_product(d, column, tile, sums_ref):
    left = jnp.concatenate(split(d.T), axis=1)
    sums_ref[column] += dot(left, pair(tile))


def write_sums(sums_ref, out_ref):
    pieces, columns, group, size = out_ref.shape
    for a in range(columns):
        total = sums_ref[a][:, :size] + sums_ref[a][:, size:]
        out_ref[:, a] = total.reshape(pieces, group, size)


def first_step(slot, covariance, list_ref, live_ref, theta_ref, tiles_ref, base_ref, d_ref, sums_ref):
    theta = theta_ref[slot]
    tile = tiles_ref[slot]
    base = theta - STEP * (covariance - tile)
    d = jnp.where(slot < live_ref[0], shrink(base) - theta, 0.0)
    base_ref[slot] = base
    d_ref[slot] = d
    halves = jnp.concatenate(split(tile), axis=1)
    add_product(d, list_ref[slot], halves, sums_ref)


def near_kernel(near, col_count, list_ref, live_ref, owned_ref, features, far_theta, far_tiles, *rest):
    count = len(near) * CORES
    blocks = rest[:count]
    (
        far_base, far_d, sums_ref, left_ref, right_ref, theta_ref, tiles_ref, base_ref, d_ref,
        left_sem, right_sem, sems,
    ) = rest[count:]
    slots, size, _ = theta_ref.shape
    samples = features.shape[1]
    per_source = CHUNK // CORES
    core = lax.rem(lax.axis_index("col"), CORES)
    arrays = [Tiles(far_theta, theta_ref, sems.at[0]), Tiles(far_tiles, tiles_ref, sems.at[1])]
    outs = [Tiles(far_base, base_ref, sems.at[2], True), Tiles(far_d, d_ref, sems.at[3], True)]

    def left_copy(n):
        place = n // CORES * CHUNK + lax.rem(core + n % CORES, CORES) * per_source
        return pltpu.make_async_copy(
            blocks[n].at[:, pl.ds(0, samples)], left_ref.at[pl.ds(place, per_source)],
            left_sem.at[n],
        )

    def right_copy(a):
        return pltpu.make_async_copy(
            features.at[owned_ref[a]], right_ref.at[a], right_sem.at[a]
        )

    for a in range(right_ref.shape[0]):
        right_copy(a).start()
    for n in range(count):
        left_copy(n).start()
    for dz in near:
        for array in arrays:
            array.start(chip_at(dz, col_count))
    sums_ref[...] = jnp.zeros_like(sums_ref)
    for a in range(right_ref.shape[0]):
        right_copy(a).wait()
    for n in range(count):
        left_copy(n).wait()
    for n, dz in enumerate(near):
        chip = chip_at(dz, col_count)
        for array in arrays:
            array.wait(chip)
        for s in range(CHUNK):
            slot = chip * CHUNK + s
            covariance = lax.dot_general(
                left_ref[n * CHUNK + s], right_ref[list_ref[slot]],
                (((0,), (0,)), ((), ())), preferred_element_type=F32,
            ) * (1.0 / samples)
            first_step(
                slot, covariance, list_ref, live_ref, theta_ref, tiles_ref, base_ref, d_ref,
                sums_ref,
            )
        for out in outs:
            out.start(chip)
    for dz in near:
        for out in outs:
            out.wait(chip_at(dz, col_count))


def first_kernel(
    far, col_count, list_ref, live_ref, cov_ref, near_sums, far_theta, far_tiles, in_base, in_d,
    far_base, far_d, out_ref, theta_ref, tiles_ref, base_ref, d_ref, sums_ref, sum_sem, sems,
):
    slots, size, _ = theta_ref.shape
    arrays = [Tiles(far_theta, theta_ref, sems.at[0]), Tiles(far_tiles, tiles_ref, sems.at[1])]
    outs = [Tiles(far_base, base_ref, sems.at[2], True), Tiles(far_d, d_ref, sems.at[3], True)]
    bring = pltpu.make_async_copy(near_sums, sums_ref, sum_sem.at[0])
    bring.start()
    for dz in far:
        for array in arrays:
            array.start(chip_at(dz, col_count))
    bring.wait()

    def step(n, carry):
        chip = chip_at(n + far[0], col_count)
        for array in arrays:
            array.wait(chip)
        for s in range(CHUNK):
            slot = chip * CHUNK + s
            covariance = cov_ref[:, n * CHUNK + s].reshape(size, size)
            first_step(
                slot, covariance, list_ref, live_ref, theta_ref, tiles_ref, base_ref, d_ref,
                sums_ref,
            )
        for out in outs:
            out.start(chip)
        return carry

    lax.fori_loop(0, len(far), step, 0)
    write_sums(sums_ref, out_ref)
    for dz in far:
        for out in outs:
            out.wait(chip_at(dz, col_count))


def diagonal_kernel(steps, list_ref, far_base, far_d, col_diag_ref, *rest):
    far_diag = rest[:-7]
    far_out, base_ref, d_ref, diag_ref, out_ref, diag_sem, sems = rest[-7:]
    slots, size, _ = d_ref.shape
    chunks = slots // CHUNK
    c = lax.axis_index("col")
    per_source = slots // len(far_diag)
    arrays = [Tiles(far_base, base_ref, sems.at[0]), Tiles(far_d, d_ref, sems.at[1])]
    out = Tiles(far_out, out_ref, sems.at[2], True)

    def diag_copy(n):
        block = far_diag[n]
        place = holder(c, *steps[n], len(far_diag)) * per_source
        return pltpu.make_async_copy(
            block.at[:, pl.ds(block.shape[1] - size, size)],
            diag_ref.at[pl.ds(place, per_source)],
            diag_sem.at[n],
        )

    for n in range(len(far_diag)):
        diag_copy(n).start()
    start_all(arrays, chunks)
    for n in range(len(far_diag)):
        diag_copy(n).wait()

    def slot_step(slot):
        d = d_ref[slot]
        half = dot(diag_ref[slot], jnp.concatenate(split(d), axis=1))
        half = half[:, :size] + half[:, size:]
        right = col_diag_ref[list_ref[slot]]
        both = dot(
            jnp.concatenate(split(half), axis=1), jnp.concatenate([right, right], axis=0)
        )
        out_ref[slot] = base_ref[slot] + d - STEP * both

    each_slot(chunks, arrays, [out], slot_step)


def sum_kernel(same_ref, in_ref, out_ref):
    same = same_ref[...].astype(BF)
    for g in range(in_ref.shape[1]):
        x = in_ref[:, g, :]
        x1, rest = x.astype(BF), x
        rest = rest - x1.astype(F32)
        x2 = rest.astype(BF)
        rest = rest - x2.astype(F32)
        x3 = rest.astype(BF)
        out_ref[:, g, :] = dot(
            jnp.concatenate([same, same, same], axis=1), jnp.concatenate([x1, x2, x3], axis=0)
        )


def sweep_kernel(
    last, list_ref, live_ref, far_t, far_theta, far_pairs, q_ref, far_d, *rest
):
    if last:
        t_ref, theta_ref, pairs_ref, d_ref, right_ref, sems = rest
    else:
        out_ref, t_ref, theta_ref, pairs_ref, d_ref, right_ref, sems, sums_ref = rest
    slots, size, _ = theta_ref.shape
    chunks = slots // CHUNK
    arrays = [
        Tiles(far_pairs, pairs_ref, sems.at[0]),
        Tiles(far_t, t_ref, sems.at[1]),
        Tiles(far_theta, theta_ref, sems.at[2]),
    ]
    out = Tiles(far_d, d_ref, sems.at[3], True)
    start_all(arrays, chunks)
    for a in range(q_ref.shape[1]):
        q = q_ref[:, a].reshape(size, size)
        right_ref[a] = pair(jnp.concatenate(split(q), axis=1))
    if not last:
        sums_ref[...] = jnp.zeros_like(sums_ref)

    def slot_step(slot):
        column = list_ref[slot]
        both = dot(pairs_ref[slot], right_ref[column])
        product = both[:, :size] + both[:, size:]
        d = shrink(t_ref[slot] - STEP * product) - theta_ref[slot]
        d = jnp.where(slot < live_ref[0], d, 0.0)
        d_ref[slot] = d
        if not last:
            add_product(d, column, pairs_ref[slot], sums_ref)

    each_slot(chunks, arrays, [out], slot_step)
    if not last:
        write_sums(sums_ref, out_ref)


def shape(dims, dtype):
    return jax.ShapeDtypeStruct(dims, dtype)


def far(x):
    return pltpu.with_memory_space_constraint(x, pltpu.HBM)


def slot_blocks(*dims):
    return pl.BlockSpec((PER_STEP,) + dims, lambda i: (i,) + (0,) * len(dims))


def body(
    features,
    diag_inverse,
    precision_tiles,
    inverse_tiles,
    slot_rows,
    slot_columns,
    owned_columns,
    live_counts,
):
    row_count = lax.axis_size("row")
    col_count = lax.axis_size("col")
    r = lax.axis_index("row")
    c = lax.axis_index("col")
    blocks, samples, size = features.shape
    slots = precision_tiles.shape[2]
    columns = owned_columns.shape[2]
    per_source = slots // col_count
    group = size // row_count
    theta = precision_tiles[0, 0]
    tiles = inverse_tiles[0, 0]
    tile_shape = (slots, size, size)
    piece_shape = (row_count, columns, group, size)

    with jax.named_scope("slices"):
        per_step = 8
        mine = pl.pallas_call(
            functools.partial(slice_kernel, group),
            grid=(blocks // per_step,),
            in_specs=[pl.BlockSpec((per_step, samples, size), lambda i: (i, 0, 0))],
            out_specs=pl.BlockSpec((per_step, group, samples), lambda i: (i, 0, 0)),
            out_shape=shape((blocks, group, samples), BF),
        )(features)
        slices = lax.all_gather(mine, "col", axis=0, tiled=True)

    with jax.named_scope("tables"):
        rows_here = lax.dynamic_index_in_dim(slot_rows, c, 1, keepdims=False)
        lists_here = lax.dynamic_index_in_dim(slot_columns, c, 1, keepdims=False)
        owned_here = lax.dynamic_index_in_dim(owned_columns, c, 1, keepdims=False) - c * blocks
        my_list = lax.dynamic_index_in_dim(lists_here, r, 0, keepdims=False)
        live = lax.dynamic_slice(live_counts, (r, c), (1, 1)).reshape(1)
        wanted = lax.dynamic_slice(
            slot_rows, (r, 0, c * per_source), (1, col_count, per_source)
        ).reshape(col_count, per_source) - c * blocks
        flat = owned_here.reshape(-1)
        same = (flat[:, None] == flat[None, :]).astype(F32)
        my_owned = lax.dynamic_index_in_dim(owned_here, r, 0, keepdims=False)
        col_diag = jnp.take(diag_inverse, my_owned, axis=0)

    tile_vmem = pltpu.VMEM(tile_shape, F32)
    tile_out = pltpu.HBM(tile_shape, F32)
    sums = pltpu.VMEM((columns, size, 2 * size), F32)
    chunks = slots // CHUNK

    def sems(*dims):
        return pltpu.SemaphoreType.DMA(dims)

    with jax.named_scope("split"):
        pairs = pl.pallas_call(
            split_kernel,
            grid=(slots // PER_STEP,),
            in_specs=[slot_blocks(size, size)],
            out_specs=slot_blocks(size, 2 * size),
            out_shape=pltpu.HBM((slots, size, 2 * size), BF),
        )(far(tiles))

    with jax.named_scope("blocks"):
        chips = col_count // CORES
        near = [0, 1, chips - 1]
        far_chips = list(range(2, chips - 1))
        cores = range(CORES)
        steps = [(dz, dk) for dz in near for dk in cores]
        steps += [(dz, dk) for dz in (2, chips - 2) for dk in cores]
        early = len(steps)
        steps += [(dz, dk) for dz in far_chips[1:-1] for dk in cores]
        near_count = len(near) * CORES
        block_shapes = [
            (per_source, samples + size if n < near_count else size, size)
            for n in range(len(steps))
        ]
        mine, wanted = lax.optimization_barrier((mine, wanted))
        blocks_out = list(pl.pallas_call(
            functools.partial(gather_kernel, steps),
            in_specs=[SMEM, HBM, HBM],
            out_specs=[HBM] * len(steps),
            out_shape=[pltpu.HBM(dims, BF) for dims in block_shapes],
            scratch_shapes=[sems(len(steps), per_source, 2)],
        )(wanted, far(features), far(diag_inverse)))

        def send(n):
            dz, dk = steps[n]
            if dz == 0 and dk == 0:
                return blocks_out[n]
            pairs_of = [
                (h, (h // CORES - dz) % chips * CORES + (h + dk) % CORES)
                for h in range(col_count)
            ]
            return lax.ppermute(blocks_out[n], "col", pairs_of)

        got_blocks = [send(n) for n in range(early)]
        slices, pairs, *got_blocks = lax.optimization_barrier((slices, pairs, *got_blocks))

    far_slots = len(far_chips) * CHUNK
    with jax.named_scope("covariance"):
        partial = pl.pallas_call(
            functools.partial(covariance_kernel, far_chips, col_count),
            in_specs=[SMEM, SMEM, SMEM, HBM, HBM],
            out_specs=VMEM,
            out_shape=pltpu.HBM((row_count, far_slots, group, size), F32),
            scratch_shapes=[
                pltpu.VMEM(slices.shape, BF),
                pltpu.VMEM((row_count, columns, samples, size), BF),
                pltpu.VMEM((far_slots * group, samples), F32),
                sems(len(far_chips)),
                sems(row_count, columns),
            ],
            compiler_params=PARAMS,
        )(rows_here, lists_here, owned_here, far(slices), far(features))
        covariance = lax.all_to_all(partial, "row", split_axis=0, concat_axis=0, tiled=True)

    with jax.named_scope("near"):
        blocks_out[early:], got_blocks, _ = lax.optimization_barrier(
            (blocks_out[early:], got_blocks, partial[0, 0])
        )
        got_blocks = got_blocks + [send(n) for n in range(early, len(steps))]
        base, d, near_sums = pl.pallas_call(
            functools.partial(near_kernel, near, col_count),
            in_specs=[SMEM, SMEM, SMEM] + [HBM] * (3 + near_count),
            out_specs=[HBM] * 2 + [VMEM],
            out_shape=[tile_out, tile_out, pltpu.HBM((columns, size, 2 * size), F32)],
            scratch_shapes=[
                pltpu.VMEM((len(near) * CHUNK, samples, size), BF),
                pltpu.VMEM((columns, samples, size), BF),
                tile_vmem, tile_vmem, tile_vmem, tile_vmem,
                sems(near_count), sems(columns), sems(4, chunks),
            ],
            compiler_params=PARAMS,
        )(
            my_list, live, my_owned, far(features), far(theta), far(tiles),
            *[far(block) for block in got_blocks[:near_count]],
        )
        covariance, got_blocks, base, d, near_sums = lax.optimization_barrier(
            (covariance, got_blocks, base, d, near_sums)
        )

    with jax.named_scope("first"):
        base, d, pieces = pl.pallas_call(
            functools.partial(first_kernel, far_chips, col_count),
            in_specs=[SMEM, SMEM, VMEM] + [HBM] * 5,
            out_specs=[HBM, HBM, VMEM],
            out_shape=[tile_out, tile_out, shape(piece_shape, F32)],
            scratch_shapes=[
                tile_vmem, tile_vmem, tile_vmem, tile_vmem, sums, sems(1), sems(4, chunks),
            ],
            input_output_aliases={6: 0, 7: 1},
            compiler_params=PARAMS,
        )(
            my_list, live, covariance, far(near_sums), far(theta), far(tiles), far(base), far(d)
        )

    for sweep in range(1, SWEEPS):
        last = sweep == SWEEPS - 1
        with jax.named_scope("exchange"):
            got = lax.all_to_all(pieces, "row", split_axis=0, concat_axis=0, tiled=True)
            flat_shape = (row_count * columns, group, size)
            summed = pl.pallas_call(
                sum_kernel,
                in_specs=[VMEM, VMEM],
                out_specs=VMEM,
                out_shape=shape(flat_shape, F32),
                compiler_params=PARAMS,
            )(same, got.reshape(flat_shape))
            q = lax.all_to_all(
                summed.reshape(piece_shape), "row", split_axis=0, concat_axis=0, tiled=True
            )
        with jax.named_scope("diagonal"):
            t = pl.pallas_call(
                functools.partial(diagonal_kernel, steps),
                in_specs=[SMEM, HBM, HBM, VMEM] + [HBM] * col_count,
                out_specs=HBM,
                out_shape=tile_out,
                scratch_shapes=[
                    tile_vmem, tile_vmem, pltpu.VMEM(tile_shape, BF), tile_vmem,
                    sems(col_count), sems(3, chunks),
                ],
                compiler_params=PARAMS,
            )(my_list, far(base), far(d), col_diag, *[far(block) for block in got_blocks])
        with jax.named_scope("sweep"):
            result = pl.pallas_call(
                functools.partial(sweep_kernel, last),
                in_specs=[SMEM, SMEM, HBM, HBM, HBM, VMEM],
                out_specs=[HBM] if last else [HBM, VMEM],
                out_shape=[tile_out] if last else [tile_out, shape(piece_shape, F32)],
                scratch_shapes=[
                    tile_vmem, tile_vmem, pltpu.VMEM((slots, size, 2 * size), BF), tile_vmem,
                    pltpu.VMEM((columns, 2 * size, 2 * size), BF), sems(4, chunks),
                ] + ([] if last else [sums]),
                compiler_params=PARAMS,
            )(my_list, live, far(t), far(theta), far(pairs), q)
            d = result[0]
            if not last:
                pieces = result[1]
    return d.reshape(precision_tiles.shape)


def solution(mesh):
    return jax.shard_map(
        body,
        mesh=mesh,
        in_specs=(
            P("col", None, None),
            P("col", None, None),
            P("row", "col", None, None, None),
            P("row", "col", None, None, None),
            P(),
            P(),
            P(),
            P(),
        ),
        out_specs=P("row", "col", None, None, None),
        check_vma=False,
    )
```

```python
import functools

import jax
import jax.numpy as jnp
from jax import lax
from jax.experimental import pallas as pl
from jax.experimental.pallas import tpu as pltpu
from jax.sharding import PartitionSpec as P

SWEEPS = 4
STEP = 0.3
LAMBDA = 0.3 * 0.6
PER_STEP = 8
CHUNK = 4
CORES = 2

BF = jnp.bfloat16
F32 = jnp.float32
VMEM = pl.BlockSpec(memory_space=pltpu.VMEM)
HBM = pl.BlockSpec(memory_space=pltpu.HBM)
SMEM = pl.BlockSpec(memory_space=pltpu.SMEM)
PARAMS = pltpu.CompilerParams(vmem_limit_bytes=20 * 1024 * 1024)


def split(x):
    high = x.astype(BF)
    low = (x - high.astype(F32)).astype(BF)
    return high, low


def dot(a, b):
    return jnp.dot(a, b, preferred_element_type=F32)


def shrink(x):
    return x - jnp.clip(x, -LAMBDA, LAMBDA)


def slice_kernel(group, features_ref, out_ref):
    r = lax.axis_index("row")
    variables = features_ref.shape[2]
    wanted = lax.broadcasted_iota(jnp.int32, (group, variables), 0) + r * group
    pick = (lax.broadcasted_iota(jnp.int32, (group, variables), 1) == wanted).astype(BF)
    for block in range(features_ref.shape[0]):
        rows = lax.dot_general(
            pick, features_ref[block], (((1,), (1,)), ((), ())), preferred_element_type=F32
        )
        out_ref[block] = rows.astype(BF)


def split_kernel(tiles_ref, out_ref):
    for s in range(tiles_ref.shape[0]):
        out_ref[s] = jnp.concatenate(split(tiles_ref[s]), axis=1)


def gather_kernel(steps, wanted_ref, features, diag, *rest):
    outs, (near_ref, far_ref, sems, out_sems) = rest[:-4], rest[-4:]
    c = lax.axis_index("col")
    samples = features.shape[1]
    size = diag.shape[1]
    near_count = near_ref.shape[0]
    copies = []
    backs = []
    for n, ((dz, dk), out) in enumerate(zip(steps, outs)):
        target = holder(c, -dz, dk, wanted_ref.shape[0])
        place = near_ref.at[n] if n < near_count else far_ref.at[n - near_count]
        begin = samples if n < near_count else 0
        mine = []
        for p in range(out.shape[0]):
            block = wanted_ref[target, p]
            if n < near_count:
                mine.append(pltpu.make_async_copy(
                    features.at[block], place.at[p, pl.ds(0, samples)], sems.at[n, p, 0]
                ))
            mine.append(pltpu.make_async_copy(
                diag.at[block], place.at[p, pl.ds(begin, size)], sems.at[n, p, 1]
            ))
        for copy in mine:
            copy.start()
        copies.append(mine)
        backs.append(pltpu.make_async_copy(place, out, out_sems.at[n]))
    for mine, back in zip(copies, backs):
        for copy in mine:
            copy.wait()
        back.start()
    for back in backs:
        back.wait()


def holder(c, dz, dk, col_count):
    chips = col_count // CORES
    z = lax.rem(c // CORES + dz + chips, chips)
    return z * CORES + lax.rem(c + dk, CORES)


def chip_at(dz, col_count):
    return lax.rem(lax.axis_index("col") // CORES + dz, col_count // CORES)


class Tiles:
    def __init__(self, far_ref, near_ref, sem, back=False):
        self.refs = (near_ref, far_ref) if back else (far_ref, near_ref)
        self.near = near_ref
        self.sem = sem
        self.chunks = near_ref.shape[0] // CHUNK

    def copy(self, i):
        part = pl.ds(i * CHUNK, CHUNK)
        source, target = (ref.at[part] for ref in self.refs)
        return pltpu.make_async_copy(source, target, self.sem.at[i])

    def start(self, i):
        self.copy(i).start()

    def wait(self, i):
        self.copy(i).wait()


def start_all(arrays, chunks):
    for i in range(chunks):
        for array in arrays:
            array.start(i)


def each_slot(chunks, arrays, outs, slot_step):
    def step(i, carry):
        for array in arrays:
            array.wait(i)
        for s in range(CHUNK):
            slot_step(i * CHUNK + s)
        for out in outs:
            out.start(i)
        return carry

    lax.fori_loop(0, chunks, step, 0)
    for i in range(chunks):
        for out in outs:
            out.wait(i)


def covariance_kernel(
    far, col_count, rows_ref, lists_ref, owned_ref, far_slices, features, out_ref,
    slices_ref, right_ref, slice_sem, right_sem,
):
    owners = rows_ref.shape[0]
    columns = owned_ref.shape[1]
    group = slices_ref.shape[1]
    samples = features.shape[1]
    size = features.shape[2]
    part = far_slices.shape[0] * CORES // col_count

    def slice_copy(n):
        here = pl.ds(chip_at(far[n], col_count) * part, part)
        return pltpu.make_async_copy(
            far_slices.at[here], slices_ref.at[here], slice_sem.at[n]
        )

    def right_copy(owner, a):
        return pltpu.make_async_copy(
            features.at[owned_ref[owner, a]], right_ref.at[owner, a], right_sem.at[owner, a]
        )

    for n in range(len(far)):
        slice_copy(n).start()
    for owner in range(owners):
        for a in range(columns):
            right_copy(owner, a).start()
    for n in range(len(far)):
        slice_copy(n).wait()

    def owner_step(owner, carry):
        for a in range(columns):
            right_copy(owner, a).wait()
        left = jnp.concatenate(
            [
                slices_ref[rows_ref[owner, chip_at(dz, col_count) * CHUNK + s]].astype(F32)
                for dz in far for s in range(CHUNK)
            ],
            axis=0,
        ).astype(BF)
        right = jnp.concatenate([right_ref[owner, a] for a in range(columns)], axis=1)
        both = dot(left, right) * (1.0 / samples)
        for n, dz in enumerate(far):
            first = chip_at(dz, col_count) * CHUNK
            for s in range(CHUNK):
                k = n * CHUNK + s
                rows = both[k * group:(k + 1) * group]
                out_ref[owner, k] = jnp.where(
                    lists_ref[owner, first + s] == 0, rows[:, :size], rows[:, size:]
                )
        return carry

    lax.fori_loop(0, owners, owner_step, 0)


def pair(x):
    size = x.shape[0]
    high = x[:, :size]
    return jnp.concatenate(
        [x, jnp.concatenate([high, jnp.zeros_like(high)], axis=1)], axis=0
    )


def add_product(d, column, tile, sums_ref):
    left = jnp.concatenate(split(d.T), axis=1)
    sums_ref[column] += dot(left, pair(tile))


def write_sums(sums_ref, out_ref):
    pieces, columns, group, size = out_ref.shape
    for a in range(columns):
        total = sums_ref[a][:, :size] + sums_ref[a][:, size:]
        out_ref[:, a] = total.reshape(pieces, group, size)


def first_step(slot, covariance, list_ref, live_ref, theta_ref, tiles_ref, base_ref, d_ref, sums_ref):
    theta = theta_ref[slot]
    tile = tiles_ref[slot]
    base = theta - STEP * (covariance - tile)
    d = jnp.where(slot < live_ref[0], shrink(base) - theta, 0.0)
    base_ref[slot] = base
    d_ref[slot] = d
    halves = jnp.concatenate(split(tile), axis=1)
    add_product(d, list_ref[slot], halves, sums_ref)


def near_kernel(near, col_count, list_ref, live_ref, owned_ref, features, far_theta, far_tiles, *rest):
    count = len(near) * CORES
    blocks = rest[:count]
    (
        far_base, far_d, sums_ref, left_ref, right_ref, theta_ref, tiles_ref, base_ref, d_ref,
        left_sem, right_sem, sems,
    ) = rest[count:]
    slots, size, _ = theta_ref.shape
    samples = features.shape[1]
    per_source = CHUNK // CORES
    core = lax.rem(lax.axis_index("col"), CORES)
    arrays = [Tiles(far_theta, theta_ref, sems.at[0]), Tiles(far_tiles, tiles_ref, sems.at[1])]
    outs = [Tiles(far_base, base_ref, sems.at[2], True), Tiles(far_d, d_ref, sems.at[3], True)]

    def left_copy(n):
        place = n // CORES * CHUNK + lax.rem(core + n % CORES, CORES) * per_source
        return pltpu.make_async_copy(
            blocks[n].at[:, pl.ds(0, samples)], left_ref.at[pl.ds(place, per_source)],
            left_sem.at[n],
        )

    def right_copy(a):
        return pltpu.make_async_copy(
            features.at[owned_ref[a]], right_ref.at[a], right_sem.at[a]
        )

    for a in range(right_ref.shape[0]):
        right_copy(a).start()
    for n in range(count):
        left_copy(n).start()
    for dz in near:
        for array in arrays:
            array.start(chip_at(dz, col_count))
    sums_ref[...] = jnp.zeros_like(sums_ref)
    for a in range(right_ref.shape[0]):
        right_copy(a).wait()
    for n in range(count):
        left_copy(n).wait()
    for n, dz in enumerate(near):
        chip = chip_at(dz, col_count)
        for array in arrays:
            array.wait(chip)
        for s in range(CHUNK):
            slot = chip * CHUNK + s
            covariance = lax.dot_general(
                left_ref[n * CHUNK + s], right_ref[list_ref[slot]],
                (((0,), (0,)), ((), ())), preferred_element_type=F32,
            ) * (1.0 / samples)
            first_step(
                slot, covariance, list_ref, live_ref, theta_ref, tiles_ref, base_ref, d_ref,
                sums_ref,
            )
        for out in outs:
            out.start(chip)
    for dz in near:
        for out in outs:
            out.wait(chip_at(dz, col_count))


def first_kernel(
    far, col_count, list_ref, live_ref, cov_ref, near_sums, far_theta, far_tiles, in_base, in_d,
    far_base, far_d, out_ref, theta_ref, tiles_ref, base_ref, d_ref, sums_ref, sum_sem, sems,
):
    slots, size, _ = theta_ref.shape
    arrays = [Tiles(far_theta, theta_ref, sems.at[0]), Tiles(far_tiles, tiles_ref, sems.at[1])]
    outs = [Tiles(far_base, base_ref, sems.at[2], True), Tiles(far_d, d_ref, sems.at[3], True)]
    bring = pltpu.make_async_copy(near_sums, sums_ref, sum_sem.at[0])
    bring.start()
    for dz in far:
        for array in arrays:
            array.start(chip_at(dz, col_count))
    bring.wait()

    def step(n, carry):
        chip = chip_at(n + far[0], col_count)
        for array in arrays:
            array.wait(chip)
        for s in range(CHUNK):
            slot = chip * CHUNK + s
            covariance = cov_ref[:, n * CHUNK + s].reshape(size, size)
            first_step(
                slot, covariance, list_ref, live_ref, theta_ref, tiles_ref, base_ref, d_ref,
                sums_ref,
            )
        for out in outs:
            out.start(chip)
        return carry

    lax.fori_loop(0, len(far), step, 0)
    write_sums(sums_ref, out_ref)
    for dz in far:
        for out in outs:
            out.wait(chip_at(dz, col_count))


def diagonal_kernel(steps, list_ref, far_base, far_d, col_diag_ref, *rest):
    far_diag = rest[:-7]
    far_out, base_ref, d_ref, diag_ref, out_ref, diag_sem, sems = rest[-7:]
    slots, size, _ = d_ref.shape
    chunks = slots // CHUNK
    c = lax.axis_index("col")
    per_source = slots // len(far_diag)
    arrays = [Tiles(far_base, base_ref, sems.at[0]), Tiles(far_d, d_ref, sems.at[1])]
    out = Tiles(far_out, out_ref, sems.at[2], True)

    def diag_copy(n):
        block = far_diag[n]
        place = holder(c, *steps[n], len(far_diag)) * per_source
        return pltpu.make_async_copy(
            block.at[:, pl.ds(block.shape[1] - size, size)],
            diag_ref.at[pl.ds(place, per_source)],
            diag_sem.at[n],
        )

    for n in range(len(far_diag)):
        diag_copy(n).start()
    start_all(arrays, chunks)
    for n in range(len(far_diag)):
        diag_copy(n).wait()

    def slot_step(slot):
        d = d_ref[slot]
        half = dot(diag_ref[slot], jnp.concatenate(split(d), axis=1))
        half = half[:, :size] + half[:, size:]
        right = col_diag_ref[list_ref[slot]]
        both = dot(
            jnp.concatenate(split(half), axis=1), jnp.concatenate([right, right], axis=0)
        )
        out_ref[slot] = base_ref[slot] + d - STEP * both

    each_slot(chunks, arrays, [out], slot_step)


def sum_kernel(same_ref, in_ref, out_ref):
    same = same_ref[...].astype(BF)
    for g in range(in_ref.shape[1]):
        x = in_ref[:, g, :]
        x1, rest = x.astype(BF), x
        rest = rest - x1.astype(F32)
        x2 = rest.astype(BF)
        rest = rest - x2.astype(F32)
        x3 = rest.astype(BF)
        out_ref[:, g, :] = dot(
            jnp.concatenate([same, same, same], axis=1), jnp.concatenate([x1, x2, x3], axis=0)
        )


def sweep_kernel(
    last, list_ref, live_ref, far_t, far_theta, far_pairs, q_ref, far_d, *rest
):
    if last:
        t_ref, theta_ref, pairs_ref, d_ref, right_ref, sems = rest
    else:
        out_ref, t_ref, theta_ref, pairs_ref, d_ref, right_ref, sems, sums_ref = rest
    slots, size, _ = theta_ref.shape
    chunks = slots // CHUNK
    arrays = [
        Tiles(far_pairs, pairs_ref, sems.at[0]),
        Tiles(far_t, t_ref, sems.at[1]),
        Tiles(far_theta, theta_ref, sems.at[2]),
    ]
    out = Tiles(far_d, d_ref, sems.at[3], True)
    start_all(arrays, chunks)
    for a in range(q_ref.shape[1]):
        q = q_ref[:, a].reshape(size, size)
        right_ref[a] = pair(jnp.concatenate(split(q), axis=1))
    if not last:
        sums_ref[...] = jnp.zeros_like(sums_ref)

    def slot_step(slot):
        column = list_ref[slot]
        both = dot(pairs_ref[slot], right_ref[column])
        product = both[:, :size] + both[:, size:]
        d = shrink(t_ref[slot] - STEP * product) - theta_ref[slot]
        d = jnp.where(slot < live_ref[0], d, 0.0)
        d_ref[slot] = d
        if not last:
            add_product(d, column, pairs_ref[slot], sums_ref)

    each_slot(chunks, arrays, [out], slot_step)
    if not last:
        write_sums(sums_ref, out_ref)


def shape(dims, dtype):
    return jax.ShapeDtypeStruct(dims, dtype)


def far(x):
    return pltpu.with_memory_space_constraint(x, pltpu.HBM)


def slot_blocks(*dims):
    return pl.BlockSpec((PER_STEP,) + dims, lambda i: (i,) + (0,) * len(dims))


def body(
    features,
    diag_inverse,
    precision_tiles,
    inverse_tiles,
    slot_rows,
    slot_columns,
    owned_columns,
    live_counts,
):
    row_count = lax.axis_size("row")
    col_count = lax.axis_size("col")
    r = lax.axis_index("row")
    c = lax.axis_index("col")
    blocks, samples, size = features.shape
    slots = precision_tiles.shape[2]
    columns = owned_columns.shape[2]
    per_source = slots // col_count
    group = size // row_count
    theta = precision_tiles[0, 0]
    tiles = inverse_tiles[0, 0]
    tile_shape = (slots, size, size)
    piece_shape = (row_count, columns, group, size)

    with jax.named_scope("slices"):
        per_step = 8
        mine = pl.pallas_call(
            functools.partial(slice_kernel, group),
            grid=(blocks // per_step,),
            in_specs=[pl.BlockSpec((per_step, samples, size), lambda i: (i, 0, 0))],
            out_specs=pl.BlockSpec((per_step, group, samples), lambda i: (i, 0, 0)),
            out_shape=shape((blocks, group, samples), BF),
        )(features)
        slices = lax.all_gather(mine, "col", axis=0, tiled=True)

    with jax.named_scope("tables"):
        rows_here = lax.dynamic_index_in_dim(slot_rows, c, 1, keepdims=False)
        lists_here = lax.dynamic_index_in_dim(slot_columns, c, 1, keepdims=False)
        owned_here = lax.dynamic_index_in_dim(owned_columns, c, 1, keepdims=False) - c * blocks
        my_list = lax.dynamic_index_in_dim(lists_here, r, 0, keepdims=False)
        live = lax.dynamic_slice(live_counts, (r, c), (1, 1)).reshape(1)
        wanted = lax.dynamic_slice(
            slot_rows, (r, 0, c * per_source), (1, col_count, per_source)
        ).reshape(col_count, per_source) - c * blocks
        flat = owned_here.reshape(-1)
        same = (flat[:, None] == flat[None, :]).astype(F32)
        my_owned = lax.dynamic_index_in_dim(owned_here, r, 0, keepdims=False)
        col_diag = jnp.take(diag_inverse, my_owned, axis=0)

    tile_vmem = pltpu.VMEM(tile_shape, F32)
    tile_out = pltpu.HBM(tile_shape, F32)
    sums = pltpu.VMEM((columns, size, 2 * size), F32)
    chunks = slots // CHUNK

    def sems(*dims):
        return pltpu.SemaphoreType.DMA(dims)

    with jax.named_scope("split"):
        pairs = pl.pallas_call(
            split_kernel,
            grid=(slots // PER_STEP,),
            in_specs=[slot_blocks(size, size)],
            out_specs=slot_blocks(size, 2 * size),
            out_shape=pltpu.HBM((slots, size, 2 * size), BF),
        )(far(tiles))

    with jax.named_scope("blocks"):
        chips = col_count // CORES
        near = [0, 1, chips - 1]
        far_chips = list(range(2, chips - 1))
        cores = range(CORES)
        steps = [(dz, dk) for dz in near for dk in cores]
        steps += [(dz, dk) for dz in (2, chips - 2) for dk in cores]
        early = len(steps)
        steps += [(dz, dk) for dz in far_chips[1:-1] for dk in cores]
        near_count = len(near) * CORES
        block_shapes = [
            (per_source, samples + size if n < near_count else size, size)
            for n in range(len(steps))
        ]
        mine, wanted = lax.optimization_barrier((mine, wanted))
        blocks_out = list(pl.pallas_call(
            functools.partial(gather_kernel, steps),
            in_specs=[SMEM, HBM, HBM],
            out_specs=[HBM] * len(steps),
            out_shape=[pltpu.HBM(dims, BF) for dims in block_shapes],
            scratch_shapes=[
                pltpu.VMEM((near_count,) + block_shapes[0], BF),
                pltpu.VMEM((len(steps) - near_count,) + block_shapes[-1], BF),
                sems(len(steps), per_source, 2),
                sems(len(steps)),
            ],
            compiler_params=PARAMS,
        )(wanted, far(features), far(diag_inverse)))

        def send(n):
            dz, dk = steps[n]
            if dz == 0 and dk == 0:
                return blocks_out[n]
            pairs_of = [
                (h, (h // CORES - dz) % chips * CORES + (h + dk) % CORES)
                for h in range(col_count)
            ]
            return lax.ppermute(blocks_out[n], "col", pairs_of)

        got_blocks = [send(n) for n in range(early)]
        base, d, near_sums = pl.pallas_call(
            functools.partial(near_kernel, near, col_count),
            in_specs=[SMEM, SMEM, SMEM] + [HBM] * (3 + near_count),
            out_specs=[HBM] * 2 + [VMEM],
            out_shape=[tile_out, tile_out, pltpu.HBM((columns, size, 2 * size), F32)],
            scratch_shapes=[
                pltpu.VMEM((len(near) * CHUNK, samples, size), BF),
                pltpu.VMEM((columns, samples, size), BF),
                tile_vmem, tile_vmem, tile_vmem, tile_vmem,
                sems(near_count), sems(columns), sems(4, chunks),
            ],
            compiler_params=PARAMS,
        )(
            my_list, live, my_owned, far(features), far(theta), far(tiles),
            *[far(block) for block in got_blocks[:near_count]],
        )
        slices, pairs, got_blocks, base, d, near_sums = lax.optimization_barrier(
            (slices, pairs, got_blocks, base, d, near_sums)
        )

    far_slots = len(far_chips) * CHUNK
    with jax.named_scope("covariance"):
        partial = pl.pallas_call(
            functools.partial(covariance_kernel, far_chips, col_count),
            in_specs=[SMEM, SMEM, SMEM, HBM, HBM],
            out_specs=VMEM,
            out_shape=pltpu.HBM((row_count, far_slots, group, size), F32),
            scratch_shapes=[
                pltpu.VMEM(slices.shape, BF),
                pltpu.VMEM((row_count, columns, samples, size), BF),
                sems(len(far_chips)),
                sems(row_count, columns),
            ],
            compiler_params=PARAMS,
        )(rows_here, lists_here, owned_here, far(slices), far(features))
        covariance = lax.all_to_all(partial, "row", split_axis=0, concat_axis=0, tiled=True)

    with jax.named_scope("diag"):
        blocks_out[early:], _ = lax.optimization_barrier((blocks_out[early:], partial[0, 0]))
        got_blocks = got_blocks + [send(n) for n in range(early, len(steps))]
        covariance, got_blocks = lax.optimization_barrier((covariance, got_blocks))

    with jax.named_scope("first"):
        base, d, pieces = pl.pallas_call(
            functools.partial(first_kernel, far_chips, col_count),
            in_specs=[SMEM, SMEM, VMEM] + [HBM] * 5,
            out_specs=[HBM, HBM, VMEM],
            out_shape=[tile_out, tile_out, shape(piece_shape, F32)],
            scratch_shapes=[
                tile_vmem, tile_vmem, tile_vmem, tile_vmem, sums, sems(1), sems(4, chunks),
            ],
            input_output_aliases={6: 0, 7: 1},
            compiler_params=PARAMS,
        )(
            my_list, live, covariance, far(near_sums), far(theta), far(tiles), far(base), far(d)
        )

    for sweep in range(1, SWEEPS):
        last = sweep == SWEEPS - 1
        with jax.named_scope("exchange"):
            got = lax.all_to_all(pieces, "row", split_axis=0, concat_axis=0, tiled=True)
            flat_shape = (row_count * columns, group, size)
            summed = pl.pallas_call(
                sum_kernel,
                in_specs=[VMEM, VMEM],
                out_specs=VMEM,
                out_shape=shape(flat_shape, F32),
                compiler_params=PARAMS,
            )(same, got.reshape(flat_shape))
            q = lax.all_to_all(
                summed.reshape(piece_shape), "row", split_axis=0, concat_axis=0, tiled=True
            )
        with jax.named_scope("diagonal"):
            t = pl.pallas_call(
                functools.partial(diagonal_kernel, steps),
                in_specs=[SMEM, HBM, HBM, VMEM] + [HBM] * col_count,
                out_specs=HBM,
                out_shape=tile_out,
                scratch_shapes=[
                    tile_vmem, tile_vmem, pltpu.VMEM(tile_shape, BF), tile_vmem,
                    sems(col_count), sems(3, chunks),
                ],
                compiler_params=PARAMS,
            )(my_list, far(base), far(d), col_diag, *[far(block) for block in got_blocks])
        with jax.named_scope("sweep"):
            result = pl.pallas_call(
                functools.partial(sweep_kernel, last),
                in_specs=[SMEM, SMEM, HBM, HBM, HBM, VMEM],
                out_specs=[HBM] if last else [HBM, VMEM],
                out_shape=[tile_out] if last else [tile_out, shape(piece_shape, F32)],
                scratch_shapes=[
                    tile_vmem, tile_vmem, pltpu.VMEM((slots, size, 2 * size), BF), tile_vmem,
                    pltpu.VMEM((columns, 2 * size, 2 * size), BF), sems(4, chunks),
                ] + ([] if last else [sums]),
                compiler_params=PARAMS,
            )(my_list, live, far(t), far(theta), far(pairs), q)
            d = result[0]
            if not last:
                pieces = result[1]
    return d.reshape(precision_tiles.shape)


def solution(mesh):
    return jax.shard_map(
        body,
        mesh=mesh,
        in_specs=(
            P("col", None, None),
            P("col", None, None),
            P("row", "col", None, None, None),
            P("row", "col", None, None, None),
            P(),
            P(),
            P(),
            P(),
        ),
        out_specs=P("row", "col", None, None, None),
        check_vma=False,
    )
```

```python
import functools

import jax
import jax.numpy as jnp
from jax import lax
from jax.experimental import pallas as pl
from jax.experimental.pallas import tpu as pltpu
from jax.sharding import PartitionSpec as P

SWEEPS = 4
STEP = 0.3
LAMBDA = 0.3 * 0.6
PER_STEP = 8
CHUNK = 4
CORES = 2
MANY = 8

BF = jnp.bfloat16
F32 = jnp.float32
VMEM = pl.BlockSpec(memory_space=pltpu.VMEM)
HBM = pl.BlockSpec(memory_space=pltpu.HBM)
SMEM = pl.BlockSpec(memory_space=pltpu.SMEM)
PARAMS = pltpu.CompilerParams(vmem_limit_bytes=20 * 1024 * 1024)


def split(x):
    high = x.astype(BF)
    low = (x - high.astype(F32)).astype(BF)
    return high, low


def dot(a, b):
    return jnp.dot(a, b, preferred_element_type=F32)


def shrink(x):
    return x - jnp.clip(x, -LAMBDA, LAMBDA)


def slice_kernel(group, features, out_ref, near_ref, sems):
    r = lax.axis_index("row")
    blocks, _, variables = features.shape
    parts = sems.shape[0]
    count = blocks // parts

    def copy(i):
        part = pl.ds(i * count, count)
        return pltpu.make_async_copy(features.at[part], near_ref.at[part], sems.at[i])

    for i in range(parts):
        copy(i).start()
    wanted = lax.broadcasted_iota(jnp.int32, (group, variables), 0) + r * group
    pick = (lax.broadcasted_iota(jnp.int32, (group, variables), 1) == wanted).astype(BF)

    def step(i, carry):
        copy(i).wait()
        for b in range(count):
            rows = lax.dot_general(
                pick, near_ref[i * count + b], (((1,), (1,)), ((), ())),
                preferred_element_type=F32,
            )
            out_ref[i * count + b] = rows.astype(BF)
        return carry

    lax.fori_loop(0, parts, step, 0)


def split_kernel(tiles_ref, out_ref):
    for s in range(tiles_ref.shape[0]):
        out_ref[s] = jnp.concatenate(split(tiles_ref[s]), axis=1)


def gather_kernel(steps, wanted_ref, features, diag, *rest):
    outs, (near_ref, far_ref, sems, out_sems) = rest[:-4], rest[-4:]
    c = lax.axis_index("col")
    samples = features.shape[1]
    size = diag.shape[1]
    near_count = near_ref.shape[0]
    copies = []
    backs = []
    for n, ((dz, dk), out) in enumerate(zip(steps, outs)):
        target = holder(c, -dz, dk, wanted_ref.shape[0])
        place = near_ref.at[n] if n < near_count else far_ref.at[n - near_count]
        begin = samples if n < near_count else 0
        mine = []
        for p in range(out.shape[0]):
            block = wanted_ref[target, p]
            if n < near_count:
                mine.append(pltpu.make_async_copy(
                    features.at[block], place.at[p, pl.ds(0, samples)], sems.at[n, p, 0]
                ))
            mine.append(pltpu.make_async_copy(
                diag.at[block], place.at[p, pl.ds(begin, size)], sems.at[n, p, 1]
            ))
        for copy in mine:
            copy.start()
        copies.append(mine)
        backs.append(pltpu.make_async_copy(place, out, out_sems.at[n]))
    for mine, back in zip(copies, backs):
        for copy in mine:
            copy.wait()
        back.start()
    for back in backs:
        back.wait()


def holder(c, dz, dk, col_count):
    chips = col_count // CORES
    z = lax.rem(c // CORES + dz + chips, chips)
    return z * CORES + lax.rem(c + dk, CORES)


def chip_at(dz, col_count):
    return lax.rem(lax.axis_index("col") // CORES + dz, col_count // CORES)


class Tiles:
    def __init__(self, far_ref, near_ref, sem, back=False, count=CHUNK):
        self.refs = (near_ref, far_ref) if back else (far_ref, near_ref)
        self.sem = sem
        self.count = count

    def copy(self, i):
        part = pl.ds(i * self.count, self.count)
        source, target = (ref.at[part] for ref in self.refs)
        return pltpu.make_async_copy(source, target, self.sem.at[i])

    def start(self, i):
        self.copy(i).start()

    def wait(self, i):
        self.copy(i).wait()


def start_all(arrays, chunks):
    for i in range(chunks):
        for array in arrays:
            array.start(i)


def each_slot(chunks, arrays, outs, slot_step):
    def step(i, carry):
        for array in arrays:
            array.wait(i)
        for s in range(CHUNK):
            slot_step(i * CHUNK + s)
        for out in outs:
            out.start(i)
        return carry

    lax.fori_loop(0, chunks, step, 0)
    for i in range(chunks):
        for out in outs:
            out.wait(i)


def covariance_kernel(
    far, col_count, rows_ref, lists_ref, owned_ref, far_slices, features, far_out,
    slices_ref, right_ref, out_ref, slice_sem, right_sem, out_sem,
):
    owners = rows_ref.shape[0]
    columns = owned_ref.shape[1]
    group = slices_ref.shape[1]
    _, samples, size = features.shape
    part = far_slices.shape[0] * CORES // col_count
    slots = [chip_at(dz, col_count) * CHUNK + s for dz in far for s in range(CHUNK)]

    def slice_copy(n):
        here = pl.ds(chip_at(far[n], col_count) * part, part)
        return pltpu.make_async_copy(
            far_slices.at[here], slices_ref.at[here], slice_sem.at[n]
        )

    def right_copy(owner, a):
        return pltpu.make_async_copy(
            features.at[owned_ref[owner, a]], right_ref.at[owner, a], right_sem.at[owner, a]
        )

    def out_copy(owner):
        return pltpu.make_async_copy(out_ref.at[owner], far_out.at[owner], out_sem.at[owner])

    for n in range(len(far)):
        slice_copy(n).start()
    for owner in range(owners):
        for a in range(columns):
            right_copy(owner, a).start()
    for n in range(len(far)):
        slice_copy(n).wait()

    def owner_step(owner, carry):
        for a in range(columns):
            right_copy(owner, a).wait()
        left = jnp.concatenate(
            [slices_ref[rows_ref[owner, slot]].astype(F32) for slot in slots], axis=0
        ).astype(BF)
        right = jnp.concatenate([right_ref[owner, a] for a in range(columns)], axis=1)
        both = dot(left, right) * (1.0 / samples)
        for k, slot in enumerate(slots):
            rows = both[k * group:(k + 1) * group]
            out_ref[owner, k] = jnp.where(
                lists_ref[owner, slot] == 0, rows[:, :size], rows[:, size:]
            )
        out_copy(owner).start()
        return carry

    lax.fori_loop(0, owners, owner_step, 0, unroll=2)
    for owner in range(owners):
        out_copy(owner).wait()


def pair(x):
    size = x.shape[0]
    high = x[:, :size]
    return jnp.concatenate(
        [x, jnp.concatenate([high, jnp.zeros_like(high)], axis=1)], axis=0
    )


def add_products(slots, ds, tiles, list_ref, sums_ref):
    lefts = [jnp.concatenate(split(d.T), axis=1) for d in ds]
    products = [dot(left, pair(tile)) for left, tile in zip(lefts, tiles)]
    for slot, product in zip(slots, products):
        sums_ref[list_ref[slot]] += product


def write_sums(sums_ref, out_ref):
    pieces, columns, group, size = out_ref.shape
    for a in range(columns):
        total = sums_ref[a][:, :size] + sums_ref[a][:, size:]
        out_ref[:, a] = total.reshape(pieces, group, size)


def first_steps(
    slots, covariances, list_ref, live_ref, theta_ref, tiles_ref, base_ref, d_ref, sums_ref
):
    ds = []
    tiles = []
    for slot, covariance in zip(slots, covariances):
        theta = theta_ref[slot]
        tile = tiles_ref[slot]
        base = theta - STEP * (covariance - tile)
        base_ref[slot] = base
        ds.append(jnp.where(slot < live_ref[0], shrink(base) - theta, 0.0))
        tiles.append(jnp.concatenate(split(tile), axis=1))
    for slot, d in zip(slots, ds):
        d_ref[slot] = d
    add_products(slots, ds, tiles, list_ref, sums_ref)


def near_kernel(near, col_count, list_ref, live_ref, owned_ref, features, far_theta, far_tiles, *rest):
    count = len(near) * CORES
    blocks = rest[:count]
    (
        far_base, far_d, sums_ref, left_ref, right_ref, theta_ref, tiles_ref, base_ref, d_ref,
        left_sem, right_sem, sems,
    ) = rest[count:]
    slots, size, _ = theta_ref.shape
    samples = features.shape[1]
    per_source = CHUNK // CORES
    core = lax.rem(lax.axis_index("col"), CORES)
    arrays = [Tiles(far_theta, theta_ref, sems.at[0]), Tiles(far_tiles, tiles_ref, sems.at[1])]
    outs = [Tiles(far_base, base_ref, sems.at[2], True), Tiles(far_d, d_ref, sems.at[3], True)]

    def left_copy(n):
        place = n // CORES * CHUNK + lax.rem(core + n % CORES, CORES) * per_source
        return pltpu.make_async_copy(
            blocks[n].at[:, pl.ds(0, samples)], left_ref.at[pl.ds(place, per_source)],
            left_sem.at[n],
        )

    def right_copy(a):
        return pltpu.make_async_copy(
            features.at[owned_ref[a]], right_ref.at[a], right_sem.at[a]
        )

    for a in range(right_ref.shape[0]):
        right_copy(a).start()
    for n in range(count):
        left_copy(n).start()
    for dz in near:
        for array in arrays:
            array.start(chip_at(dz, col_count))
    sums_ref[...] = jnp.zeros_like(sums_ref)
    for a in range(right_ref.shape[0]):
        right_copy(a).wait()
    for n in range(count):
        left_copy(n).wait()
    for n, dz in enumerate(near):
        chip = chip_at(dz, col_count)
        for array in arrays:
            array.wait(chip)
        slots_here = [chip * CHUNK + s for s in range(CHUNK)]
        covariances = [
            lax.dot_general(
                left_ref[n * CHUNK + s], right_ref[list_ref[slot]],
                (((0,), (0,)), ((), ())), preferred_element_type=F32,
            ) * (1.0 / samples)
            for s, slot in enumerate(slots_here)
        ]
        first_steps(
            slots_here, covariances, list_ref, live_ref, theta_ref, tiles_ref, base_ref, d_ref,
            sums_ref,
        )
        for out in outs:
            out.start(chip)
    for dz in near:
        for out in outs:
            out.wait(chip_at(dz, col_count))


def first_kernel(
    far, col_count, list_ref, live_ref, cov_ref, near_sums, far_theta, far_tiles, in_base, in_d,
    far_base, far_d, out_ref, theta_ref, tiles_ref, base_ref, d_ref, sums_ref, sum_sem, sems,
):
    slots, size, _ = theta_ref.shape
    arrays = [Tiles(far_theta, theta_ref, sems.at[0]), Tiles(far_tiles, tiles_ref, sems.at[1])]
    outs = [Tiles(far_base, base_ref, sems.at[2], True), Tiles(far_d, d_ref, sems.at[3], True)]
    bring = pltpu.make_async_copy(near_sums, sums_ref, sum_sem.at[0])
    bring.start()
    for dz in far:
        for array in arrays:
            array.start(chip_at(dz, col_count))
    bring.wait()
    for begin in range(0, len(far), 2):
        part = range(begin, min(begin + 2, len(far)))
        chips = [chip_at(far[n], col_count) for n in part]
        for chip in chips:
            for array in arrays:
                array.wait(chip)
        first_steps(
            [chip * CHUNK + s for chip in chips for s in range(CHUNK)],
            [
                cov_ref[:, n * CHUNK + s].reshape(size, size)
                for n in part for s in range(CHUNK)
            ],
            list_ref, live_ref, theta_ref, tiles_ref, base_ref, d_ref, sums_ref,
        )
        for chip in chips:
            for out in outs:
                out.start(chip)
    write_sums(sums_ref, out_ref)
    for dz in far:
        for out in outs:
            out.wait(chip_at(dz, col_count))


def diagonal_kernel(steps, list_ref, far_base, far_d, col_diag_ref, *rest):
    far_diag = rest[:-7]
    far_out, base_ref, d_ref, diag_ref, out_ref, diag_sem, sems = rest[-7:]
    slots, size, _ = d_ref.shape
    chunks = slots // CHUNK
    c = lax.axis_index("col")
    per_source = slots // len(far_diag)
    arrays = [Tiles(far_base, base_ref, sems.at[0]), Tiles(far_d, d_ref, sems.at[1])]
    out = Tiles(far_out, out_ref, sems.at[2], True)

    def diag_copy(n):
        block = far_diag[n]
        place = holder(c, *steps[n], len(far_diag)) * per_source
        return pltpu.make_async_copy(
            block.at[:, pl.ds(block.shape[1] - size, size)],
            diag_ref.at[pl.ds(place, per_source)],
            diag_sem.at[n],
        )

    for n in range(len(far_diag)):
        diag_copy(n).start()
    start_all(arrays, chunks)
    for n in range(len(far_diag)):
        diag_copy(n).wait()

    def slot_step(slot):
        d = d_ref[slot]
        half = dot(diag_ref[slot], jnp.concatenate(split(d), axis=1))
        half = half[:, :size] + half[:, size:]
        right = col_diag_ref[list_ref[slot]]
        both = dot(
            jnp.concatenate(split(half), axis=1), jnp.concatenate([right, right], axis=0)
        )
        out_ref[slot] = base_ref[slot] + d - STEP * both

    each_slot(chunks, arrays, [out], slot_step)


def sum_kernel(same_ref, in_ref, out_ref):
    same = same_ref[...].astype(BF)
    for g in range(in_ref.shape[1]):
        x = in_ref[:, g, :]
        x1, rest = x.astype(BF), x
        rest = rest - x1.astype(F32)
        x2 = rest.astype(BF)
        rest = rest - x2.astype(F32)
        x3 = rest.astype(BF)
        out_ref[:, g, :] = dot(
            jnp.concatenate([same, same, same], axis=1), jnp.concatenate([x1, x2, x3], axis=0)
        )


def sweep_kernel(
    last, list_ref, live_ref, far_t, far_theta, far_pairs, q_ref, far_d, *rest
):
    if last:
        t_ref, theta_ref, pairs_ref, d_ref, right_ref, sems = rest
    else:
        out_ref, t_ref, theta_ref, pairs_ref, d_ref, right_ref, sems, sums_ref = rest
    slots, size, _ = theta_ref.shape
    chunks = slots // MANY
    arrays = [
        Tiles(far_pairs, pairs_ref, sems.at[0], count=MANY),
        Tiles(far_t, t_ref, sems.at[1], count=MANY),
        Tiles(far_theta, theta_ref, sems.at[2], count=MANY),
    ]
    out = Tiles(far_d, d_ref, sems.at[3], True, count=MANY)
    start_all(arrays, chunks)
    for a in range(q_ref.shape[1]):
        q = q_ref[:, a].reshape(size, size)
        right_ref[a] = pair(jnp.concatenate(split(q), axis=1))
    if not last:
        sums_ref[...] = jnp.zeros_like(sums_ref)

    def step(i, carry):
        for array in arrays:
            array.wait(i)
        slots_here = [i * MANY + s for s in range(MANY)]
        both = [dot(pairs_ref[slot], right_ref[list_ref[slot]]) for slot in slots_here]
        ds = []
        for slot, x in zip(slots_here, both):
            product = x[:, :size] + x[:, size:]
            d = shrink(t_ref[slot] - STEP * product) - theta_ref[slot]
            ds.append(jnp.where(slot < live_ref[0], d, 0.0))
        for slot, d in zip(slots_here, ds):
            d_ref[slot] = d
        if not last:
            tiles = [pairs_ref[slot] for slot in slots_here]
            add_products(slots_here, ds, tiles, list_ref, sums_ref)
        out.start(i)
        return carry

    lax.fori_loop(0, chunks, step, 0)
    if not last:
        write_sums(sums_ref, out_ref)
    for i in range(chunks):
        out.wait(i)


def shape(dims, dtype):
    return jax.ShapeDtypeStruct(dims, dtype)


def far(x):
    return pltpu.with_memory_space_constraint(x, pltpu.HBM)


def slot_blocks(*dims):
    return pl.BlockSpec((PER_STEP,) + dims, lambda i: (i,) + (0,) * len(dims))


def body(
    features,
    diag_inverse,
    precision_tiles,
    inverse_tiles,
    slot_rows,
    slot_columns,
    owned_columns,
    live_counts,
):
    row_count = lax.axis_size("row")
    col_count = lax.axis_size("col")
    r = lax.axis_index("row")
    c = lax.axis_index("col")
    blocks, samples, size = features.shape
    slots = precision_tiles.shape[2]
    columns = owned_columns.shape[2]
    per_source = slots // col_count
    group = size // row_count
    theta = precision_tiles[0, 0]
    tiles = inverse_tiles[0, 0]
    tile_shape = (slots, size, size)
    piece_shape = (row_count, columns, group, size)

    with jax.named_scope("slices"):
        mine = pl.pallas_call(
            functools.partial(slice_kernel, group),
            in_specs=[HBM],
            out_specs=VMEM,
            out_shape=shape((blocks, group, samples), BF),
            scratch_shapes=[
                pltpu.VMEM(features.shape, BF), pltpu.SemaphoreType.DMA((4,))
            ],
            compiler_params=PARAMS,
        )(far(features))
        slices = lax.all_gather(mine, "col", axis=0, tiled=True)

    with jax.named_scope("tables"):
        rows_here = lax.dynamic_index_in_dim(slot_rows, c, 1, keepdims=False)
        lists_here = lax.dynamic_index_in_dim(slot_columns, c, 1, keepdims=False)
        owned_here = lax.dynamic_index_in_dim(owned_columns, c, 1, keepdims=False) - c * blocks
        my_list = lax.dynamic_index_in_dim(lists_here, r, 0, keepdims=False)
        live = lax.dynamic_slice(live_counts, (r, c), (1, 1)).reshape(1)
        wanted = lax.dynamic_slice(
            slot_rows, (r, 0, c * per_source), (1, col_count, per_source)
        ).reshape(col_count, per_source) - c * blocks
        flat = owned_here.reshape(-1)
        same = (flat[:, None] == flat[None, :]).astype(F32)
        my_owned = lax.dynamic_index_in_dim(owned_here, r, 0, keepdims=False)
        col_diag = jnp.take(diag_inverse, my_owned, axis=0)

    tile_vmem = pltpu.VMEM(tile_shape, F32)
    tile_out = pltpu.HBM(tile_shape, F32)
    sums = pltpu.VMEM((columns, size, 2 * size), F32)
    chunks = slots // CHUNK

    def sems(*dims):
        return pltpu.SemaphoreType.DMA(dims)

    with jax.named_scope("split"):
        pairs = pl.pallas_call(
            split_kernel,
            grid=(slots // PER_STEP,),
            in_specs=[slot_blocks(size, size)],
            out_specs=slot_blocks(size, 2 * size),
            out_shape=pltpu.HBM((slots, size, 2 * size), BF),
        )(far(tiles))

    with jax.named_scope("blocks"):
        chips = col_count // CORES
        near = [0]
        far_chips = list(range(1, chips))
        cores = range(CORES)
        steps = [(dz, dk) for dz in near for dk in cores]
        steps += [(dz, dk) for dz in (1, chips - 1) for dk in cores]
        early = len(steps)
        steps += [(dz, dk) for dz in far_chips[1:-1] for dk in cores]
        near_count = len(near) * CORES
        block_shapes = [
            (per_source, samples + size if n < near_count else size, size)
            for n in range(len(steps))
        ]
        mine, wanted = lax.optimization_barrier((mine, wanted))
        blocks_out = list(pl.pallas_call(
            functools.partial(gather_kernel, steps),
            in_specs=[SMEM, HBM, HBM],
            out_specs=[HBM] * len(steps),
            out_shape=[pltpu.HBM(dims, BF) for dims in block_shapes],
            scratch_shapes=[
                pltpu.VMEM((near_count,) + block_shapes[0], BF),
                pltpu.VMEM((len(steps) - near_count,) + block_shapes[-1], BF),
                sems(len(steps), per_source, 2),
                sems(len(steps)),
            ],
            compiler_params=PARAMS,
        )(wanted, far(features), far(diag_inverse)))

        def send(n):
            dz, dk = steps[n]
            if dz == 0 and dk == 0:
                return blocks_out[n]
            pairs_of = [
                (h, (h // CORES - dz) % chips * CORES + (h + dk) % CORES)
                for h in range(col_count)
            ]
            return lax.ppermute(blocks_out[n], "col", pairs_of)

        got_blocks = [send(n) for n in range(early)]
        base, d, near_sums = pl.pallas_call(
            functools.partial(near_kernel, near, col_count),
            in_specs=[SMEM, SMEM, SMEM] + [HBM] * (3 + near_count),
            out_specs=[HBM] * 2 + [VMEM],
            out_shape=[tile_out, tile_out, pltpu.HBM((columns, size, 2 * size), F32)],
            scratch_shapes=[
                pltpu.VMEM((len(near) * CHUNK, samples, size), BF),
                pltpu.VMEM((columns, samples, size), BF),
                tile_vmem, tile_vmem, tile_vmem, tile_vmem,
                sems(near_count), sems(columns), sems(4, chunks),
            ],
            compiler_params=PARAMS,
        )(
            my_list, live, my_owned, far(features), far(theta), far(tiles),
            *[far(block) for block in got_blocks[:near_count]],
        )
        slices, pairs, got_blocks, base, d, near_sums = lax.optimization_barrier(
            (slices, pairs, got_blocks, base, d, near_sums)
        )

    far_slots = len(far_chips) * CHUNK
    with jax.named_scope("covariance"):
        partial = pl.pallas_call(
            functools.partial(covariance_kernel, far_chips, col_count),
            in_specs=[SMEM, SMEM, SMEM, HBM, HBM],
            out_specs=HBM,
            out_shape=pltpu.HBM((row_count, far_slots, group, size), F32),
            scratch_shapes=[
                pltpu.VMEM(slices.shape, BF),
                pltpu.VMEM((row_count, columns, samples, size), BF),
                pltpu.VMEM((row_count, far_slots, group, size), F32),
                sems(len(far_chips)),
                sems(row_count, columns),
                sems(row_count),
            ],
            compiler_params=PARAMS,
        )(rows_here, lists_here, owned_here, far(slices), far(features))
        covariance = lax.all_to_all(partial, "row", split_axis=0, concat_axis=0, tiled=True)

    with jax.named_scope("diag"):
        blocks_out[early:], _ = lax.optimization_barrier((blocks_out[early:], partial[0, 0]))
        got_blocks = got_blocks + [send(n) for n in range(early, len(steps))]
        covariance, got_blocks = lax.optimization_barrier((covariance, got_blocks))

    with jax.named_scope("first"):
        base, d, pieces = pl.pallas_call(
            functools.partial(first_kernel, far_chips, col_count),
            in_specs=[SMEM, SMEM, VMEM] + [HBM] * 5,
            out_specs=[HBM, HBM, VMEM],
            out_shape=[tile_out, tile_out, shape(piece_shape, F32)],
            scratch_shapes=[
                tile_vmem, tile_vmem, tile_vmem, tile_vmem, sums, sems(1), sems(4, chunks),
            ],
            input_output_aliases={6: 0, 7: 1},
            compiler_params=PARAMS,
        )(
            my_list, live, covariance, far(near_sums), far(theta), far(tiles), far(base), far(d)
        )

    for sweep in range(1, SWEEPS):
        last = sweep == SWEEPS - 1
        with jax.named_scope("exchange"):
            got = lax.all_to_all(pieces, "row", split_axis=0, concat_axis=0, tiled=True)
            flat_shape = (row_count * columns, group, size)
            summed = pl.pallas_call(
                sum_kernel,
                in_specs=[VMEM, VMEM],
                out_specs=VMEM,
                out_shape=shape(flat_shape, F32),
                compiler_params=PARAMS,
            )(same, got.reshape(flat_shape))
            q = lax.all_to_all(
                summed.reshape(piece_shape), "row", split_axis=0, concat_axis=0, tiled=True
            )
        with jax.named_scope("diagonal"):
            t = pl.pallas_call(
                functools.partial(diagonal_kernel, steps),
                in_specs=[SMEM, HBM, HBM, VMEM] + [HBM] * col_count,
                out_specs=HBM,
                out_shape=tile_out,
                scratch_shapes=[
                    tile_vmem, tile_vmem, pltpu.VMEM(tile_shape, BF), tile_vmem,
                    sems(col_count), sems(3, chunks),
                ],
                compiler_params=PARAMS,
            )(my_list, far(base), far(d), col_diag, *[far(block) for block in got_blocks])
        with jax.named_scope("sweep"):
            result = pl.pallas_call(
                functools.partial(sweep_kernel, last),
                in_specs=[SMEM, SMEM, HBM, HBM, HBM, VMEM],
                out_specs=[HBM] if last else [HBM, VMEM],
                out_shape=[tile_out] if last else [tile_out, shape(piece_shape, F32)],
                scratch_shapes=[
                    tile_vmem, tile_vmem, pltpu.VMEM((slots, size, 2 * size), BF), tile_vmem,
                    pltpu.VMEM((columns, 2 * size, 2 * size), BF), sems(4, slots // MANY),
                ] + ([] if last else [sums]),
                compiler_params=PARAMS,
            )(my_list, live, far(t), far(theta), far(pairs), q)
            d = result[0]
            if not last:
                pieces = result[1]
    return d.reshape(precision_tiles.shape)


def solution(mesh):
    return jax.shard_map(
        body,
        mesh=mesh,
        in_specs=(
            P("col", None, None),
            P("col", None, None),
            P("row", "col", None, None, None),
            P("row", "col", None, None, None),
            P(),
            P(),
            P(),
            P(),
        ),
        out_specs=P("row", "col", None, None, None),
        check_vma=False,
    )
```

```python
import functools

import jax
import jax.numpy as jnp
from jax import lax
from jax.experimental import pallas as pl
from jax.experimental.pallas import tpu as pltpu
from jax.sharding import PartitionSpec as P

SWEEPS = 4
STEP = 0.3
LAMBDA = 0.3 * 0.6
PER_STEP = 8
CHUNK = 4
CORES = 2
MANY = 8

BF = jnp.bfloat16
F32 = jnp.float32
VMEM = pl.BlockSpec(memory_space=pltpu.VMEM)
HBM = pl.BlockSpec(memory_space=pltpu.HBM)
SMEM = pl.BlockSpec(memory_space=pltpu.SMEM)
PARAMS = pltpu.CompilerParams(vmem_limit_bytes=20 * 1024 * 1024)


def split(x):
    high = x.astype(BF)
    low = (x - high.astype(F32)).astype(BF)
    return high, low


def dot(a, b):
    return jnp.dot(a, b, preferred_element_type=F32)


def shrink(x):
    return x - jnp.clip(x, -LAMBDA, LAMBDA)


def slice_kernel(group, features, out_ref, near_ref, sems):
    r = lax.axis_index("row")
    blocks, _, variables = features.shape
    parts = sems.shape[0]
    count = blocks // parts

    def copy(i):
        part = pl.ds(i * count, count)
        return pltpu.make_async_copy(features.at[part], near_ref.at[part], sems.at[i])

    for i in range(parts):
        copy(i).start()
    wanted = lax.broadcasted_iota(jnp.int32, (group, variables), 0) + r * group
    pick = (lax.broadcasted_iota(jnp.int32, (group, variables), 1) == wanted).astype(BF)

    def step(i, carry):
        copy(i).wait()
        for b in range(count):
            rows = lax.dot_general(
                pick, near_ref[i * count + b], (((1,), (1,)), ((), ())),
                preferred_element_type=F32,
            )
            out_ref[i * count + b] = rows.astype(BF)
        return carry

    lax.fori_loop(0, parts, step, 0)


def split_kernel(tiles_ref, out_ref):
    for s in range(tiles_ref.shape[0]):
        out_ref[s] = jnp.concatenate(split(tiles_ref[s]), axis=1)


def gather_kernel(steps, wanted_ref, features, diag, *rest):
    outs, (near_ref, far_ref, sems, out_sems) = rest[:-4], rest[-4:]
    c = lax.axis_index("col")
    samples = features.shape[1]
    size = diag.shape[1]
    near_count = near_ref.shape[0]
    copies = []
    backs = []
    for n, ((dz, dk), out) in enumerate(zip(steps, outs)):
        target = holder(c, -dz, dk, wanted_ref.shape[0])
        place = near_ref.at[n] if n < near_count else far_ref.at[n - near_count]
        begin = samples if n < near_count else 0
        mine = []
        for p in range(out.shape[0]):
            block = wanted_ref[target, p]
            if n < near_count:
                mine.append(pltpu.make_async_copy(
                    features.at[block], place.at[p, pl.ds(0, samples)], sems.at[n, p, 0]
                ))
            mine.append(pltpu.make_async_copy(
                diag.at[block], place.at[p, pl.ds(begin, size)], sems.at[n, p, 1]
            ))
        for copy in mine:
            copy.start()
        copies.append(mine)
        backs.append(pltpu.make_async_copy(place, out, out_sems.at[n]))
    for mine, back in zip(copies, backs):
        for copy in mine:
            copy.wait()
        back.start()
    for back in backs:
        back.wait()


def holder(c, dz, dk, col_count):
    chips = col_count // CORES
    z = lax.rem(c // CORES + dz + chips, chips)
    return z * CORES + lax.rem(c + dk, CORES)


def chip_at(dz, col_count):
    return lax.rem(lax.axis_index("col") // CORES + dz, col_count // CORES)


class Tiles:
    def __init__(self, far_ref, near_ref, sem, back=False, count=CHUNK):
        self.refs = (near_ref, far_ref) if back else (far_ref, near_ref)
        self.sem = sem
        self.count = count

    def copy(self, i):
        part = pl.ds(i * self.count, self.count)
        source, target = (ref.at[part] for ref in self.refs)
        return pltpu.make_async_copy(source, target, self.sem.at[i])

    def start(self, i):
        self.copy(i).start()

    def wait(self, i):
        self.copy(i).wait()


def start_all(arrays, chunks):
    for i in range(chunks):
        for array in arrays:
            array.start(i)


def each_slot(chunks, arrays, outs, slot_step):
    def step(i, carry):
        for array in arrays:
            array.wait(i)
        for s in range(CHUNK):
            slot_step(i * CHUNK + s)
        for out in outs:
            out.start(i)
        return carry

    lax.fori_loop(0, chunks, step, 0)
    for i in range(chunks):
        for out in outs:
            out.wait(i)


def covariance_kernel(
    far, col_count, rows_ref, lists_ref, owned_ref, far_slices, features, far_out,
    slices_ref, right_ref, out_ref, slice_sem, right_sem, out_sem,
):
    owners = rows_ref.shape[0]
    columns = owned_ref.shape[1]
    group = slices_ref.shape[1]
    _, samples, size = features.shape
    part = far_slices.shape[0] * CORES // col_count
    slots = [chip_at(dz, col_count) * CHUNK + s for dz in far for s in range(CHUNK)]

    def slice_copy(n):
        here = pl.ds(chip_at(far[n], col_count) * part, part)
        return pltpu.make_async_copy(
            far_slices.at[here], slices_ref.at[here], slice_sem.at[n]
        )

    def right_copy(owner, a):
        return pltpu.make_async_copy(
            features.at[owned_ref[owner, a]], right_ref.at[owner, a], right_sem.at[owner, a]
        )

    def out_copy(owner):
        return pltpu.make_async_copy(out_ref.at[owner], far_out.at[owner], out_sem.at[owner])

    for n in range(len(far)):
        slice_copy(n).start()
    for owner in range(owners):
        for a in range(columns):
            right_copy(owner, a).start()
    for n in range(len(far)):
        slice_copy(n).wait()

    def owner_step(owner, carry):
        for a in range(columns):
            right_copy(owner, a).wait()
        left = jnp.concatenate(
            [slices_ref[rows_ref[owner, slot]].astype(F32) for slot in slots], axis=0
        ).astype(BF)
        right = jnp.concatenate([right_ref[owner, a] for a in range(columns)], axis=1)
        both = dot(left, right) * (1.0 / samples)
        for k, slot in enumerate(slots):
            rows = both[k * group:(k + 1) * group]
            out_ref[owner, k] = jnp.where(
                lists_ref[owner, slot] == 0, rows[:, :size], rows[:, size:]
            )
        out_copy(owner).start()
        return carry

    lax.fori_loop(0, owners, owner_step, 0, unroll=2)
    for owner in range(owners):
        out_copy(owner).wait()


def pair(x):
    size = x.shape[0]
    high = x[:, :size]
    return jnp.concatenate(
        [x, jnp.concatenate([high, jnp.zeros_like(high)], axis=1)], axis=0
    )


def add_products(slots, ds, tiles, list_ref, sums_ref):
    lefts = [jnp.concatenate(split(d.T), axis=1) for d in ds]
    products = [dot(left, pair(tile)) for left, tile in zip(lefts, tiles)]
    for slot, product in zip(slots, products):
        sums_ref[list_ref[slot]] += product


def write_sums(sums_ref, out_ref):
    pieces, columns, group, size = out_ref.shape
    for a in range(columns):
        total = sums_ref[a][:, :size] + sums_ref[a][:, size:]
        out_ref[:, a] = total.reshape(pieces, group, size)


def first_steps(
    slots, covariances, list_ref, live_ref, theta_ref, tiles_ref, base_ref, d_ref, sums_ref
):
    ds = []
    tiles = []
    for slot, covariance in zip(slots, covariances):
        theta = theta_ref[slot]
        tile = tiles_ref[slot]
        base = theta - STEP * (covariance - tile)
        base_ref[slot] = base
        ds.append(jnp.where(slot < live_ref[0], shrink(base) - theta, 0.0))
        tiles.append(jnp.concatenate(split(tile), axis=1))
    for slot, d in zip(slots, ds):
        d_ref[slot] = d
    add_products(slots, ds, tiles, list_ref, sums_ref)


def near_kernel(near, col_count, list_ref, live_ref, owned_ref, features, far_theta, far_tiles, *rest):
    count = len(near) * CORES
    blocks = rest[:count]
    (
        far_base, far_d, sums_ref, left_ref, right_ref, theta_ref, tiles_ref, base_ref, d_ref,
        left_sem, right_sem, sems,
    ) = rest[count:]
    slots, size, _ = theta_ref.shape
    samples = features.shape[1]
    per_source = CHUNK // CORES
    core = lax.rem(lax.axis_index("col"), CORES)
    arrays = [Tiles(far_theta, theta_ref, sems.at[0]), Tiles(far_tiles, tiles_ref, sems.at[1])]
    outs = [Tiles(far_base, base_ref, sems.at[2], True), Tiles(far_d, d_ref, sems.at[3], True)]

    def left_copy(n):
        place = n // CORES * CHUNK + lax.rem(core + n % CORES, CORES) * per_source
        return pltpu.make_async_copy(
            blocks[n].at[:, pl.ds(0, samples)], left_ref.at[pl.ds(place, per_source)],
            left_sem.at[n],
        )

    def right_copy(a):
        return pltpu.make_async_copy(
            features.at[owned_ref[a]], right_ref.at[a], right_sem.at[a]
        )

    for a in range(right_ref.shape[0]):
        right_copy(a).start()
    for n in range(count):
        left_copy(n).start()
    for dz in near:
        for array in arrays:
            array.start(chip_at(dz, col_count))
    sums_ref[...] = jnp.zeros_like(sums_ref)
    for a in range(right_ref.shape[0]):
        right_copy(a).wait()
    for n in range(count):
        left_copy(n).wait()
    for n, dz in enumerate(near):
        chip = chip_at(dz, col_count)
        for array in arrays:
            array.wait(chip)
        slots_here = [chip * CHUNK + s for s in range(CHUNK)]
        covariances = [
            lax.dot_general(
                left_ref[n * CHUNK + s], right_ref[list_ref[slot]],
                (((0,), (0,)), ((), ())), preferred_element_type=F32,
            ) * (1.0 / samples)
            for s, slot in enumerate(slots_here)
        ]
        first_steps(
            slots_here, covariances, list_ref, live_ref, theta_ref, tiles_ref, base_ref, d_ref,
            sums_ref,
        )
        for out in outs:
            out.start(chip)
    for dz in near:
        for out in outs:
            out.wait(chip_at(dz, col_count))


def first_kernel(
    far, col_count, list_ref, live_ref, cov_ref, near_sums, far_theta, far_tiles, in_base, in_d,
    far_base, far_d, out_ref, theta_ref, tiles_ref, base_ref, d_ref, sums_ref, sum_sem, sems,
):
    slots, size, _ = theta_ref.shape
    arrays = [Tiles(far_theta, theta_ref, sems.at[0]), Tiles(far_tiles, tiles_ref, sems.at[1])]
    outs = [Tiles(far_base, base_ref, sems.at[2], True), Tiles(far_d, d_ref, sems.at[3], True)]
    bring = pltpu.make_async_copy(near_sums, sums_ref, sum_sem.at[0])
    bring.start()
    for dz in far:
        for array in arrays:
            array.start(chip_at(dz, col_count))
    bring.wait()
    for begin in range(0, len(far), 2):
        part = range(begin, min(begin + 2, len(far)))
        chips = [chip_at(far[n], col_count) for n in part]
        for chip in chips:
            for array in arrays:
                array.wait(chip)
        first_steps(
            [chip * CHUNK + s for chip in chips for s in range(CHUNK)],
            [
                cov_ref[:, n * CHUNK + s].reshape(size, size)
                for n in part for s in range(CHUNK)
            ],
            list_ref, live_ref, theta_ref, tiles_ref, base_ref, d_ref, sums_ref,
        )
        for chip in chips:
            for out in outs:
                out.start(chip)
    write_sums(sums_ref, out_ref)
    for dz in far:
        for out in outs:
            out.wait(chip_at(dz, col_count))


def diagonal_kernel(steps, half, list_ref, far_base, far_d, col_diag_ref, *rest):
    far_diag = rest[:len(steps)]
    far_out, base_ref, d_ref, diag_ref, out_ref, diag_sem, sems = rest[-7:]
    slots, size, _ = d_ref.shape
    chunks = slots // MANY
    mine = range(half * chunks // 2, (half + 1) * chunks // 2)
    c = lax.axis_index("col")
    per_source = slots // len(far_diag)
    arrays = [
        Tiles(far_d, d_ref, sems.at[1], count=MANY),
        Tiles(far_base, base_ref, sems.at[0], count=MANY),
    ]
    out = Tiles(far_out, out_ref, sems.at[2], True, count=MANY)

    def with_diag(n, use):
        block = far_diag[n]
        place = holder(c, *steps[n], len(far_diag)) * per_source

        @pl.when(place // (slots // 2) == half)
        def _():
            use(pltpu.make_async_copy(
                block.at[:, pl.ds(block.shape[1] - size, size)],
                diag_ref.at[pl.ds(place, per_source)],
                diag_sem.at[n],
            ))

    for n in range(len(far_diag)):
        with_diag(n, lambda copy: copy.start())
    for i in mine:
        for array in arrays:
            array.start(i)
    for n in range(len(far_diag)):
        with_diag(n, lambda copy: copy.wait())
    for i in mine:
        for array in arrays:
            array.wait(i)
        slots_here = [i * MANY + s for s in range(MANY)]
        halves = [
            dot(diag_ref[slot], jnp.concatenate(split(d_ref[slot]), axis=1))
            for slot in slots_here
        ]
        for slot, x in zip(slots_here, halves):
            left = jnp.concatenate(split(x[:, :size] + x[:, size:]), axis=1)
            right = col_diag_ref[list_ref[slot]]
            both = dot(left, jnp.concatenate([right, right], axis=0))
            out_ref[slot] = base_ref[slot] + d_ref[slot] - STEP * both
        out.start(i)
    for i in mine:
        out.wait(i)


def sum_kernel(same_ref, in_ref, out_ref):
    same = same_ref[...].astype(BF)
    for g in range(in_ref.shape[1]):
        x = in_ref[:, g, :]
        x1, rest = x.astype(BF), x
        rest = rest - x1.astype(F32)
        x2 = rest.astype(BF)
        rest = rest - x2.astype(F32)
        x3 = rest.astype(BF)
        out_ref[:, g, :] = dot(
            jnp.concatenate([same, same, same], axis=1), jnp.concatenate([x1, x2, x3], axis=0)
        )


def sweep_kernel(
    last, list_ref, live_ref, far_t, far_theta, far_pairs, q_ref, far_d, *rest
):
    if last:
        t_ref, theta_ref, pairs_ref, d_ref, right_ref, sems = rest
    else:
        out_ref, t_ref, theta_ref, pairs_ref, d_ref, right_ref, sems, sums_ref = rest
    slots, size, _ = theta_ref.shape
    chunks = slots // MANY
    arrays = [
        Tiles(far_pairs, pairs_ref, sems.at[0], count=MANY),
        Tiles(far_t, t_ref, sems.at[1], count=MANY),
        Tiles(far_theta, theta_ref, sems.at[2], count=MANY),
    ]
    out = Tiles(far_d, d_ref, sems.at[3], True, count=MANY)
    start_all(arrays, chunks)
    for a in range(q_ref.shape[1]):
        q = q_ref[:, a].reshape(size, size)
        right_ref[a] = pair(jnp.concatenate(split(q), axis=1))
    if not last:
        sums_ref[...] = jnp.zeros_like(sums_ref)

    def step(i, carry):
        for array in arrays:
            array.wait(i)
        slots_here = [i * MANY + s for s in range(MANY)]
        both = [dot(pairs_ref[slot], right_ref[list_ref[slot]]) for slot in slots_here]
        ds = []
        for slot, x in zip(slots_here, both):
            product = x[:, :size] + x[:, size:]
            d = shrink(t_ref[slot] - STEP * product) - theta_ref[slot]
            ds.append(jnp.where(slot < live_ref[0], d, 0.0))
        for slot, d in zip(slots_here, ds):
            d_ref[slot] = d
        if not last:
            tiles = [pairs_ref[slot] for slot in slots_here]
            add_products(slots_here, ds, tiles, list_ref, sums_ref)
        out.start(i)
        return carry

    lax.fori_loop(0, chunks, step, 0)
    if not last:
        write_sums(sums_ref, out_ref)
    for i in range(chunks):
        out.wait(i)


def shape(dims, dtype):
    return jax.ShapeDtypeStruct(dims, dtype)


def far(x):
    return pltpu.with_memory_space_constraint(x, pltpu.HBM)


def slot_blocks(*dims):
    return pl.BlockSpec((PER_STEP,) + dims, lambda i: (i,) + (0,) * len(dims))


def body(
    features,
    diag_inverse,
    precision_tiles,
    inverse_tiles,
    slot_rows,
    slot_columns,
    owned_columns,
    live_counts,
):
    row_count = lax.axis_size("row")
    col_count = lax.axis_size("col")
    r = lax.axis_index("row")
    c = lax.axis_index("col")
    blocks, samples, size = features.shape
    slots = precision_tiles.shape[2]
    columns = owned_columns.shape[2]
    per_source = slots // col_count
    group = size // row_count
    theta = precision_tiles[0, 0]
    tiles = inverse_tiles[0, 0]
    tile_shape = (slots, size, size)
    piece_shape = (row_count, columns, group, size)

    with jax.named_scope("slices"):
        mine = pl.pallas_call(
            functools.partial(slice_kernel, group),
            in_specs=[HBM],
            out_specs=VMEM,
            out_shape=shape((blocks, group, samples), BF),
            scratch_shapes=[
                pltpu.VMEM(features.shape, BF), pltpu.SemaphoreType.DMA((4,))
            ],
            compiler_params=PARAMS,
        )(far(features))
        slices = lax.all_gather(mine, "col", axis=0, tiled=True)

    with jax.named_scope("tables"):
        rows_here = lax.dynamic_index_in_dim(slot_rows, c, 1, keepdims=False)
        lists_here = lax.dynamic_index_in_dim(slot_columns, c, 1, keepdims=False)
        owned_here = lax.dynamic_index_in_dim(owned_columns, c, 1, keepdims=False) - c * blocks
        my_list = lax.dynamic_index_in_dim(lists_here, r, 0, keepdims=False)
        live = lax.dynamic_slice(live_counts, (r, c), (1, 1)).reshape(1)
        wanted = lax.dynamic_slice(
            slot_rows, (r, 0, c * per_source), (1, col_count, per_source)
        ).reshape(col_count, per_source) - c * blocks
        flat = owned_here.reshape(-1)
        same = (flat[:, None] == flat[None, :]).astype(F32)
        my_owned = lax.dynamic_index_in_dim(owned_here, r, 0, keepdims=False)
        col_diag = jnp.take(diag_inverse, my_owned, axis=0)

    tile_vmem = pltpu.VMEM(tile_shape, F32)
    tile_out = pltpu.HBM(tile_shape, F32)
    sums = pltpu.VMEM((columns, size, 2 * size), F32)
    chunks = slots // CHUNK

    def sems(*dims):
        return pltpu.SemaphoreType.DMA(dims)

    with jax.named_scope("split"):
        pairs = pl.pallas_call(
            split_kernel,
            grid=(slots // PER_STEP,),
            in_specs=[slot_blocks(size, size)],
            out_specs=slot_blocks(size, 2 * size),
            out_shape=pltpu.HBM((slots, size, 2 * size), BF),
        )(far(tiles))

    with jax.named_scope("blocks"):
        chips = col_count // CORES
        near = [0]
        far_chips = list(range(1, chips))
        cores = range(CORES)
        steps = [(dz, dk) for dz in near for dk in cores]
        steps += [(dz, dk) for dz in (1, chips - 1, 2, chips - 2) for dk in cores]
        early = len(steps)
        steps += [(dz, dk) for dz in far_chips[2:-2] for dk in cores]
        near_count = len(near) * CORES
        block_shapes = [
            (per_source, samples + size if n < near_count else size, size)
            for n in range(len(steps))
        ]
        mine, wanted = lax.optimization_barrier((mine, wanted))
        blocks_out = list(pl.pallas_call(
            functools.partial(gather_kernel, steps),
            in_specs=[SMEM, HBM, HBM],
            out_specs=[HBM] * len(steps),
            out_shape=[pltpu.HBM(dims, BF) for dims in block_shapes],
            scratch_shapes=[
                pltpu.VMEM((near_count,) + block_shapes[0], BF),
                pltpu.VMEM((len(steps) - near_count,) + block_shapes[-1], BF),
                sems(len(steps), per_source, 2),
                sems(len(steps)),
            ],
            compiler_params=PARAMS,
        )(wanted, far(features), far(diag_inverse)))

        def send(n):
            dz, dk = steps[n]
            if dz == 0 and dk == 0:
                return blocks_out[n]
            pairs_of = [
                (h, (h // CORES - dz) % chips * CORES + (h + dk) % CORES)
                for h in range(col_count)
            ]
            return lax.ppermute(blocks_out[n], "col", pairs_of)

        got_blocks = [send(n) for n in range(early)]
        base, d, near_sums = pl.pallas_call(
            functools.partial(near_kernel, near, col_count),
            in_specs=[SMEM, SMEM, SMEM] + [HBM] * (3 + near_count),
            out_specs=[HBM] * 2 + [VMEM],
            out_shape=[tile_out, tile_out, pltpu.HBM((columns, size, 2 * size), F32)],
            scratch_shapes=[
                pltpu.VMEM((len(near) * CHUNK, samples, size), BF),
                pltpu.VMEM((columns, samples, size), BF),
                tile_vmem, tile_vmem, tile_vmem, tile_vmem,
                sems(near_count), sems(columns), sems(4, chunks),
            ],
            compiler_params=PARAMS,
        )(
            my_list, live, my_owned, far(features), far(theta), far(tiles),
            *[far(block) for block in got_blocks[:near_count]],
        )
        slices, pairs, got_blocks, base, d, near_sums = lax.optimization_barrier(
            (slices, pairs, got_blocks, base, d, near_sums)
        )

    far_slots = len(far_chips) * CHUNK
    with jax.named_scope("covariance"):
        partial = pl.pallas_call(
            functools.partial(covariance_kernel, far_chips, col_count),
            in_specs=[SMEM, SMEM, SMEM, HBM, HBM],
            out_specs=HBM,
            out_shape=pltpu.HBM((row_count, far_slots, group, size), F32),
            scratch_shapes=[
                pltpu.VMEM(slices.shape, BF),
                pltpu.VMEM((row_count, columns, samples, size), BF),
                pltpu.VMEM((row_count, far_slots, group, size), F32),
                sems(len(far_chips)),
                sems(row_count, columns),
                sems(row_count),
            ],
            compiler_params=PARAMS,
        )(rows_here, lists_here, owned_here, far(slices), far(features))
        covariance = lax.all_to_all(partial, "row", split_axis=0, concat_axis=0, tiled=True)

    with jax.named_scope("diag"):
        blocks_out[early:], _ = lax.optimization_barrier((blocks_out[early:], partial[0, 0]))
        got_blocks = got_blocks + [send(n) for n in range(early, len(steps))]
        covariance, got_blocks = lax.optimization_barrier((covariance, got_blocks))

    with jax.named_scope("first"):
        base, d, pieces = pl.pallas_call(
            functools.partial(first_kernel, far_chips, col_count),
            in_specs=[SMEM, SMEM, VMEM] + [HBM] * 5,
            out_specs=[HBM, HBM, VMEM],
            out_shape=[tile_out, tile_out, shape(piece_shape, F32)],
            scratch_shapes=[
                tile_vmem, tile_vmem, tile_vmem, tile_vmem, sums, sems(1), sems(4, chunks),
            ],
            input_output_aliases={6: 0, 7: 1},
            compiler_params=PARAMS,
        )(
            my_list, live, covariance, far(near_sums), far(theta), far(tiles), far(base), far(d)
        )

    def diagonal(half, base, d, col_diag, before=()):
        operands = [my_list, far(base), far(d), col_diag]
        operands += [far(block) for block in got_blocks] + [far(x) for x in before]
        with jax.named_scope("diagonal"):
            return pl.pallas_call(
                functools.partial(diagonal_kernel, steps, half),
                in_specs=[SMEM, HBM, HBM, VMEM] + [HBM] * (len(operands) - 4),
                out_specs=HBM,
                out_shape=tile_out,
                scratch_shapes=[
                    tile_vmem, tile_vmem, pltpu.VMEM(tile_shape, BF), tile_vmem,
                    sems(col_count), sems(3, slots // MANY),
                ],
                input_output_aliases={len(operands) - 1: 0} if before else {},
                compiler_params=PARAMS,
            )(*operands)

    for sweep in range(1, SWEEPS):
        last = sweep == SWEEPS - 1
        with jax.named_scope("exchange"):
            flat_shape = (row_count * columns, group, size)
            got = lax.all_to_all(pieces, "row", split_axis=0, concat_axis=0, tiled=True)
            t = diagonal(0, base, d, col_diag)
            got, t = lax.optimization_barrier((got, t))
            summed = pl.pallas_call(
                sum_kernel,
                in_specs=[VMEM, VMEM],
                out_specs=VMEM,
                out_shape=shape(flat_shape, F32),
                compiler_params=PARAMS,
            )(same, got.reshape(flat_shape))
            q = lax.all_to_all(
                summed.reshape(piece_shape), "row", split_axis=0, concat_axis=0, tiled=True
            )
            d, t, _ = lax.optimization_barrier((d, t, summed[0]))
            t = diagonal(1, base, d, col_diag, (t,))
        with jax.named_scope("sweep"):
            result = pl.pallas_call(
                functools.partial(sweep_kernel, last),
                in_specs=[SMEM, SMEM, HBM, HBM, HBM, VMEM],
                out_specs=[HBM] if last else [HBM, VMEM],
                out_shape=[tile_out] if last else [tile_out, shape(piece_shape, F32)],
                scratch_shapes=[
                    tile_vmem, tile_vmem, pltpu.VMEM((slots, size, 2 * size), BF), tile_vmem,
                    pltpu.VMEM((columns, 2 * size, 2 * size), BF), sems(4, slots // MANY),
                ] + ([] if last else [sums]),
                compiler_params=PARAMS,
            )(my_list, live, far(t), far(theta), far(pairs), q)
            d = result[0]
            if not last:
                pieces = result[1]
    return d.reshape(precision_tiles.shape)


def solution(mesh):
    return jax.shard_map(
        body,
        mesh=mesh,
        in_specs=(
            P("col", None, None),
            P("col", None, None),
            P("row", "col", None, None, None),
            P("row", "col", None, None, None),
            P(),
            P(),
            P(),
            P(),
        ),
        out_specs=P("row", "col", None, None, None),
        check_vma=False,
    )
```

```python
import functools

import jax
import jax.numpy as jnp
from jax import lax
from jax.experimental import pallas as pl
from jax.experimental.pallas import tpu as pltpu
from jax.sharding import PartitionSpec as P

SWEEPS = 4
STEP = 0.3
LAMBDA = 0.3 * 0.6
PER_STEP = 8
CHUNK = 4
CORES = 2
MANY = 8

BF = jnp.bfloat16
F32 = jnp.float32
VMEM = pl.BlockSpec(memory_space=pltpu.VMEM)
HBM = pl.BlockSpec(memory_space=pltpu.HBM)
SMEM = pl.BlockSpec(memory_space=pltpu.SMEM)
PARAMS = pltpu.CompilerParams(vmem_limit_bytes=20 * 1024 * 1024)


def split(x):
    high = x.astype(BF)
    low = (x - high.astype(F32)).astype(BF)
    return high, low


def dot(a, b):
    return jnp.dot(a, b, preferred_element_type=F32)


def shrink(x):
    return x - jnp.clip(x, -LAMBDA, LAMBDA)


def slice_kernel(group, features, out_ref, near_ref, sems):
    r = lax.axis_index("row")
    blocks, _, variables = features.shape
    parts = sems.shape[0]
    count = blocks // parts

    def copy(i):
        part = pl.ds(i * count, count)
        return pltpu.make_async_copy(features.at[part], near_ref.at[part], sems.at[i])

    for i in range(parts):
        copy(i).start()
    wanted = lax.broadcasted_iota(jnp.int32, (group, variables), 0) + r * group
    pick = (lax.broadcasted_iota(jnp.int32, (group, variables), 1) == wanted).astype(BF)

    def step(i, carry):
        copy(i).wait()
        for b in range(count):
            rows = lax.dot_general(
                pick, near_ref[i * count + b], (((1,), (1,)), ((), ())),
                preferred_element_type=F32,
            )
            out_ref[i * count + b] = rows.astype(BF)
        return carry

    lax.fori_loop(0, parts, step, 0)


def split_kernel(tiles_ref, out_ref):
    for s in range(tiles_ref.shape[0]):
        out_ref[s] = jnp.concatenate(split(tiles_ref[s]), axis=1)


def near_gather_kernel(wanted_ref, features, diag, own_out, other_out, swap_out, near_ref, swap_ref, sems, swap_sems, out_sems):
    c = lax.axis_index("col")
    col_count = wanted_ref.shape[0]
    samples = features.shape[1]
    size = diag.shape[1]
    outs = (own_out, other_out)
    first = []
    for dk in range(CORES):
        target = holder(c, 0, dk, col_count)
        for p in range(own_out.shape[0]):
            block = wanted_ref[target, p]
            first.append(pltpu.make_async_copy(
                features.at[block], near_ref.at[dk, p, pl.ds(0, samples)], sems.at[dk, p, 0]
            ))
            first.append(pltpu.make_async_copy(
                diag.at[block], near_ref.at[dk, p, pl.ds(samples, size)], sems.at[dk, p, 1]
            ))
    second = [
        pltpu.make_async_copy(
            diag.at[wanted_ref[holder(c, -(n + 1), 1, col_count), p]],
            swap_ref.at[n, p],
            swap_sems.at[n, p],
        )
        for n in range(swap_ref.shape[0]) for p in range(swap_ref.shape[1])
    ]
    for copy in first + second:
        copy.start()
    backs = [
        pltpu.make_async_copy(near_ref.at[dk], outs[dk], out_sems.at[dk]) for dk in range(CORES)
    ]
    backs.append(pltpu.make_async_copy(swap_ref, swap_out, out_sems.at[CORES]))
    for copy in first:
        copy.wait()
    for back in backs[:-1]:
        back.start()
    for copy in second:
        copy.wait()
    backs[-1].start()
    for back in backs:
        back.wait()


def far_gather_kernel(wanted_ref, diag, swapped, *rest):
    outs, (near_ref, sems, out_sems) = rest[:-3], rest[-3:]
    c = lax.axis_index("col")
    count = swapped.shape[1]
    backs = []
    copies = []
    for n, out in enumerate(outs):
        target = holder(c, -(n + 1), 0, wanted_ref.shape[0])
        mine = [
            pltpu.make_async_copy(
                diag.at[wanted_ref[target, p]], near_ref.at[n, p], sems.at[n, p]
            )
            for p in range(count)
        ]
        mine.append(pltpu.make_async_copy(
            swapped.at[n], near_ref.at[n, pl.ds(count, count)], sems.at[n, count]
        ))
        for copy in mine:
            copy.start()
        copies.append(mine)
        backs.append(pltpu.make_async_copy(near_ref.at[n], out, out_sems.at[n]))
    for mine, back in zip(copies, backs):
        for copy in mine:
            copy.wait()
        back.start()
    for back in backs:
        back.wait()


def holder(c, dz, dk, col_count):
    chips = col_count // CORES
    z = lax.rem(c // CORES + dz + chips, chips)
    return z * CORES + lax.rem(c + dk, CORES)


def chip_at(dz, col_count):
    return lax.rem(lax.axis_index("col") // CORES + dz, col_count // CORES)


class Tiles:
    def __init__(self, far_ref, near_ref, sem, back=False, count=CHUNK):
        self.refs = (near_ref, far_ref) if back else (far_ref, near_ref)
        self.sem = sem
        self.count = count

    def copy(self, i):
        part = pl.ds(i * self.count, self.count)
        source, target = (ref.at[part] for ref in self.refs)
        return pltpu.make_async_copy(source, target, self.sem.at[i])

    def start(self, i):
        self.copy(i).start()

    def wait(self, i):
        self.copy(i).wait()


def start_all(arrays, chunks):
    for i in range(chunks):
        for array in arrays:
            array.start(i)


def each_slot(chunks, arrays, outs, slot_step):
    def step(i, carry):
        for array in arrays:
            array.wait(i)
        for s in range(CHUNK):
            slot_step(i * CHUNK + s)
        for out in outs:
            out.start(i)
        return carry

    lax.fori_loop(0, chunks, step, 0)
    for i in range(chunks):
        for out in outs:
            out.wait(i)


def covariance_kernel(
    far, col_count, rows_ref, lists_ref, owned_ref, far_slices, features, far_out,
    slices_ref, right_ref, out_ref, slice_sem, right_sem, out_sem,
):
    owners = rows_ref.shape[0]
    columns = owned_ref.shape[1]
    group = slices_ref.shape[1]
    _, samples, size = features.shape
    slots = [chip_at(dz, col_count) * CHUNK + s for dz in far for s in range(CHUNK)]

    def halves(source, target, sem):
        count = source.shape[0] // 2
        parts = [pl.ds(i * count, count) for i in range(2)]
        return [
            pltpu.make_async_copy(source.at[part], target.at[part], sem.at[i])
            for i, part in enumerate(parts)
        ]

    def out_copy(owner):
        return pltpu.make_async_copy(out_ref.at[owner], far_out.at[owner], out_sem.at[owner])

    copies = halves(far_slices, slices_ref, slice_sem) + halves(features, right_ref, right_sem)
    for copy in copies:
        copy.start()
    for copy in copies:
        copy.wait()

    def owner_step(owner, carry):
        left = jnp.concatenate(
            [slices_ref[rows_ref[owner, slot]].astype(F32) for slot in slots], axis=0
        ).astype(BF)
        right = jnp.concatenate(
            [right_ref[owned_ref[owner, a]] for a in range(columns)], axis=1
        )
        both = dot(left, right) * (1.0 / samples)
        for k, slot in enumerate(slots):
            rows = both[k * group:(k + 1) * group]
            out_ref[owner, k] = jnp.where(
                lists_ref[owner, slot] == 0, rows[:, :size], rows[:, size:]
            )
        out_copy(owner).start()
        return carry

    lax.fori_loop(0, owners, owner_step, 0, unroll=4)
    for owner in range(owners):
        out_copy(owner).wait()


def pair(x):
    size = x.shape[0]
    high = x[:, :size]
    return jnp.concatenate(
        [x, jnp.concatenate([high, jnp.zeros_like(high)], axis=1)], axis=0
    )


def add_products(slots, ds, tiles, list_ref, sums_ref):
    lefts = [jnp.concatenate(split(d.T), axis=1) for d in ds]
    products = [dot(left, pair(tile)) for left, tile in zip(lefts, tiles)]
    for slot, product in zip(slots, products):
        sums_ref[list_ref[slot]] += product


def write_sums(sums_ref, out_ref):
    pieces, columns, group, size = out_ref.shape
    for a in range(columns):
        total = sums_ref[a][:, :size] + sums_ref[a][:, size:]
        out_ref[:, a] = total.reshape(pieces, group, size)


def first_steps(
    slots, covariances, list_ref, live_ref, theta_ref, tiles_ref, base_ref, d_ref, sums_ref
):
    ds = []
    tiles = []
    for slot, covariance in zip(slots, covariances):
        theta = theta_ref[slot]
        tile = tiles_ref[slot]
        base = theta - STEP * (covariance - tile)
        base_ref[slot] = base
        ds.append(jnp.where(slot < live_ref[0], shrink(base) - theta, 0.0))
        tiles.append(jnp.concatenate(split(tile), axis=1))
    for slot, d in zip(slots, ds):
        d_ref[slot] = d
    add_products(slots, ds, tiles, list_ref, sums_ref)


def near_kernel(near, col_count, list_ref, live_ref, owned_ref, features, far_theta, far_tiles, *rest):
    count = len(near) * CORES
    blocks = rest[:count]
    (
        far_base, far_d, sums_ref, left_ref, right_ref, theta_ref, tiles_ref, base_ref, d_ref,
        left_sem, right_sem, sems,
    ) = rest[count:]
    slots, size, _ = theta_ref.shape
    samples = features.shape[1]
    per_source = CHUNK // CORES
    core = lax.rem(lax.axis_index("col"), CORES)
    arrays = [Tiles(far_theta, theta_ref, sems.at[0]), Tiles(far_tiles, tiles_ref, sems.at[1])]
    outs = [Tiles(far_base, base_ref, sems.at[2], True), Tiles(far_d, d_ref, sems.at[3], True)]

    def left_copy(n):
        place = n // CORES * CHUNK + lax.rem(core + n % CORES, CORES) * per_source
        return pltpu.make_async_copy(
            blocks[n].at[:, pl.ds(0, samples)], left_ref.at[pl.ds(place, per_source)],
            left_sem.at[n],
        )

    def right_copy(a):
        return pltpu.make_async_copy(
            features.at[owned_ref[a]], right_ref.at[a], right_sem.at[a]
        )

    for a in range(right_ref.shape[0]):
        right_copy(a).start()
    for n in range(count):
        left_copy(n).start()
    for dz in near:
        for array in arrays:
            array.start(chip_at(dz, col_count))
    sums_ref[...] = jnp.zeros_like(sums_ref)
    for a in range(right_ref.shape[0]):
        right_copy(a).wait()
    for n in range(count):
        left_copy(n).wait()
    for n, dz in enumerate(near):
        chip = chip_at(dz, col_count)
        for array in arrays:
            array.wait(chip)
        slots_here = [chip * CHUNK + s for s in range(CHUNK)]
        covariances = [
            lax.dot_general(
                left_ref[n * CHUNK + s], right_ref[list_ref[slot]],
                (((0,), (0,)), ((), ())), preferred_element_type=F32,
            ) * (1.0 / samples)
            for s, slot in enumerate(slots_here)
        ]
        first_steps(
            slots_here, covariances, list_ref, live_ref, theta_ref, tiles_ref, base_ref, d_ref,
            sums_ref,
        )
        for out in outs:
            out.start(chip)
    for dz in near:
        for out in outs:
            out.wait(chip_at(dz, col_count))


def first_kernel(
    far, col_count, list_ref, live_ref, cov_ref, near_sums, far_theta, far_tiles, in_base, in_d,
    far_base, far_d, out_ref, theta_ref, tiles_ref, base_ref, d_ref, sums_ref, sum_sem, sems,
):
    slots, size, _ = theta_ref.shape
    arrays = [Tiles(far_theta, theta_ref, sems.at[0]), Tiles(far_tiles, tiles_ref, sems.at[1])]
    outs = [Tiles(far_base, base_ref, sems.at[2], True), Tiles(far_d, d_ref, sems.at[3], True)]
    bring = pltpu.make_async_copy(near_sums, sums_ref, sum_sem.at[0])
    bring.start()
    for dz in far:
        for array in arrays:
            array.start(chip_at(dz, col_count))
    bring.wait()
    for begin in range(0, len(far), 2):
        part = range(begin, min(begin + 2, len(far)))
        chips = [chip_at(far[n], col_count) for n in part]
        for chip in chips:
            for array in arrays:
                array.wait(chip)
        first_steps(
            [chip * CHUNK + s for chip in chips for s in range(CHUNK)],
            [
                cov_ref[:, n * CHUNK + s].reshape(size, size)
                for n in part for s in range(CHUNK)
            ],
            list_ref, live_ref, theta_ref, tiles_ref, base_ref, d_ref, sums_ref,
        )
        for chip in chips:
            for out in outs:
                out.start(chip)
    write_sums(sums_ref, out_ref)
    for dz in far:
        for out in outs:
            out.wait(chip_at(dz, col_count))


def diagonal_kernel(half, list_ref, far_base, far_d, col_diag_ref, *rest):
    far_out, base_ref, d_ref, diag_ref, out_ref, diag_sem, sems = rest[-7:]
    chips = diag_sem.shape[0] // CORES
    near, far_diag = rest[:CORES], rest[CORES:CORES + chips - 1]
    slots, size, _ = d_ref.shape
    chunks = slots // MANY
    mine = range(half * chunks // 2, (half + 1) * chunks // 2)
    c = lax.axis_index("col")
    per_source = CHUNK // CORES
    arrays = [
        Tiles(far_d, d_ref, sems.at[1], count=MANY),
        Tiles(far_base, base_ref, sems.at[0], count=MANY),
    ]
    out = Tiles(far_out, out_ref, sems.at[2], True, count=MANY)

    def with_diag(n, use):
        dz, dk = n // CORES, n % CORES
        if dz == 0:
            source = near[dk].at[:, pl.ds(near[dk].shape[1] - size, size)]
        else:
            source = far_diag[dz - 1].at[pl.ds(dk * per_source, per_source)]
        place = holder(c, dz, dk, chips * CORES) * per_source

        @pl.when(place // (slots // 2) == half)
        def _():
            use(pltpu.make_async_copy(
                source, diag_ref.at[pl.ds(place, per_source)], diag_sem.at[n]
            ))

    for n in range(chips * CORES):
        with_diag(n, lambda copy: copy.start())
    for i in mine:
        for array in arrays:
            array.start(i)
    for n in range(chips * CORES):
        with_diag(n, lambda copy: copy.wait())
    for i in mine:
        for array in arrays:
            array.wait(i)
        slots_here = [i * MANY + s for s in range(MANY)]
        halves = [
            dot(diag_ref[slot], jnp.concatenate(split(d_ref[slot]), axis=1))
            for slot in slots_here
        ]
        for slot, x in zip(slots_here, halves):
            left = jnp.concatenate(split(x[:, :size] + x[:, size:]), axis=1)
            right = col_diag_ref[list_ref[slot]]
            both = dot(left, jnp.concatenate([right, right], axis=0))
            out_ref[slot] = base_ref[slot] + d_ref[slot] - STEP * both
        out.start(i)
    for i in mine:
        out.wait(i)


def sum_kernel(same_ref, in_ref, out_ref):
    same = same_ref[...].astype(BF)
    for g in range(in_ref.shape[1]):
        x = in_ref[:, g, :]
        x1, rest = x.astype(BF), x
        rest = rest - x1.astype(F32)
        x2 = rest.astype(BF)
        rest = rest - x2.astype(F32)
        x3 = rest.astype(BF)
        out_ref[:, g, :] = dot(
            jnp.concatenate([same, same, same], axis=1), jnp.concatenate([x1, x2, x3], axis=0)
        )


def sweep_kernel(
    last, list_ref, live_ref, far_t, far_theta, far_pairs, q_ref, far_d, *rest
):
    if last:
        t_ref, theta_ref, pairs_ref, d_ref, right_ref, sems = rest
    else:
        out_ref, t_ref, theta_ref, pairs_ref, d_ref, right_ref, sems, sums_ref = rest
    slots, size, _ = theta_ref.shape
    chunks = slots // MANY
    arrays = [
        Tiles(far_pairs, pairs_ref, sems.at[0], count=MANY),
        Tiles(far_t, t_ref, sems.at[1], count=MANY),
        Tiles(far_theta, theta_ref, sems.at[2], count=MANY),
    ]
    out = Tiles(far_d, d_ref, sems.at[3], True, count=MANY)
    start_all(arrays, chunks)
    for a in range(q_ref.shape[1]):
        q = q_ref[:, a].reshape(size, size)
        right_ref[a] = pair(jnp.concatenate(split(q), axis=1))
    if not last:
        sums_ref[...] = jnp.zeros_like(sums_ref)

    def step(i, carry):
        for array in arrays:
            array.wait(i)
        slots_here = [i * MANY + s for s in range(MANY)]
        both = [dot(pairs_ref[slot], right_ref[list_ref[slot]]) for slot in slots_here]
        ds = []
        for slot, x in zip(slots_here, both):
            product = x[:, :size] + x[:, size:]
            d = shrink(t_ref[slot] - STEP * product) - theta_ref[slot]
            ds.append(jnp.where(slot < live_ref[0], d, 0.0))
        for slot, d in zip(slots_here, ds):
            d_ref[slot] = d
        if not last:
            tiles = [pairs_ref[slot] for slot in slots_here]
            add_products(slots_here, ds, tiles, list_ref, sums_ref)
        out.start(i)
        return carry

    lax.fori_loop(0, chunks, step, 0)
    if not last:
        write_sums(sums_ref, out_ref)
    for i in range(chunks):
        out.wait(i)


def shape(dims, dtype):
    return jax.ShapeDtypeStruct(dims, dtype)


def far(x):
    return pltpu.with_memory_space_constraint(x, pltpu.HBM)


def slot_blocks(*dims):
    return pl.BlockSpec((PER_STEP,) + dims, lambda i: (i,) + (0,) * len(dims))


def body(
    features,
    diag_inverse,
    precision_tiles,
    inverse_tiles,
    slot_rows,
    slot_columns,
    owned_columns,
    live_counts,
):
    row_count = lax.axis_size("row")
    col_count = lax.axis_size("col")
    r = lax.axis_index("row")
    c = lax.axis_index("col")
    blocks, samples, size = features.shape
    slots = precision_tiles.shape[2]
    columns = owned_columns.shape[2]
    per_source = slots // col_count
    group = size // row_count
    theta = precision_tiles[0, 0]
    tiles = inverse_tiles[0, 0]
    tile_shape = (slots, size, size)
    piece_shape = (row_count, columns, group, size)

    with jax.named_scope("slices"):
        mine = pl.pallas_call(
            functools.partial(slice_kernel, group),
            in_specs=[HBM],
            out_specs=VMEM,
            out_shape=shape((blocks, group, samples), BF),
            scratch_shapes=[
                pltpu.VMEM(features.shape, BF), pltpu.SemaphoreType.DMA((4,))
            ],
            compiler_params=PARAMS,
        )(far(features))
        slices = lax.all_gather(mine, "col", axis=0, tiled=True)

    with jax.named_scope("tables"):
        rows_here = lax.dynamic_index_in_dim(slot_rows, c, 1, keepdims=False)
        lists_here = lax.dynamic_index_in_dim(slot_columns, c, 1, keepdims=False)
        owned_here = lax.dynamic_index_in_dim(owned_columns, c, 1, keepdims=False) - c * blocks
        my_list = lax.dynamic_index_in_dim(lists_here, r, 0, keepdims=False)
        live = lax.dynamic_slice(live_counts, (r, c), (1, 1)).reshape(1)
        wanted = lax.dynamic_slice(
            slot_rows, (r, 0, c * per_source), (1, col_count, per_source)
        ).reshape(col_count, per_source) - c * blocks
        flat = owned_here.reshape(-1)
        same = (flat[:, None] == flat[None, :]).astype(F32)
        my_owned = lax.dynamic_index_in_dim(owned_here, r, 0, keepdims=False)
        col_diag = jnp.take(diag_inverse, my_owned, axis=0)

    tile_vmem = pltpu.VMEM(tile_shape, F32)
    tile_out = pltpu.HBM(tile_shape, F32)
    sums = pltpu.VMEM((columns, size, 2 * size), F32)
    chunks = slots // CHUNK

    def sems(*dims):
        return pltpu.SemaphoreType.DMA(dims)

    with jax.named_scope("split"):
        pairs = pl.pallas_call(
            split_kernel,
            grid=(slots // PER_STEP,),
            in_specs=[slot_blocks(size, size)],
            out_specs=slot_blocks(size, 2 * size),
            out_shape=pltpu.HBM((slots, size, 2 * size), BF),
        )(far(tiles))

    with jax.named_scope("blocks"):
        chips = col_count // CORES
        near = [0]
        far_chips = list(range(1, chips))
        near_count = CORES
        near_shape = (per_source, samples + size, size)
        swap_shape = (chips - 1, per_source, size, size)
        far_shape = (CORES * per_source, size, size)
        mine, wanted = lax.optimization_barrier((mine, wanted))
        own, other, swap = pl.pallas_call(
            near_gather_kernel,
            in_specs=[SMEM, HBM, HBM],
            out_specs=[HBM] * 3,
            out_shape=[
                pltpu.HBM(near_shape, BF), pltpu.HBM(near_shape, BF), pltpu.HBM(swap_shape, BF)
            ],
            scratch_shapes=[
                pltpu.VMEM((CORES,) + near_shape, BF),
                pltpu.VMEM(swap_shape, BF),
                sems(CORES, per_source, 2),
                sems(chips - 1, per_source),
                sems(CORES + 1),
            ],
            compiler_params=PARAMS,
        )(wanted, far(features), far(diag_inverse))
        to_other = [
            (i, i // CORES * CORES + (i + 1) % CORES) for i in range(col_count)
        ]
        swapped = lax.ppermute(swap, "col", to_other)
        got_blocks = [own, lax.ppermute(other, "col", to_other)]
        far_out = list(pl.pallas_call(
            far_gather_kernel,
            in_specs=[SMEM, HBM, HBM],
            out_specs=[HBM] * (chips - 1),
            out_shape=[pltpu.HBM(far_shape, BF)] * (chips - 1),
            scratch_shapes=[
                pltpu.VMEM((chips - 1,) + far_shape, BF),
                sems(chips - 1, per_source + 1),
                sems(chips - 1),
            ],
            compiler_params=PARAMS,
        )(wanted, far(diag_inverse), far(swapped)))

        def send(dz):
            return lax.ppermute(far_out[dz - 1], "col", [
                (h, (h // CORES - dz) % chips * CORES + h % CORES) for h in range(col_count)
            ])

        early = [1, chips - 1]
        late = far_chips[1:-1]
        sent = {dz: send(dz) for dz in early}
        base, d, near_sums = pl.pallas_call(
            functools.partial(near_kernel, near, col_count),
            in_specs=[SMEM, SMEM, SMEM] + [HBM] * (3 + near_count),
            out_specs=[HBM] * 2 + [VMEM],
            out_shape=[tile_out, tile_out, pltpu.HBM((columns, size, 2 * size), F32)],
            scratch_shapes=[
                pltpu.VMEM((len(near) * CHUNK, samples, size), BF),
                pltpu.VMEM((columns, samples, size), BF),
                tile_vmem, tile_vmem, tile_vmem, tile_vmem,
                sems(near_count), sems(columns), sems(4, chunks),
            ],
            compiler_params=PARAMS,
        )(
            my_list, live, my_owned, far(features), far(theta), far(tiles),
            *[far(block) for block in got_blocks[:near_count]],
        )
        slices, pairs, got_blocks, base, d, near_sums, sent, far_out = lax.optimization_barrier(
            (slices, pairs, got_blocks, base, d, near_sums, sent, far_out)
        )

    far_slots = len(far_chips) * CHUNK
    with jax.named_scope("covariance"):
        partial = pl.pallas_call(
            functools.partial(covariance_kernel, far_chips, col_count),
            in_specs=[SMEM, SMEM, SMEM, HBM, HBM],
            out_specs=HBM,
            out_shape=pltpu.HBM((row_count, far_slots, group, size), F32),
            scratch_shapes=[
                pltpu.VMEM(slices.shape, BF),
                pltpu.VMEM(features.shape, BF),
                pltpu.VMEM((row_count, far_slots, group, size), F32),
                sems(2),
                sems(2),
                sems(row_count),
            ],
            compiler_params=PARAMS,
        )(rows_here, lists_here, owned_here, far(slices), far(features))
        covariance = lax.all_to_all(partial, "row", split_axis=0, concat_axis=0, tiled=True)

    with jax.named_scope("diag"):
        far_out, _ = lax.optimization_barrier((far_out, partial[0, 0]))
        sent.update({dz: send(dz) for dz in late})
        got_blocks = got_blocks + [sent[dz] for dz in far_chips]

    with jax.named_scope("first"):
        base, d, pieces = pl.pallas_call(
            functools.partial(first_kernel, far_chips, col_count),
            in_specs=[SMEM, SMEM, VMEM] + [HBM] * 5,
            out_specs=[HBM, HBM, VMEM],
            out_shape=[tile_out, tile_out, shape(piece_shape, F32)],
            scratch_shapes=[
                tile_vmem, tile_vmem, tile_vmem, tile_vmem, sums, sems(1), sems(4, chunks),
            ],
            input_output_aliases={6: 0, 7: 1},
            compiler_params=PARAMS,
        )(
            my_list, live, covariance, far(near_sums), far(theta), far(tiles), far(base), far(d)
        )

    def diagonal(half, base, d, col_diag, before=()):
        operands = [my_list, far(base), far(d), col_diag]
        operands += [far(block) for block in got_blocks] + [far(x) for x in before]
        with jax.named_scope("diagonal"):
            return pl.pallas_call(
                functools.partial(diagonal_kernel, half),
                in_specs=[SMEM, HBM, HBM, VMEM] + [HBM] * (len(operands) - 4),
                out_specs=HBM,
                out_shape=tile_out,
                scratch_shapes=[
                    tile_vmem, tile_vmem, pltpu.VMEM(tile_shape, BF), tile_vmem,
                    sems(col_count), sems(3, slots // MANY),
                ],
                input_output_aliases={len(operands) - 1: 0} if before else {},
                compiler_params=PARAMS,
            )(*operands)

    for sweep in range(1, SWEEPS):
        last = sweep == SWEEPS - 1
        with jax.named_scope("exchange"):
            flat_shape = (row_count * columns, group, size)
            got = lax.all_to_all(pieces, "row", split_axis=0, concat_axis=0, tiled=True)
            t = diagonal(0, base, d, col_diag)
            got, t = lax.optimization_barrier((got, t))
            summed = pl.pallas_call(
                sum_kernel,
                in_specs=[VMEM, VMEM],
                out_specs=VMEM,
                out_shape=shape(flat_shape, F32),
                compiler_params=PARAMS,
            )(same, got.reshape(flat_shape))
            q = lax.all_to_all(
                summed.reshape(piece_shape), "row", split_axis=0, concat_axis=0, tiled=True
            )
            d, t, _ = lax.optimization_barrier((d, t, summed[0]))
            t = diagonal(1, base, d, col_diag, (t,))
        with jax.named_scope("sweep"):
            result = pl.pallas_call(
                functools.partial(sweep_kernel, last),
                in_specs=[SMEM, SMEM, HBM, HBM, HBM, VMEM],
                out_specs=[HBM] if last else [HBM, VMEM],
                out_shape=[tile_out] if last else [tile_out, shape(piece_shape, F32)],
                scratch_shapes=[
                    tile_vmem, tile_vmem, pltpu.VMEM((slots, size, 2 * size), BF), tile_vmem,
                    pltpu.VMEM((columns, 2 * size, 2 * size), BF), sems(4, slots // MANY),
                ] + ([] if last else [sums]),
                compiler_params=PARAMS,
            )(my_list, live, far(t), far(theta), far(pairs), q)
            d = result[0]
            if not last:
                pieces = result[1]
    return d.reshape(precision_tiles.shape)


def solution(mesh):
    return jax.shard_map(
        body,
        mesh=mesh,
        in_specs=(
            P("col", None, None),
            P("col", None, None),
            P("row", "col", None, None, None),
            P("row", "col", None, None, None),
            P(),
            P(),
            P(),
            P(),
        ),
        out_specs=P("row", "col", None, None, None),
        check_vma=False,
    )
```

```python
import functools

import jax
import jax.numpy as jnp
from jax import lax
from jax.experimental import pallas as pl
from jax.experimental.pallas import tpu as pltpu
from jax.sharding import PartitionSpec as P

SWEEPS = 4
STEP = 0.3
LAMBDA = 0.3 * 0.6
PER_STEP = 8
CHUNK = 4
CORES = 2
MANY = 8

BF = jnp.bfloat16
F32 = jnp.float32
VMEM = pl.BlockSpec(memory_space=pltpu.VMEM)
HBM = pl.BlockSpec(memory_space=pltpu.HBM)
SMEM = pl.BlockSpec(memory_space=pltpu.SMEM)
PARAMS = pltpu.CompilerParams(vmem_limit_bytes=20 * 1024 * 1024)


def split(x):
    high = x.astype(BF)
    low = (x - high.astype(F32)).astype(BF)
    return high, low


def dot(a, b):
    return jnp.dot(a, b, preferred_element_type=F32)


def shrink(x):
    return x - jnp.clip(x, -LAMBDA, LAMBDA)


def slice_kernel(group, features, out_ref, near_ref, sems):
    r = lax.axis_index("row")
    blocks, _, variables = features.shape
    parts = sems.shape[0]
    count = blocks // parts

    def copy(i):
        part = pl.ds(i * count, count)
        return pltpu.make_async_copy(features.at[part], near_ref.at[part], sems.at[i])

    for i in range(parts):
        copy(i).start()
    wanted = lax.broadcasted_iota(jnp.int32, (group, variables), 0) + r * group
    pick = (lax.broadcasted_iota(jnp.int32, (group, variables), 1) == wanted).astype(BF)

    def step(i, carry):
        copy(i).wait()
        for b in range(count):
            rows = lax.dot_general(
                pick, near_ref[i * count + b], (((1,), (1,)), ((), ())),
                preferred_element_type=F32,
            )
            out_ref[i * count + b] = rows.astype(BF)
        return carry

    lax.fori_loop(0, parts, step, 0)


def split_kernel(tiles_ref, out_ref):
    for s in range(tiles_ref.shape[0]):
        out_ref[s] = jnp.concatenate(split(tiles_ref[s]), axis=1)


def near_gather_kernel(wanted_ref, features, diag, own_out, other_out, swap_out, near_ref, swap_ref, sems, swap_sems, out_sems):
    c = lax.axis_index("col")
    col_count = wanted_ref.shape[0]
    samples = features.shape[1]
    size = diag.shape[1]
    outs = (own_out, other_out)
    first = []
    for dk in range(CORES):
        target = holder(c, 0, dk, col_count)
        for p in range(own_out.shape[0]):
            block = wanted_ref[target, p]
            first.append(pltpu.make_async_copy(
                features.at[block], near_ref.at[dk, p, pl.ds(0, samples)], sems.at[dk, p, 0]
            ))
            first.append(pltpu.make_async_copy(
                diag.at[block], near_ref.at[dk, p, pl.ds(samples, size)], sems.at[dk, p, 1]
            ))
    second = [
        pltpu.make_async_copy(
            diag.at[wanted_ref[holder(c, -(n + 1), 1, col_count), p]],
            swap_ref.at[n, p],
            swap_sems.at[n, p],
        )
        for n in range(swap_ref.shape[0]) for p in range(swap_ref.shape[1])
    ]
    for copy in first + second:
        copy.start()
    backs = [
        pltpu.make_async_copy(near_ref.at[dk], outs[dk], out_sems.at[dk]) for dk in range(CORES)
    ]
    backs.append(pltpu.make_async_copy(swap_ref, swap_out, out_sems.at[CORES]))
    for copy in first:
        copy.wait()
    for back in backs[:-1]:
        back.start()
    for copy in second:
        copy.wait()
    backs[-1].start()
    for back in backs:
        back.wait()


def far_gather_kernel(wanted_ref, diag, swapped, *rest):
    outs, (near_ref, sems, out_sems) = rest[:-3], rest[-3:]
    c = lax.axis_index("col")
    count = swapped.shape[1]
    backs = []
    copies = []
    for n, out in enumerate(outs):
        target = holder(c, -(n + 1), 0, wanted_ref.shape[0])
        mine = [
            pltpu.make_async_copy(
                diag.at[wanted_ref[target, p]], near_ref.at[n, p], sems.at[n, p]
            )
            for p in range(count)
        ]
        mine.append(pltpu.make_async_copy(
            swapped.at[n], near_ref.at[n, pl.ds(count, count)], sems.at[n, count]
        ))
        for copy in mine:
            copy.start()
        copies.append(mine)
        backs.append(pltpu.make_async_copy(near_ref.at[n], out, out_sems.at[n]))
    for mine, back in zip(copies, backs):
        for copy in mine:
            copy.wait()
        back.start()
    for back in backs:
        back.wait()


def holder(c, dz, dk, col_count):
    chips = col_count // CORES
    z = lax.rem(c // CORES + dz + chips, chips)
    return z * CORES + lax.rem(c + dk, CORES)


def chip_at(dz, col_count):
    return lax.rem(lax.axis_index("col") // CORES + dz, col_count // CORES)


class Tiles:
    def __init__(self, far_ref, near_ref, sem, back=False, count=CHUNK):
        self.refs = (near_ref, far_ref) if back else (far_ref, near_ref)
        self.sem = sem
        self.count = count

    def copy(self, i):
        part = pl.ds(i * self.count, self.count)
        source, target = (ref.at[part] for ref in self.refs)
        return pltpu.make_async_copy(source, target, self.sem.at[i])

    def start(self, i):
        self.copy(i).start()

    def wait(self, i):
        self.copy(i).wait()


def start_all(arrays, chunks):
    for i in range(chunks):
        for array in arrays:
            array.start(i)


def each_slot(chunks, arrays, outs, slot_step):
    def step(i, carry):
        for array in arrays:
            array.wait(i)
        for s in range(CHUNK):
            slot_step(i * CHUNK + s)
        for out in outs:
            out.start(i)
        return carry

    lax.fori_loop(0, chunks, step, 0)
    for i in range(chunks):
        for out in outs:
            out.wait(i)


def covariance_kernel(
    far, col_count, rows_ref, lists_ref, owned_ref, far_slices, features, far_out,
    slices_ref, right_ref, out_ref, slice_sem, right_sem, out_sem,
):
    owners = rows_ref.shape[0]
    columns = owned_ref.shape[1]
    group = slices_ref.shape[1]
    _, samples, size = features.shape
    slots = [chip_at(dz, col_count) * CHUNK + s for dz in far for s in range(CHUNK)]

    def halves(source, target, sem):
        count = source.shape[0] // 2
        parts = [pl.ds(i * count, count) for i in range(2)]
        return [
            pltpu.make_async_copy(source.at[part], target.at[part], sem.at[i])
            for i, part in enumerate(parts)
        ]

    def out_copy(owner):
        return pltpu.make_async_copy(out_ref.at[owner], far_out.at[owner], out_sem.at[owner])

    copies = halves(far_slices, slices_ref, slice_sem) + halves(features, right_ref, right_sem)
    for copy in copies:
        copy.start()
    for copy in copies:
        copy.wait()

    def owner_step(owner, carry):
        left = jnp.concatenate(
            [slices_ref[rows_ref[owner, slot]].astype(F32) for slot in slots], axis=0
        ).astype(BF)
        right = jnp.concatenate(
            [right_ref[owned_ref[owner, a]] for a in range(columns)], axis=1
        )
        both = dot(left, right) * (1.0 / samples)
        for k, slot in enumerate(slots):
            rows = both[k * group:(k + 1) * group]
            out_ref[owner, k] = jnp.where(
                lists_ref[owner, slot] == 0, rows[:, :size], rows[:, size:]
            )
        out_copy(owner).start()
        return carry

    lax.fori_loop(0, owners, owner_step, 0, unroll=4)
    for owner in range(owners):
        out_copy(owner).wait()


def pair(x):
    size = x.shape[0]
    high = x[:, :size]
    return jnp.concatenate(
        [x, jnp.concatenate([high, jnp.zeros_like(high)], axis=1)], axis=0
    )


def add_products(slots, ds, tiles, list_ref, sums_ref):
    lefts = [jnp.concatenate(split(d.T), axis=1) for d in ds]
    products = [dot(left, pair(tile)) for left, tile in zip(lefts, tiles)]
    for slot, product in zip(slots, products):
        sums_ref[list_ref[slot]] += product


def write_sums(sums_ref, out_ref):
    pieces, columns, group, size = out_ref.shape
    for a in range(columns):
        total = sums_ref[a][:, :size] + sums_ref[a][:, size:]
        out_ref[:, a] = total.reshape(pieces, group, size)


def first_steps(
    slots, covariances, list_ref, live_ref, theta_ref, tiles_ref, base_ref, d_ref, sums_ref
):
    ds = []
    tiles = []
    for slot, covariance in zip(slots, covariances):
        theta = theta_ref[slot]
        tile = tiles_ref[slot]
        base = theta - STEP * (covariance - tile)
        base_ref[slot] = base
        ds.append(jnp.where(slot < live_ref[0], shrink(base) - theta, 0.0))
        tiles.append(jnp.concatenate(split(tile), axis=1))
    for slot, d in zip(slots, ds):
        d_ref[slot] = d
    add_products(slots, ds, tiles, list_ref, sums_ref)


def near_kernel(near, col_count, list_ref, live_ref, owned_ref, features, far_theta, far_tiles, *rest):
    count = len(near) * CORES
    blocks = rest[:count]
    (
        far_base, far_d, sums_ref, left_ref, right_ref, theta_ref, tiles_ref, base_ref, d_ref,
        left_sem, right_sem, sems,
    ) = rest[count:]
    slots, size, _ = theta_ref.shape
    samples = features.shape[1]
    per_source = CHUNK // CORES
    core = lax.rem(lax.axis_index("col"), CORES)
    arrays = [Tiles(far_theta, theta_ref, sems.at[0]), Tiles(far_tiles, tiles_ref, sems.at[1])]
    outs = [Tiles(far_base, base_ref, sems.at[2], True), Tiles(far_d, d_ref, sems.at[3], True)]

    def left_copy(n):
        place = n // CORES * CHUNK + lax.rem(core + n % CORES, CORES) * per_source
        return pltpu.make_async_copy(
            blocks[n].at[:, pl.ds(0, samples)], left_ref.at[pl.ds(place, per_source)],
            left_sem.at[n],
        )

    def right_copy(a):
        return pltpu.make_async_copy(
            features.at[owned_ref[a]], right_ref.at[a], right_sem.at[a]
        )

    for a in range(right_ref.shape[0]):
        right_copy(a).start()
    for n in range(count):
        left_copy(n).start()
    for dz in near:
        for array in arrays:
            array.start(chip_at(dz, col_count))
    sums_ref[...] = jnp.zeros_like(sums_ref)
    for a in range(right_ref.shape[0]):
        right_copy(a).wait()
    for n in range(count):
        left_copy(n).wait()
    for n, dz in enumerate(near):
        chip = chip_at(dz, col_count)
        for array in arrays:
            array.wait(chip)
        slots_here = [chip * CHUNK + s for s in range(CHUNK)]
        covariances = [
            lax.dot_general(
                left_ref[n * CHUNK + s], right_ref[list_ref[slot]],
                (((0,), (0,)), ((), ())), preferred_element_type=F32,
            ) * (1.0 / samples)
            for s, slot in enumerate(slots_here)
        ]
        first_steps(
            slots_here, covariances, list_ref, live_ref, theta_ref, tiles_ref, base_ref, d_ref,
            sums_ref,
        )
        for out in outs:
            out.start(chip)
    for dz in near:
        for out in outs:
            out.wait(chip_at(dz, col_count))


def first_kernel(
    far, col_count, list_ref, live_ref, cov_ref, near_sums, far_theta, far_tiles, in_base, in_d,
    far_base, far_d, out_ref, theta_ref, tiles_ref, base_ref, d_ref, sums_ref, sum_sem, sems,
):
    slots, size, _ = theta_ref.shape
    arrays = [Tiles(far_theta, theta_ref, sems.at[0]), Tiles(far_tiles, tiles_ref, sems.at[1])]
    outs = [Tiles(far_base, base_ref, sems.at[2], True), Tiles(far_d, d_ref, sems.at[3], True)]
    bring = pltpu.make_async_copy(near_sums, sums_ref, sum_sem.at[0])
    bring.start()
    for dz in far:
        for array in arrays:
            array.start(chip_at(dz, col_count))
    bring.wait()
    for begin in range(0, len(far), 2):
        part = range(begin, min(begin + 2, len(far)))
        chips = [chip_at(far[n], col_count) for n in part]
        for chip in chips:
            for array in arrays:
                array.wait(chip)
        first_steps(
            [chip * CHUNK + s for chip in chips for s in range(CHUNK)],
            [
                cov_ref[:, n * CHUNK + s].reshape(size, size)
                for n in part for s in range(CHUNK)
            ],
            list_ref, live_ref, theta_ref, tiles_ref, base_ref, d_ref, sums_ref,
        )
        for chip in chips:
            for out in outs:
                out.start(chip)
    write_sums(sums_ref, out_ref)
    for dz in far:
        for out in outs:
            out.wait(chip_at(dz, col_count))


def diagonal_kernel(half, list_ref, far_base, far_d, col_diag_ref, *rest):
    far_out, base_ref, d_ref, diag_ref, out_ref, diag_sem, sems = rest[-7:]
    chips = diag_sem.shape[0] // CORES
    near, far_diag = rest[:CORES], rest[CORES:CORES + chips - 1]
    slots, size, _ = d_ref.shape
    chunks = slots // MANY
    mine = range(half * chunks // 2, (half + 1) * chunks // 2)
    c = lax.axis_index("col")
    per_source = CHUNK // CORES
    arrays = [
        Tiles(far_d, d_ref, sems.at[1], count=MANY),
        Tiles(far_base, base_ref, sems.at[0], count=MANY),
    ]
    out = Tiles(far_out, out_ref, sems.at[2], True, count=MANY)

    def with_diag(n, use):
        dz, dk = n // CORES, n % CORES
        if dz == 0:
            source = near[dk].at[:, pl.ds(near[dk].shape[1] - size, size)]
        else:
            source = far_diag[dz - 1].at[pl.ds(dk * per_source, per_source)]
        place = holder(c, dz, dk, chips * CORES) * per_source

        @pl.when(place // (slots // 2) == half)
        def _():
            use(pltpu.make_async_copy(
                source, diag_ref.at[pl.ds(place, per_source)], diag_sem.at[n]
            ))

    for n in range(chips * CORES):
        with_diag(n, lambda copy: copy.start())
    for i in mine:
        for array in arrays:
            array.start(i)
    for n in range(chips * CORES):
        with_diag(n, lambda copy: copy.wait())
    for i in mine:
        for array in arrays:
            array.wait(i)
        slots_here = [i * MANY + s for s in range(MANY)]
        halves = [
            dot(diag_ref[slot], jnp.concatenate(split(d_ref[slot]), axis=1))
            for slot in slots_here
        ]
        for slot, x in zip(slots_here, halves):
            left = jnp.concatenate(split(x[:, :size] + x[:, size:]), axis=1)
            right = col_diag_ref[list_ref[slot]]
            both = dot(left, jnp.concatenate([right, right], axis=0))
            out_ref[slot] = base_ref[slot] + d_ref[slot] - STEP * both
        out.start(i)
    for i in mine:
        out.wait(i)


def sum_kernel(same_ref, in_ref, out_ref):
    same = same_ref[...].astype(BF)
    for g in range(in_ref.shape[1]):
        x = in_ref[:, g, :]
        x1, rest = x.astype(BF), x
        rest = rest - x1.astype(F32)
        x2 = rest.astype(BF)
        rest = rest - x2.astype(F32)
        x3 = rest.astype(BF)
        out_ref[:, g, :] = dot(
            jnp.concatenate([same, same, same], axis=1), jnp.concatenate([x1, x2, x3], axis=0)
        )


def sweep_kernel(
    last, list_ref, live_ref, far_t, far_theta, far_pairs, q_ref, far_d, *rest
):
    if last:
        t_ref, theta_ref, pairs_ref, d_ref, right_ref, sems = rest
    else:
        out_ref, t_ref, theta_ref, pairs_ref, d_ref, right_ref, sems, sums_ref = rest
    slots, size, _ = theta_ref.shape
    chunks = slots // MANY
    arrays = [
        Tiles(far_pairs, pairs_ref, sems.at[0], count=MANY),
        Tiles(far_t, t_ref, sems.at[1], count=MANY),
        Tiles(far_theta, theta_ref, sems.at[2], count=MANY),
    ]
    out = Tiles(far_d, d_ref, sems.at[3], True, count=MANY)
    start_all(arrays, chunks)
    for a in range(q_ref.shape[1]):
        q = q_ref[:, a].reshape(size, size)
        right_ref[a] = pair(jnp.concatenate(split(q), axis=1))
    if not last:
        sums_ref[...] = jnp.zeros_like(sums_ref)

    def step(i, carry):
        for array in arrays:
            array.wait(i)
        slots_here = [i * MANY + s for s in range(MANY)]
        both = [dot(pairs_ref[slot], right_ref[list_ref[slot]]) for slot in slots_here]
        ds = []
        for slot, x in zip(slots_here, both):
            product = x[:, :size] + x[:, size:]
            d = shrink(t_ref[slot] - STEP * product) - theta_ref[slot]
            ds.append(jnp.where(slot < live_ref[0], d, 0.0))
        for slot, d in zip(slots_here, ds):
            d_ref[slot] = d
        if not last:
            tiles = [pairs_ref[slot] for slot in slots_here]
            add_products(slots_here, ds, tiles, list_ref, sums_ref)
        out.start(i)
        return carry

    lax.fori_loop(0, chunks, step, 0)
    if not last:
        write_sums(sums_ref, out_ref)
    for i in range(chunks):
        out.wait(i)


def shape(dims, dtype):
    return jax.ShapeDtypeStruct(dims, dtype)


def far(x):
    return pltpu.with_memory_space_constraint(x, pltpu.HBM)


def slot_blocks(*dims):
    return pl.BlockSpec((PER_STEP,) + dims, lambda i: (i,) + (0,) * len(dims))


def body(
    features,
    diag_inverse,
    precision_tiles,
    inverse_tiles,
    slot_rows,
    slot_columns,
    owned_columns,
    live_counts,
):
    row_count = lax.axis_size("row")
    col_count = lax.axis_size("col")
    r = lax.axis_index("row")
    c = lax.axis_index("col")
    blocks, samples, size = features.shape
    slots = precision_tiles.shape[2]
    columns = owned_columns.shape[2]
    per_source = slots // col_count
    group = size // row_count
    theta = precision_tiles[0, 0]
    tiles = inverse_tiles[0, 0]
    tile_shape = (slots, size, size)
    piece_shape = (row_count, columns, group, size)

    with jax.named_scope("slices"):
        mine = pl.pallas_call(
            functools.partial(slice_kernel, group),
            in_specs=[HBM],
            out_specs=VMEM,
            out_shape=shape((blocks, group, samples), BF),
            scratch_shapes=[
                pltpu.VMEM(features.shape, BF), pltpu.SemaphoreType.DMA((4,))
            ],
            compiler_params=PARAMS,
        )(far(features))
        slices = lax.all_gather(mine, "col", axis=0, tiled=True)

    with jax.named_scope("tables"):
        rows_here = lax.dynamic_index_in_dim(slot_rows, c, 1, keepdims=False)
        lists_here = lax.dynamic_index_in_dim(slot_columns, c, 1, keepdims=False)
        owned_here = lax.dynamic_index_in_dim(owned_columns, c, 1, keepdims=False) - c * blocks
        my_list = lax.dynamic_index_in_dim(lists_here, r, 0, keepdims=False)
        live = lax.dynamic_slice(live_counts, (r, c), (1, 1)).reshape(1)
        wanted = lax.dynamic_slice(
            slot_rows, (r, 0, c * per_source), (1, col_count, per_source)
        ).reshape(col_count, per_source) - c * blocks
        flat = owned_here.reshape(-1)
        same = (flat[:, None] == flat[None, :]).astype(F32)
        my_owned = lax.dynamic_index_in_dim(owned_here, r, 0, keepdims=False)
        col_diag = jnp.take(diag_inverse, my_owned, axis=0)

    tile_vmem = pltpu.VMEM(tile_shape, F32)
    tile_out = pltpu.HBM(tile_shape, F32)
    sums = pltpu.VMEM((columns, size, 2 * size), F32)
    chunks = slots // CHUNK

    def sems(*dims):
        return pltpu.SemaphoreType.DMA(dims)

    with jax.named_scope("split"):
        pairs = pl.pallas_call(
            split_kernel,
            grid=(slots // PER_STEP,),
            in_specs=[slot_blocks(size, size)],
            out_specs=slot_blocks(size, 2 * size),
            out_shape=pltpu.HBM((slots, size, 2 * size), BF),
        )(far(tiles))

    with jax.named_scope("blocks"):
        chips = col_count // CORES
        near = [0]
        far_chips = list(range(1, chips))
        near_count = CORES
        near_shape = (per_source, samples + size, size)
        swap_shape = (chips - 1, per_source, size, size)
        far_shape = (CORES * per_source, size, size)
        mine, wanted = lax.optimization_barrier((mine, wanted))
        own, other, swap = pl.pallas_call(
            near_gather_kernel,
            in_specs=[SMEM, HBM, HBM],
            out_specs=[HBM] * 3,
            out_shape=[
                pltpu.HBM(near_shape, BF), pltpu.HBM(near_shape, BF), pltpu.HBM(swap_shape, BF)
            ],
            scratch_shapes=[
                pltpu.VMEM((CORES,) + near_shape, BF),
                pltpu.VMEM(swap_shape, BF),
                sems(CORES, per_source, 2),
                sems(chips - 1, per_source),
                sems(CORES + 1),
            ],
            compiler_params=PARAMS,
        )(wanted, far(features), far(diag_inverse))
        to_other = [
            (i, i // CORES * CORES + (i + 1) % CORES) for i in range(col_count)
        ]
        swapped = lax.ppermute(swap, "col", to_other)
        got_blocks = [own, lax.ppermute(other, "col", to_other)]
        far_out = list(pl.pallas_call(
            far_gather_kernel,
            in_specs=[SMEM, HBM, HBM],
            out_specs=[HBM] * (chips - 1),
            out_shape=[pltpu.HBM(far_shape, BF)] * (chips - 1),
            scratch_shapes=[
                pltpu.VMEM((chips - 1,) + far_shape, BF),
                sems(chips - 1, per_source + 1),
                sems(chips - 1),
            ],
            compiler_params=PARAMS,
        )(wanted, far(diag_inverse), far(swapped)))

        def send(dz):
            return lax.ppermute(far_out[dz - 1], "col", [
                (h, (h // CORES - dz) % chips * CORES + h % CORES) for h in range(col_count)
            ])

        base, d, near_sums = pl.pallas_call(
            functools.partial(near_kernel, near, col_count),
            in_specs=[SMEM, SMEM, SMEM] + [HBM] * (3 + near_count),
            out_specs=[HBM] * 2 + [VMEM],
            out_shape=[tile_out, tile_out, pltpu.HBM((columns, size, 2 * size), F32)],
            scratch_shapes=[
                pltpu.VMEM((len(near) * CHUNK, samples, size), BF),
                pltpu.VMEM((columns, samples, size), BF),
                tile_vmem, tile_vmem, tile_vmem, tile_vmem,
                sems(near_count), sems(columns), sems(4, chunks),
            ],
            compiler_params=PARAMS,
        )(
            my_list, live, my_owned, far(features), far(theta), far(tiles),
            *[far(block) for block in got_blocks[:near_count]],
        )
        slices, pairs, got_blocks, base, d, near_sums, far_out = lax.optimization_barrier(
            (slices, pairs, got_blocks, base, d, near_sums, far_out)
        )

    far_slots = len(far_chips) * CHUNK
    with jax.named_scope("covariance"):
        partial = pl.pallas_call(
            functools.partial(covariance_kernel, far_chips, col_count),
            in_specs=[SMEM, SMEM, SMEM, HBM, HBM],
            out_specs=HBM,
            out_shape=pltpu.HBM((row_count, far_slots, group, size), F32),
            scratch_shapes=[
                pltpu.VMEM(slices.shape, BF),
                pltpu.VMEM(features.shape, BF),
                pltpu.VMEM((row_count, far_slots, group, size), F32),
                sems(2),
                sems(2),
                sems(row_count),
            ],
            compiler_params=PARAMS,
        )(rows_here, lists_here, owned_here, far(slices), far(features))
        covariance = lax.all_to_all(partial, "row", split_axis=0, concat_axis=0, tiled=True)

    with jax.named_scope("diag"):
        far_out, _ = lax.optimization_barrier((far_out, partial[0, 0]))
        soon = [1, chips - 1]
        sent = {dz: send(dz) for dz in soon}
        covariance, sent = lax.optimization_barrier((covariance, sent))
        sent.update({dz: send(dz) for dz in far_chips if dz not in soon})
        got_blocks = got_blocks + [sent[dz] for dz in far_chips]

    with jax.named_scope("first"):
        base, d, pieces = pl.pallas_call(
            functools.partial(first_kernel, far_chips, col_count),
            in_specs=[SMEM, SMEM, VMEM] + [HBM] * 5,
            out_specs=[HBM, HBM, VMEM],
            out_shape=[tile_out, tile_out, shape(piece_shape, F32)],
            scratch_shapes=[
                tile_vmem, tile_vmem, tile_vmem, tile_vmem, sums, sems(1), sems(4, chunks),
            ],
            input_output_aliases={6: 0, 7: 1},
            compiler_params=PARAMS,
        )(
            my_list, live, covariance, far(near_sums), far(theta), far(tiles), far(base), far(d)
        )

    def diagonal(half, base, d, col_diag, before=()):
        operands = [my_list, far(base), far(d), col_diag]
        operands += [far(block) for block in got_blocks] + [far(x) for x in before]
        with jax.named_scope("diagonal"):
            return pl.pallas_call(
                functools.partial(diagonal_kernel, half),
                in_specs=[SMEM, HBM, HBM, VMEM] + [HBM] * (len(operands) - 4),
                out_specs=HBM,
                out_shape=tile_out,
                scratch_shapes=[
                    tile_vmem, tile_vmem, pltpu.VMEM(tile_shape, BF), tile_vmem,
                    sems(col_count), sems(3, slots // MANY),
                ],
                input_output_aliases={len(operands) - 1: 0} if before else {},
                compiler_params=PARAMS,
            )(*operands)

    for sweep in range(1, SWEEPS):
        last = sweep == SWEEPS - 1
        with jax.named_scope("exchange"):
            flat_shape = (row_count * columns, group, size)
            got = lax.all_to_all(pieces, "row", split_axis=0, concat_axis=0, tiled=True)
            t = diagonal(0, base, d, col_diag)
            got, t = lax.optimization_barrier((got, t))
            summed = pl.pallas_call(
                sum_kernel,
                in_specs=[VMEM, VMEM],
                out_specs=VMEM,
                out_shape=shape(flat_shape, F32),
                compiler_params=PARAMS,
            )(same, got.reshape(flat_shape))
            q = lax.all_to_all(
                summed.reshape(piece_shape), "row", split_axis=0, concat_axis=0, tiled=True
            )
            d, t, _ = lax.optimization_barrier((d, t, summed[0]))
            t = diagonal(1, base, d, col_diag, (t,))
        with jax.named_scope("sweep"):
            result = pl.pallas_call(
                functools.partial(sweep_kernel, last),
                in_specs=[SMEM, SMEM, HBM, HBM, HBM, VMEM],
                out_specs=[HBM] if last else [HBM, VMEM],
                out_shape=[tile_out] if last else [tile_out, shape(piece_shape, F32)],
                scratch_shapes=[
                    tile_vmem, tile_vmem, pltpu.VMEM((slots, size, 2 * size), BF), tile_vmem,
                    pltpu.VMEM((columns, 2 * size, 2 * size), BF), sems(4, slots // MANY),
                ] + ([] if last else [sums]),
                compiler_params=PARAMS,
            )(my_list, live, far(t), far(theta), far(pairs), q)
            d = result[0]
            if not last:
                pieces = result[1]
    return d.reshape(precision_tiles.shape)


def solution(mesh):
    return jax.shard_map(
        body,
        mesh=mesh,
        in_specs=(
            P("col", None, None),
            P("col", None, None),
            P("row", "col", None, None, None),
            P("row", "col", None, None, None),
            P(),
            P(),
            P(),
            P(),
        ),
        out_specs=P("row", "col", None, None, None),
        check_vma=False,
    )
```

```python
import functools

import jax
import jax.numpy as jnp
from jax import lax
from jax.experimental import pallas as pl
from jax.experimental.pallas import tpu as pltpu
from jax.sharding import PartitionSpec as P

SWEEPS = 4
STEP = 0.3
LAMBDA = 0.3 * 0.6
PER_STEP = 8
CHUNK = 4
CORES = 2
MANY = 8

BF = jnp.bfloat16
F32 = jnp.float32
VMEM = pl.BlockSpec(memory_space=pltpu.VMEM)
HBM = pl.BlockSpec(memory_space=pltpu.HBM)
SMEM = pl.BlockSpec(memory_space=pltpu.SMEM)
PARAMS = pltpu.CompilerParams(vmem_limit_bytes=20 * 1024 * 1024)


def split(x):
    high = x.astype(BF)
    low = (x - high.astype(F32)).astype(BF)
    return high, low


def dot(a, b):
    return jnp.dot(a, b, preferred_element_type=F32)


def shrink(x):
    return x - jnp.clip(x, -LAMBDA, LAMBDA)


def slice_kernel(group, features, out_ref, near_ref, sems):
    r = lax.axis_index("row")
    blocks, _, variables = features.shape
    parts = sems.shape[0]
    count = blocks // parts

    def copy(i):
        part = pl.ds(i * count, count)
        return pltpu.make_async_copy(features.at[part], near_ref.at[part], sems.at[i])

    for i in range(parts):
        copy(i).start()
    wanted = lax.broadcasted_iota(jnp.int32, (group, variables), 0) + r * group
    pick = (lax.broadcasted_iota(jnp.int32, (group, variables), 1) == wanted).astype(BF)

    def step(i, carry):
        copy(i).wait()
        for b in range(count):
            rows = lax.dot_general(
                pick, near_ref[i * count + b], (((1,), (1,)), ((), ())),
                preferred_element_type=F32,
            )
            out_ref[i * count + b] = rows.astype(BF)
        return carry

    lax.fori_loop(0, parts, step, 0)


def split_kernel(tiles_ref, out_ref):
    for s in range(tiles_ref.shape[0]):
        out_ref[s] = jnp.concatenate(split(tiles_ref[s]), axis=1)


def near_gather_kernel(wanted_ref, features, diag, own_out, other_out, swap_out, near_ref, swap_ref, sems, swap_sems, out_sems):
    c = lax.axis_index("col")
    col_count = wanted_ref.shape[0]
    samples = features.shape[1]
    size = diag.shape[1]
    outs = (own_out, other_out)
    first = []
    for dk in range(CORES):
        target = holder(c, 0, dk, col_count)
        for p in range(own_out.shape[0]):
            block = wanted_ref[target, p]
            first.append(pltpu.make_async_copy(
                features.at[block], near_ref.at[dk, p, pl.ds(0, samples)], sems.at[dk, p, 0]
            ))
            first.append(pltpu.make_async_copy(
                diag.at[block], near_ref.at[dk, p, pl.ds(samples, size)], sems.at[dk, p, 1]
            ))
    second = [
        pltpu.make_async_copy(
            diag.at[wanted_ref[holder(c, -(n + 1), 1, col_count), p]],
            swap_ref.at[n, p],
            swap_sems.at[n, p],
        )
        for n in range(swap_ref.shape[0]) for p in range(swap_ref.shape[1])
    ]
    for copy in first + second:
        copy.start()
    backs = [
        pltpu.make_async_copy(near_ref.at[dk], outs[dk], out_sems.at[dk]) for dk in range(CORES)
    ]
    backs.append(pltpu.make_async_copy(swap_ref, swap_out, out_sems.at[CORES]))
    for copy in first:
        copy.wait()
    for back in backs[:-1]:
        back.start()
    for copy in second:
        copy.wait()
    backs[-1].start()
    for back in backs:
        back.wait()


def far_gather_kernel(wanted_ref, diag, swapped, *rest):
    outs, (near_ref, sems, out_sems) = rest[:-3], rest[-3:]
    c = lax.axis_index("col")
    count = swapped.shape[1]
    backs = []
    copies = []
    for n, out in enumerate(outs):
        target = holder(c, -(n + 1), 0, wanted_ref.shape[0])
        mine = [
            pltpu.make_async_copy(
                diag.at[wanted_ref[target, p]], near_ref.at[n, p], sems.at[n, p]
            )
            for p in range(count)
        ]
        mine.append(pltpu.make_async_copy(
            swapped.at[n], near_ref.at[n, pl.ds(count, count)], sems.at[n, count]
        ))
        for copy in mine:
            copy.start()
        copies.append(mine)
        backs.append(pltpu.make_async_copy(near_ref.at[n], out, out_sems.at[n]))
    for mine, back in zip(copies, backs):
        for copy in mine:
            copy.wait()
        back.start()
    for back in backs:
        back.wait()


def holder(c, dz, dk, col_count):
    chips = col_count // CORES
    z = lax.rem(c // CORES + dz + chips, chips)
    return z * CORES + lax.rem(c + dk, CORES)


def chip_at(dz, col_count):
    return lax.rem(lax.axis_index("col") // CORES + dz, col_count // CORES)


class Tiles:
    def __init__(self, far_ref, near_ref, sem, back=False, count=CHUNK):
        self.refs = (near_ref, far_ref) if back else (far_ref, near_ref)
        self.sem = sem
        self.count = count

    def copy(self, i):
        part = pl.ds(i * self.count, self.count)
        source, target = (ref.at[part] for ref in self.refs)
        return pltpu.make_async_copy(source, target, self.sem.at[i])

    def start(self, i):
        self.copy(i).start()

    def wait(self, i):
        self.copy(i).wait()


def start_all(arrays, chunks):
    for i in range(chunks):
        for array in arrays:
            array.start(i)


def each_slot(chunks, arrays, outs, slot_step):
    def step(i, carry):
        for array in arrays:
            array.wait(i)
        for s in range(CHUNK):
            slot_step(i * CHUNK + s)
        for out in outs:
            out.start(i)
        return carry

    lax.fori_loop(0, chunks, step, 0)
    for i in range(chunks):
        for out in outs:
            out.wait(i)


def covariance_kernel(
    far, col_count, rows_ref, lists_ref, owned_ref, far_slices, features, far_out,
    slices_ref, right_ref, out_ref, slice_sem, right_sem, out_sem,
):
    owners = rows_ref.shape[0]
    columns = owned_ref.shape[1]
    group = slices_ref.shape[1]
    _, samples, size = features.shape
    slots = [chip_at(dz, col_count) * CHUNK + s for dz in far for s in range(CHUNK)]

    def halves(source, target, sem):
        count = source.shape[0] // 2
        parts = [pl.ds(i * count, count) for i in range(2)]
        return [
            pltpu.make_async_copy(source.at[part], target.at[part], sem.at[i])
            for i, part in enumerate(parts)
        ]

    def out_copy(owner):
        return pltpu.make_async_copy(out_ref.at[owner], far_out.at[owner], out_sem.at[owner])

    copies = halves(far_slices, slices_ref, slice_sem) + halves(features, right_ref, right_sem)
    for copy in copies:
        copy.start()
    for copy in copies:
        copy.wait()

    def owner_step(owner, carry):
        left = jnp.concatenate(
            [slices_ref[rows_ref[owner, slot]].astype(F32) for slot in slots], axis=0
        ).astype(BF)
        right = jnp.concatenate(
            [right_ref[owned_ref[owner, a]] for a in range(columns)], axis=1
        )
        both = dot(left, right) * (1.0 / samples)
        for k, slot in enumerate(slots):
            rows = both[k * group:(k + 1) * group]
            out_ref[owner, k] = jnp.where(
                lists_ref[owner, slot] == 0, rows[:, :size], rows[:, size:]
            )
        out_copy(owner).start()
        return carry

    lax.fori_loop(0, owners, owner_step, 0, unroll=8)
    for owner in range(owners):
        out_copy(owner).wait()


def pair(x):
    size = x.shape[0]
    high = x[:, :size]
    return jnp.concatenate(
        [x, jnp.concatenate([high, jnp.zeros_like(high)], axis=1)], axis=0
    )


def add_products(slots, ds, tiles, list_ref, sums_ref):
    lefts = [jnp.concatenate(split(d.T), axis=1) for d in ds]
    products = [dot(left, pair(tile)) for left, tile in zip(lefts, tiles)]
    for slot, product in zip(slots, products):
        sums_ref[list_ref[slot]] += product


def write_sums(sums_ref, out_ref):
    pieces, columns, group, size = out_ref.shape
    for a in range(columns):
        total = sums_ref[a][:, :size] + sums_ref[a][:, size:]
        out_ref[:, a] = total.reshape(pieces, group, size)


def first_steps(
    slots, covariances, list_ref, live_ref, theta_ref, tiles_ref, base_ref, d_ref, sums_ref
):
    ds = []
    tiles = []
    for slot, covariance in zip(slots, covariances):
        theta = theta_ref[slot]
        tile = tiles_ref[slot]
        base = theta - STEP * (covariance - tile)
        base_ref[slot] = base
        ds.append(jnp.where(slot < live_ref[0], shrink(base) - theta, 0.0))
        tiles.append(jnp.concatenate(split(tile), axis=1))
    for slot, d in zip(slots, ds):
        d_ref[slot] = d
    add_products(slots, ds, tiles, list_ref, sums_ref)


def near_kernel(near, col_count, list_ref, live_ref, owned_ref, features, far_theta, far_tiles, *rest):
    count = len(near) * CORES
    blocks = rest[:count]
    (
        far_base, far_d, sums_ref, left_ref, right_ref, theta_ref, tiles_ref, base_ref, d_ref,
        left_sem, right_sem, sems,
    ) = rest[count:]
    slots, size, _ = theta_ref.shape
    samples = features.shape[1]
    per_source = CHUNK // CORES
    core = lax.rem(lax.axis_index("col"), CORES)
    arrays = [Tiles(far_theta, theta_ref, sems.at[0]), Tiles(far_tiles, tiles_ref, sems.at[1])]
    outs = [Tiles(far_base, base_ref, sems.at[2], True), Tiles(far_d, d_ref, sems.at[3], True)]

    def left_copy(n):
        place = n // CORES * CHUNK + lax.rem(core + n % CORES, CORES) * per_source
        return pltpu.make_async_copy(
            blocks[n].at[:, pl.ds(0, samples)], left_ref.at[pl.ds(place, per_source)],
            left_sem.at[n],
        )

    def right_copy(a):
        return pltpu.make_async_copy(
            features.at[owned_ref[a]], right_ref.at[a], right_sem.at[a]
        )

    for a in range(right_ref.shape[0]):
        right_copy(a).start()
    for n in range(count):
        left_copy(n).start()
    for dz in near:
        for array in arrays:
            array.start(chip_at(dz, col_count))
    sums_ref[...] = jnp.zeros_like(sums_ref)
    for a in range(right_ref.shape[0]):
        right_copy(a).wait()
    for n in range(count):
        left_copy(n).wait()
    for n, dz in enumerate(near):
        chip = chip_at(dz, col_count)
        for array in arrays:
            array.wait(chip)
        slots_here = [chip * CHUNK + s for s in range(CHUNK)]
        covariances = [
            lax.dot_general(
                left_ref[n * CHUNK + s], right_ref[list_ref[slot]],
                (((0,), (0,)), ((), ())), preferred_element_type=F32,
            ) * (1.0 / samples)
            for s, slot in enumerate(slots_here)
        ]
        first_steps(
            slots_here, covariances, list_ref, live_ref, theta_ref, tiles_ref, base_ref, d_ref,
            sums_ref,
        )
        for out in outs:
            out.start(chip)
    for dz in near:
        for out in outs:
            out.wait(chip_at(dz, col_count))


def first_kernel(
    far, col_count, list_ref, live_ref, cov_ref, near_sums, far_theta, far_tiles, in_base, in_d,
    far_base, far_d, out_ref, theta_ref, tiles_ref, base_ref, d_ref, sums_ref, sum_sem, sems,
):
    slots, size, _ = theta_ref.shape
    arrays = [Tiles(far_theta, theta_ref, sems.at[0]), Tiles(far_tiles, tiles_ref, sems.at[1])]
    outs = [Tiles(far_base, base_ref, sems.at[2], True), Tiles(far_d, d_ref, sems.at[3], True)]
    bring = pltpu.make_async_copy(near_sums, sums_ref, sum_sem.at[0])
    bring.start()
    for dz in far:
        for array in arrays:
            array.start(chip_at(dz, col_count))
    bring.wait()
    for begin in range(0, len(far), 4):
        part = range(begin, min(begin + 4, len(far)))
        chips = [chip_at(far[n], col_count) for n in part]
        for chip in chips:
            for array in arrays:
                array.wait(chip)
        first_steps(
            [chip * CHUNK + s for chip in chips for s in range(CHUNK)],
            [
                cov_ref[:, n * CHUNK + s].reshape(size, size)
                for n in part for s in range(CHUNK)
            ],
            list_ref, live_ref, theta_ref, tiles_ref, base_ref, d_ref, sums_ref,
        )
        for chip in chips:
            for out in outs:
                out.start(chip)
    write_sums(sums_ref, out_ref)
    for dz in far:
        for out in outs:
            out.wait(chip_at(dz, col_count))


def diagonal_kernel(half, list_ref, far_base, far_d, col_diag_ref, *rest):
    far_out, base_ref, d_ref, diag_ref, out_ref, diag_sem, sems = rest[-7:]
    chips = diag_sem.shape[0] // CORES
    near, far_diag = rest[:CORES], rest[CORES:CORES + chips - 1]
    slots, size, _ = d_ref.shape
    chunks = slots // MANY
    mine = range(half * chunks // 2, (half + 1) * chunks // 2)
    c = lax.axis_index("col")
    per_source = CHUNK // CORES
    arrays = [
        Tiles(far_d, d_ref, sems.at[1], count=MANY),
        Tiles(far_base, base_ref, sems.at[0], count=MANY),
    ]
    out = Tiles(far_out, out_ref, sems.at[2], True, count=MANY)

    def with_diag(n, use):
        dz, dk = n // CORES, n % CORES
        if dz == 0:
            source = near[dk].at[:, pl.ds(near[dk].shape[1] - size, size)]
        else:
            source = far_diag[dz - 1].at[pl.ds(dk * per_source, per_source)]
        place = holder(c, dz, dk, chips * CORES) * per_source

        @pl.when(place // (slots // 2) == half)
        def _():
            use(pltpu.make_async_copy(
                source, diag_ref.at[pl.ds(place, per_source)], diag_sem.at[n]
            ))

    for n in range(chips * CORES):
        with_diag(n, lambda copy: copy.start())
    for i in mine:
        for array in arrays:
            array.start(i)
    for n in range(chips * CORES):
        with_diag(n, lambda copy: copy.wait())
    for i in mine:
        for array in arrays:
            array.wait(i)
        slots_here = [i * MANY + s for s in range(MANY)]
        halves = [
            dot(diag_ref[slot], jnp.concatenate(split(d_ref[slot]), axis=1))
            for slot in slots_here
        ]
        for slot, x in zip(slots_here, halves):
            left = jnp.concatenate(split(x[:, :size] + x[:, size:]), axis=1)
            right = col_diag_ref[list_ref[slot]]
            both = dot(left, jnp.concatenate([right, right], axis=0))
            out_ref[slot] = base_ref[slot] + d_ref[slot] - STEP * both
        out.start(i)
    for i in mine:
        out.wait(i)


def sum_kernel(same_ref, in_ref, out_ref):
    same = same_ref[...].astype(BF)
    for g in range(in_ref.shape[1]):
        x = in_ref[:, g, :]
        x1, rest = x.astype(BF), x
        rest = rest - x1.astype(F32)
        x2 = rest.astype(BF)
        rest = rest - x2.astype(F32)
        x3 = rest.astype(BF)
        out_ref[:, g, :] = dot(
            jnp.concatenate([same, same, same], axis=1), jnp.concatenate([x1, x2, x3], axis=0)
        )


def sweep_kernel(
    last, list_ref, live_ref, far_t, far_theta, far_pairs, q_ref, far_d, *rest
):
    if last:
        t_ref, theta_ref, pairs_ref, d_ref, right_ref, sems = rest
    else:
        out_ref, t_ref, theta_ref, pairs_ref, d_ref, right_ref, sems, sums_ref = rest
    slots, size, _ = theta_ref.shape
    chunks = slots // MANY
    arrays = [
        Tiles(far_pairs, pairs_ref, sems.at[0], count=MANY),
        Tiles(far_t, t_ref, sems.at[1], count=MANY),
        Tiles(far_theta, theta_ref, sems.at[2], count=MANY),
    ]
    out = Tiles(far_d, d_ref, sems.at[3], True, count=MANY)
    start_all(arrays, chunks)
    for a in range(q_ref.shape[1]):
        q = q_ref[:, a].reshape(size, size)
        right_ref[a] = pair(jnp.concatenate(split(q), axis=1))
    if not last:
        sums_ref[...] = jnp.zeros_like(sums_ref)

    def step(i, carry):
        for array in arrays:
            array.wait(i)
        slots_here = [i * MANY + s for s in range(MANY)]
        both = [dot(pairs_ref[slot], right_ref[list_ref[slot]]) for slot in slots_here]
        ds = []
        for slot, x in zip(slots_here, both):
            product = x[:, :size] + x[:, size:]
            d = shrink(t_ref[slot] - STEP * product) - theta_ref[slot]
            ds.append(jnp.where(slot < live_ref[0], d, 0.0))
        for slot, d in zip(slots_here, ds):
            d_ref[slot] = d
        if not last:
            tiles = [pairs_ref[slot] for slot in slots_here]
            add_products(slots_here, ds, tiles, list_ref, sums_ref)
        out.start(i)
        return carry

    lax.fori_loop(0, chunks, step, 0)
    if not last:
        write_sums(sums_ref, out_ref)
    for i in range(chunks):
        out.wait(i)


def shape(dims, dtype):
    return jax.ShapeDtypeStruct(dims, dtype)


def far(x):
    return pltpu.with_memory_space_constraint(x, pltpu.HBM)


def slot_blocks(*dims):
    return pl.BlockSpec((PER_STEP,) + dims, lambda i: (i,) + (0,) * len(dims))


def body(
    features,
    diag_inverse,
    precision_tiles,
    inverse_tiles,
    slot_rows,
    slot_columns,
    owned_columns,
    live_counts,
):
    row_count = lax.axis_size("row")
    col_count = lax.axis_size("col")
    r = lax.axis_index("row")
    c = lax.axis_index("col")
    blocks, samples, size = features.shape
    slots = precision_tiles.shape[2]
    columns = owned_columns.shape[2]
    per_source = slots // col_count
    group = size // row_count
    theta = precision_tiles[0, 0]
    tiles = inverse_tiles[0, 0]
    tile_shape = (slots, size, size)
    piece_shape = (row_count, columns, group, size)

    with jax.named_scope("slices"):
        mine = pl.pallas_call(
            functools.partial(slice_kernel, group),
            in_specs=[HBM],
            out_specs=VMEM,
            out_shape=shape((blocks, group, samples), BF),
            scratch_shapes=[
                pltpu.VMEM(features.shape, BF), pltpu.SemaphoreType.DMA((4,))
            ],
            compiler_params=PARAMS,
        )(far(features))
        slices = lax.all_gather(mine, "col", axis=0, tiled=True)

    with jax.named_scope("tables"):
        rows_here = lax.dynamic_index_in_dim(slot_rows, c, 1, keepdims=False)
        lists_here = lax.dynamic_index_in_dim(slot_columns, c, 1, keepdims=False)
        owned_here = lax.dynamic_index_in_dim(owned_columns, c, 1, keepdims=False) - c * blocks
        my_list = lax.dynamic_index_in_dim(lists_here, r, 0, keepdims=False)
        live = lax.dynamic_slice(live_counts, (r, c), (1, 1)).reshape(1)
        wanted = lax.dynamic_slice(
            slot_rows, (r, 0, c * per_source), (1, col_count, per_source)
        ).reshape(col_count, per_source) - c * blocks
        flat = owned_here.reshape(-1)
        same = (flat[:, None] == flat[None, :]).astype(F32)
        my_owned = lax.dynamic_index_in_dim(owned_here, r, 0, keepdims=False)
        col_diag = jnp.take(diag_inverse, my_owned, axis=0)

    tile_vmem = pltpu.VMEM(tile_shape, F32)
    tile_out = pltpu.HBM(tile_shape, F32)
    sums = pltpu.VMEM((columns, size, 2 * size), F32)
    chunks = slots // CHUNK

    def sems(*dims):
        return pltpu.SemaphoreType.DMA(dims)

    with jax.named_scope("split"):
        pairs = pl.pallas_call(
            split_kernel,
            grid=(slots // PER_STEP,),
            in_specs=[slot_blocks(size, size)],
            out_specs=slot_blocks(size, 2 * size),
            out_shape=pltpu.HBM((slots, size, 2 * size), BF),
        )(far(tiles))

    with jax.named_scope("blocks"):
        chips = col_count // CORES
        near = [0]
        far_chips = list(range(1, chips))
        near_count = CORES
        near_shape = (per_source, samples + size, size)
        swap_shape = (chips - 1, per_source, size, size)
        far_shape = (CORES * per_source, size, size)
        mine, wanted = lax.optimization_barrier((mine, wanted))
        own, other, swap = pl.pallas_call(
            near_gather_kernel,
            in_specs=[SMEM, HBM, HBM],
            out_specs=[HBM] * 3,
            out_shape=[
                pltpu.HBM(near_shape, BF), pltpu.HBM(near_shape, BF), pltpu.HBM(swap_shape, BF)
            ],
            scratch_shapes=[
                pltpu.VMEM((CORES,) + near_shape, BF),
                pltpu.VMEM(swap_shape, BF),
                sems(CORES, per_source, 2),
                sems(chips - 1, per_source),
                sems(CORES + 1),
            ],
            compiler_params=PARAMS,
        )(wanted, far(features), far(diag_inverse))
        to_other = [
            (i, i // CORES * CORES + (i + 1) % CORES) for i in range(col_count)
        ]
        swapped = lax.ppermute(swap, "col", to_other)
        got_blocks = [own, lax.ppermute(other, "col", to_other)]
        far_out = list(pl.pallas_call(
            far_gather_kernel,
            in_specs=[SMEM, HBM, HBM],
            out_specs=[HBM] * (chips - 1),
            out_shape=[pltpu.HBM(far_shape, BF)] * (chips - 1),
            scratch_shapes=[
                pltpu.VMEM((chips - 1,) + far_shape, BF),
                sems(chips - 1, per_source + 1),
                sems(chips - 1),
            ],
            compiler_params=PARAMS,
        )(wanted, far(diag_inverse), far(swapped)))

        def send(dz):
            return lax.ppermute(far_out[dz - 1], "col", [
                (h, (h // CORES - dz) % chips * CORES + h % CORES) for h in range(col_count)
            ])

        base, d, near_sums = pl.pallas_call(
            functools.partial(near_kernel, near, col_count),
            in_specs=[SMEM, SMEM, SMEM] + [HBM] * (3 + near_count),
            out_specs=[HBM] * 2 + [VMEM],
            out_shape=[tile_out, tile_out, pltpu.HBM((columns, size, 2 * size), F32)],
            scratch_shapes=[
                pltpu.VMEM((len(near) * CHUNK, samples, size), BF),
                pltpu.VMEM((columns, samples, size), BF),
                tile_vmem, tile_vmem, tile_vmem, tile_vmem,
                sems(near_count), sems(columns), sems(4, chunks),
            ],
            compiler_params=PARAMS,
        )(
            my_list, live, my_owned, far(features), far(theta), far(tiles),
            *[far(block) for block in got_blocks[:near_count]],
        )
        slices, pairs, got_blocks, base, d, near_sums, far_out = lax.optimization_barrier(
            (slices, pairs, got_blocks, base, d, near_sums, far_out)
        )

    far_slots = len(far_chips) * CHUNK
    with jax.named_scope("covariance"):
        partial = pl.pallas_call(
            functools.partial(covariance_kernel, far_chips, col_count),
            in_specs=[SMEM, SMEM, SMEM, HBM, HBM],
            out_specs=HBM,
            out_shape=pltpu.HBM((row_count, far_slots, group, size), F32),
            scratch_shapes=[
                pltpu.VMEM(slices.shape, BF),
                pltpu.VMEM(features.shape, BF),
                pltpu.VMEM((row_count, far_slots, group, size), F32),
                sems(2),
                sems(2),
                sems(row_count),
            ],
            compiler_params=PARAMS,
        )(rows_here, lists_here, owned_here, far(slices), far(features))
        covariance = lax.all_to_all(partial, "row", split_axis=0, concat_axis=0, tiled=True)

    with jax.named_scope("diag"):
        far_out, _ = lax.optimization_barrier((far_out, partial[0, 0]))
        soon = [1, chips - 1]
        sent = {dz: send(dz) for dz in soon}
        covariance, sent = lax.optimization_barrier((covariance, sent))
        sent.update({dz: send(dz) for dz in far_chips if dz not in soon})
        got_blocks = got_blocks + [sent[dz] for dz in far_chips]

    with jax.named_scope("first"):
        base, d, pieces = pl.pallas_call(
            functools.partial(first_kernel, far_chips, col_count),
            in_specs=[SMEM, SMEM, VMEM] + [HBM] * 5,
            out_specs=[HBM, HBM, VMEM],
            out_shape=[tile_out, tile_out, shape(piece_shape, F32)],
            scratch_shapes=[
                tile_vmem, tile_vmem, tile_vmem, tile_vmem, sums, sems(1), sems(4, chunks),
            ],
            input_output_aliases={6: 0, 7: 1},
            compiler_params=PARAMS,
        )(
            my_list, live, covariance, far(near_sums), far(theta), far(tiles), far(base), far(d)
        )

    def diagonal(half, base, d, col_diag, before=()):
        operands = [my_list, far(base), far(d), col_diag]
        operands += [far(block) for block in got_blocks] + [far(x) for x in before]
        with jax.named_scope("diagonal"):
            return pl.pallas_call(
                functools.partial(diagonal_kernel, half),
                in_specs=[SMEM, HBM, HBM, VMEM] + [HBM] * (len(operands) - 4),
                out_specs=HBM,
                out_shape=tile_out,
                scratch_shapes=[
                    tile_vmem, tile_vmem, pltpu.VMEM(tile_shape, BF), tile_vmem,
                    sems(col_count), sems(3, slots // MANY),
                ],
                input_output_aliases={len(operands) - 1: 0} if before else {},
                compiler_params=PARAMS,
            )(*operands)

    for sweep in range(1, SWEEPS):
        last = sweep == SWEEPS - 1
        with jax.named_scope("exchange"):
            flat_shape = (row_count * columns, group, size)
            got = lax.all_to_all(pieces, "row", split_axis=0, concat_axis=0, tiled=True)
            t = diagonal(0, base, d, col_diag)
            got, t = lax.optimization_barrier((got, t))
            summed = pl.pallas_call(
                sum_kernel,
                in_specs=[VMEM, VMEM],
                out_specs=VMEM,
                out_shape=shape(flat_shape, F32),
                compiler_params=PARAMS,
            )(same, got.reshape(flat_shape))
            q = lax.all_to_all(
                summed.reshape(piece_shape), "row", split_axis=0, concat_axis=0, tiled=True
            )
            d, t, _ = lax.optimization_barrier((d, t, summed[0]))
            t = diagonal(1, base, d, col_diag, (t,))
        with jax.named_scope("sweep"):
            result = pl.pallas_call(
                functools.partial(sweep_kernel, last),
                in_specs=[SMEM, SMEM, HBM, HBM, HBM, VMEM],
                out_specs=[HBM] if last else [HBM, VMEM],
                out_shape=[tile_out] if last else [tile_out, shape(piece_shape, F32)],
                scratch_shapes=[
                    tile_vmem, tile_vmem, pltpu.VMEM((slots, size, 2 * size), BF), tile_vmem,
                    pltpu.VMEM((columns, 2 * size, 2 * size), BF), sems(4, slots // MANY),
                ] + ([] if last else [sums]),
                compiler_params=PARAMS,
            )(my_list, live, far(t), far(theta), far(pairs), q)
            d = result[0]
            if not last:
                pieces = result[1]
    return d.reshape(precision_tiles.shape)


def solution(mesh):
    return jax.shard_map(
        body,
        mesh=mesh,
        in_specs=(
            P("col", None, None),
            P("col", None, None),
            P("row", "col", None, None, None),
            P("row", "col", None, None, None),
            P(),
            P(),
            P(),
            P(),
        ),
        out_specs=P("row", "col", None, None, None),
        check_vma=False,
    )
```

```python
import functools

import jax
import jax.numpy as jnp
from jax import lax
from jax.experimental import pallas as pl
from jax.experimental.pallas import tpu as pltpu
from jax.sharding import PartitionSpec as P

SWEEPS = 4
STEP = 0.3
LAMBDA = 0.3 * 0.6
PER_STEP = 8
CHUNK = 4
CORES = 2
MANY = 8

BF = jnp.bfloat16
F32 = jnp.float32
VMEM = pl.BlockSpec(memory_space=pltpu.VMEM)
HBM = pl.BlockSpec(memory_space=pltpu.HBM)
SMEM = pl.BlockSpec(memory_space=pltpu.SMEM)
PARAMS = pltpu.CompilerParams(vmem_limit_bytes=20 * 1024 * 1024)


def split(x):
    high = x.astype(BF)
    low = (x - high.astype(F32)).astype(BF)
    return high, low


def dot(a, b):
    return jnp.dot(a, b, preferred_element_type=F32)


def shrink(x):
    return x - jnp.clip(x, -LAMBDA, LAMBDA)


def slice_kernel(group, features, out_ref, near_ref, sems):
    r = lax.axis_index("row")
    blocks, _, variables = features.shape
    parts = sems.shape[0]
    count = blocks // parts

    def copy(i):
        part = pl.ds(i * count, count)
        return pltpu.make_async_copy(features.at[part], near_ref.at[part], sems.at[i])

    for i in range(parts):
        copy(i).start()
    wanted = lax.broadcasted_iota(jnp.int32, (group, variables), 0) + r * group
    pick = (lax.broadcasted_iota(jnp.int32, (group, variables), 1) == wanted).astype(BF)

    def step(i, carry):
        copy(i).wait()
        for b in range(count):
            rows = lax.dot_general(
                pick, near_ref[i * count + b], (((1,), (1,)), ((), ())),
                preferred_element_type=F32,
            )
            out_ref[i * count + b] = rows.astype(BF)
        return carry

    lax.fori_loop(0, parts, step, 0)


def split_kernel(tiles_ref, out_ref):
    for s in range(tiles_ref.shape[0]):
        out_ref[s] = jnp.concatenate(split(tiles_ref[s]), axis=1)


def near_gather_kernel(wanted_ref, features, diag, own_out, other_out, swap_out, near_ref, swap_ref, sems, swap_sems, out_sems):
    c = lax.axis_index("col")
    col_count = wanted_ref.shape[0]
    samples = features.shape[1]
    size = diag.shape[1]
    outs = (own_out, other_out)
    first = []
    for dk in range(CORES):
        target = holder(c, 0, dk, col_count)
        for p in range(own_out.shape[0]):
            block = wanted_ref[target, p]
            first.append(pltpu.make_async_copy(
                features.at[block], near_ref.at[dk, p, pl.ds(0, samples)], sems.at[dk, p, 0]
            ))
            first.append(pltpu.make_async_copy(
                diag.at[block], near_ref.at[dk, p, pl.ds(samples, size)], sems.at[dk, p, 1]
            ))
    second = [
        pltpu.make_async_copy(
            diag.at[wanted_ref[holder(c, -(n + 1), 1, col_count), p]],
            swap_ref.at[n, p],
            swap_sems.at[n, p],
        )
        for n in range(swap_ref.shape[0]) for p in range(swap_ref.shape[1])
    ]
    for copy in first + second:
        copy.start()
    backs = [
        pltpu.make_async_copy(near_ref.at[dk], outs[dk], out_sems.at[dk]) for dk in range(CORES)
    ]
    backs.append(pltpu.make_async_copy(swap_ref, swap_out, out_sems.at[CORES]))
    for copy in first:
        copy.wait()
    for back in backs[:-1]:
        back.start()
    for copy in second:
        copy.wait()
    backs[-1].start()
    for back in backs:
        back.wait()


def far_gather_kernel(wanted_ref, diag, swapped, *rest):
    outs, (near_ref, sems, out_sems) = rest[:-3], rest[-3:]
    c = lax.axis_index("col")
    count = swapped.shape[1]
    backs = []
    copies = []
    for n, out in enumerate(outs):
        target = holder(c, -(n + 1), 0, wanted_ref.shape[0])
        mine = [
            pltpu.make_async_copy(
                diag.at[wanted_ref[target, p]], near_ref.at[n, p], sems.at[n, p]
            )
            for p in range(count)
        ]
        mine.append(pltpu.make_async_copy(
            swapped.at[n], near_ref.at[n, pl.ds(count, count)], sems.at[n, count]
        ))
        for copy in mine:
            copy.start()
        copies.append(mine)
        backs.append(pltpu.make_async_copy(near_ref.at[n], out, out_sems.at[n]))
    for mine, back in zip(copies, backs):
        for copy in mine:
            copy.wait()
        back.start()
    for back in backs:
        back.wait()


def holder(c, dz, dk, col_count):
    chips = col_count // CORES
    z = lax.rem(c // CORES + dz + chips, chips)
    return z * CORES + lax.rem(c + dk, CORES)


def chip_at(dz, col_count):
    return lax.rem(lax.axis_index("col") // CORES + dz, col_count // CORES)


class Tiles:
    def __init__(self, far_ref, near_ref, sem, back=False, count=CHUNK):
        self.refs = (near_ref, far_ref) if back else (far_ref, near_ref)
        self.sem = sem
        self.count = count

    def copy(self, i):
        part = pl.ds(i * self.count, self.count)
        source, target = (ref.at[part] for ref in self.refs)
        return pltpu.make_async_copy(source, target, self.sem.at[i])

    def start(self, i):
        self.copy(i).start()

    def wait(self, i):
        self.copy(i).wait()


def start_all(arrays, chunks):
    for i in range(chunks):
        for array in arrays:
            array.start(i)


def each_slot(chunks, arrays, outs, slot_step):
    def step(i, carry):
        for array in arrays:
            array.wait(i)
        for s in range(CHUNK):
            slot_step(i * CHUNK + s)
        for out in outs:
            out.start(i)
        return carry

    lax.fori_loop(0, chunks, step, 0)
    for i in range(chunks):
        for out in outs:
            out.wait(i)


def covariance_kernel(
    far, col_count, rows_ref, lists_ref, owned_ref, far_slices, features, far_out,
    slices_ref, right_ref, out_ref, slice_sem, right_sem, out_sem,
):
    owners = rows_ref.shape[0]
    columns = owned_ref.shape[1]
    group = slices_ref.shape[1]
    _, samples, size = features.shape
    slots = [chip_at(dz, col_count) * CHUNK + s for dz in far for s in range(CHUNK)]

    def halves(source, target, sem):
        count = source.shape[0] // 2
        parts = [pl.ds(i * count, count) for i in range(2)]
        return [
            pltpu.make_async_copy(source.at[part], target.at[part], sem.at[i])
            for i, part in enumerate(parts)
        ]

    def out_copy(owner):
        return pltpu.make_async_copy(out_ref.at[owner], far_out.at[owner], out_sem.at[owner])

    copies = halves(far_slices, slices_ref, slice_sem) + halves(features, right_ref, right_sem)
    for copy in copies:
        copy.start()
    for copy in copies:
        copy.wait()

    def owner_step(owner, carry):
        left = jnp.concatenate(
            [slices_ref[rows_ref[owner, slot]].astype(F32) for slot in slots], axis=0
        ).astype(BF)
        right = jnp.concatenate(
            [right_ref[owned_ref[owner, a]] for a in range(columns)], axis=1
        )
        both = dot(left, right) * (1.0 / samples)
        for k, slot in enumerate(slots):
            rows = both[k * group:(k + 1) * group]
            out_ref[owner, k] = jnp.where(
                lists_ref[owner, slot] == 0, rows[:, :size], rows[:, size:]
            )
        out_copy(owner).start()
        return carry

    lax.fori_loop(0, owners, owner_step, 0, unroll=4)
    for owner in range(owners):
        out_copy(owner).wait()


def pair(x):
    size = x.shape[0]
    high = x[:, :size]
    return jnp.concatenate(
        [x, jnp.concatenate([high, jnp.zeros_like(high)], axis=1)], axis=0
    )


def add_products(slots, ds, tiles, list_ref, sums_ref):
    lefts = [jnp.concatenate(split(d.T), axis=1) for d in ds]
    products = [dot(left, pair(tile)) for left, tile in zip(lefts, tiles)]
    for slot, product in zip(slots, products):
        sums_ref[list_ref[slot]] += product


def write_sums(sums_ref, out_ref):
    pieces, columns, group, size = out_ref.shape
    for a in range(columns):
        total = sums_ref[a][:, :size] + sums_ref[a][:, size:]
        out_ref[:, a] = total.reshape(pieces, group, size)


def first_steps(
    slots, covariances, list_ref, live_ref, theta_ref, tiles_ref, base_ref, d_ref, sums_ref
):
    ds = []
    tiles = []
    for slot, covariance in zip(slots, covariances):
        theta = theta_ref[slot]
        tile = tiles_ref[slot]
        base = theta - STEP * (covariance - tile)
        base_ref[slot] = base
        ds.append(jnp.where(slot < live_ref[0], shrink(base) - theta, 0.0))
        tiles.append(jnp.concatenate(split(tile), axis=1))
    for slot, d in zip(slots, ds):
        d_ref[slot] = d
    add_products(slots, ds, tiles, list_ref, sums_ref)


def near_kernel(near, col_count, list_ref, live_ref, owned_ref, features, far_theta, far_tiles, *rest):
    count = len(near) * CORES
    blocks = rest[:count]
    (
        far_base, far_d, sums_ref, left_ref, right_ref, theta_ref, tiles_ref, base_ref, d_ref,
        left_sem, right_sem, sems,
    ) = rest[count:]
    slots, size, _ = theta_ref.shape
    samples = features.shape[1]
    per_source = CHUNK // CORES
    core = lax.rem(lax.axis_index("col"), CORES)
    arrays = [Tiles(far_theta, theta_ref, sems.at[0]), Tiles(far_tiles, tiles_ref, sems.at[1])]
    outs = [Tiles(far_base, base_ref, sems.at[2], True), Tiles(far_d, d_ref, sems.at[3], True)]

    def left_copy(n):
        place = n // CORES * CHUNK + lax.rem(core + n % CORES, CORES) * per_source
        return pltpu.make_async_copy(
            blocks[n].at[:, pl.ds(0, samples)], left_ref.at[pl.ds(place, per_source)],
            left_sem.at[n],
        )

    def right_copy(a):
        return pltpu.make_async_copy(
            features.at[owned_ref[a]], right_ref.at[a], right_sem.at[a]
        )

    for a in range(right_ref.shape[0]):
        right_copy(a).start()
    for n in range(count):
        left_copy(n).start()
    for dz in near:
        for array in arrays:
            array.start(chip_at(dz, col_count))
    sums_ref[...] = jnp.zeros_like(sums_ref)
    for a in range(right_ref.shape[0]):
        right_copy(a).wait()
    for n in range(count):
        left_copy(n).wait()
    for n, dz in enumerate(near):
        chip = chip_at(dz, col_count)
        for array in arrays:
            array.wait(chip)
        slots_here = [chip * CHUNK + s for s in range(CHUNK)]
        covariances = [
            lax.dot_general(
                left_ref[n * CHUNK + s], right_ref[list_ref[slot]],
                (((0,), (0,)), ((), ())), preferred_element_type=F32,
            ) * (1.0 / samples)
            for s, slot in enumerate(slots_here)
        ]
        first_steps(
            slots_here, covariances, list_ref, live_ref, theta_ref, tiles_ref, base_ref, d_ref,
            sums_ref,
        )
        for out in outs:
            out.start(chip)
    for dz in near:
        for out in outs:
            out.wait(chip_at(dz, col_count))


def first_kernel(
    far, col_count, list_ref, live_ref, cov_ref, near_sums, far_theta, far_tiles, in_base, in_d,
    far_base, far_d, out_ref, theta_ref, tiles_ref, base_ref, d_ref, sums_ref, sum_sem, sems,
):
    slots, size, _ = theta_ref.shape
    arrays = [Tiles(far_theta, theta_ref, sems.at[0]), Tiles(far_tiles, tiles_ref, sems.at[1])]
    outs = [Tiles(far_base, base_ref, sems.at[2], True), Tiles(far_d, d_ref, sems.at[3], True)]
    bring = pltpu.make_async_copy(near_sums, sums_ref, sum_sem.at[0])
    bring.start()
    for dz in far:
        for array in arrays:
            array.start(chip_at(dz, col_count))
    bring.wait()
    for begin in range(0, len(far), 2):
        part = range(begin, min(begin + 2, len(far)))
        chips = [chip_at(far[n], col_count) for n in part]
        for chip in chips:
            for array in arrays:
                array.wait(chip)
        first_steps(
            [chip * CHUNK + s for chip in chips for s in range(CHUNK)],
            [
                cov_ref[:, n * CHUNK + s].reshape(size, size)
                for n in part for s in range(CHUNK)
            ],
            list_ref, live_ref, theta_ref, tiles_ref, base_ref, d_ref, sums_ref,
        )
        for chip in chips:
            for out in outs:
                out.start(chip)
    write_sums(sums_ref, out_ref)
    for dz in far:
        for out in outs:
            out.wait(chip_at(dz, col_count))


def diagonal_kernel(half, list_ref, far_base, far_d, col_diag_ref, *rest):
    far_out, base_ref, d_ref, diag_ref, out_ref, diag_sem, sems = rest[-7:]
    chips = diag_sem.shape[0] // CORES
    near, far_diag = rest[:CORES], rest[CORES:CORES + chips - 1]
    slots, size, _ = d_ref.shape
    chunks = slots // MANY
    mine = range(half * chunks // 2, (half + 1) * chunks // 2)
    c = lax.axis_index("col")
    per_source = CHUNK // CORES
    arrays = [
        Tiles(far_d, d_ref, sems.at[1], count=MANY),
        Tiles(far_base, base_ref, sems.at[0], count=MANY),
    ]
    out = Tiles(far_out, out_ref, sems.at[2], True, count=MANY)

    def with_diag(n, use):
        dz, dk = n // CORES, n % CORES
        if dz == 0:
            source = near[dk].at[:, pl.ds(near[dk].shape[1] - size, size)]
        else:
            source = far_diag[dz - 1].at[pl.ds(dk * per_source, per_source)]
        place = holder(c, dz, dk, chips * CORES) * per_source

        @pl.when(place // (slots // 2) == half)
        def _():
            use(pltpu.make_async_copy(
                source, diag_ref.at[pl.ds(place, per_source)], diag_sem.at[n]
            ))

    for n in range(chips * CORES):
        with_diag(n, lambda copy: copy.start())
    for i in mine:
        for array in arrays:
            array.start(i)
    for n in range(chips * CORES):
        with_diag(n, lambda copy: copy.wait())
    for i in mine:
        for array in arrays:
            array.wait(i)
        slots_here = [i * MANY + s for s in range(MANY)]
        halves = [
            dot(diag_ref[slot], jnp.concatenate(split(d_ref[slot]), axis=1))
            for slot in slots_here
        ]
        for slot, x in zip(slots_here, halves):
            left = jnp.concatenate(split(x[:, :size] + x[:, size:]), axis=1)
            right = col_diag_ref[list_ref[slot]]
            both = dot(left, jnp.concatenate([right, right], axis=0))
            out_ref[slot] = base_ref[slot] + d_ref[slot] - STEP * both
        out.start(i)
    for i in mine:
        out.wait(i)


def sum_kernel(same_ref, in_ref, out_ref):
    same = same_ref[...].astype(BF)
    for g in range(in_ref.shape[1]):
        x = in_ref[:, g, :]
        x1, rest = x.astype(BF), x
        rest = rest - x1.astype(F32)
        x2 = rest.astype(BF)
        rest = rest - x2.astype(F32)
        x3 = rest.astype(BF)
        out_ref[:, g, :] = dot(
            jnp.concatenate([same, same, same], axis=1), jnp.concatenate([x1, x2, x3], axis=0)
        )


def sweep_kernel(
    last, list_ref, live_ref, far_t, far_theta, far_pairs, q_ref, far_d, *rest
):
    if last:
        t_ref, theta_ref, pairs_ref, d_ref, right_ref, sems = rest
    else:
        out_ref, t_ref, theta_ref, pairs_ref, d_ref, right_ref, sems, sums_ref = rest
    slots, size, _ = theta_ref.shape
    chunks = slots // MANY
    arrays = [
        Tiles(far_pairs, pairs_ref, sems.at[0], count=MANY),
        Tiles(far_t, t_ref, sems.at[1], count=MANY),
        Tiles(far_theta, theta_ref, sems.at[2], count=MANY),
    ]
    out = Tiles(far_d, d_ref, sems.at[3], True, count=MANY)
    start_all(arrays, chunks)
    for a in range(q_ref.shape[1]):
        q = q_ref[:, a].reshape(size, size)
        right_ref[a] = pair(jnp.concatenate(split(q), axis=1))
    if not last:
        sums_ref[...] = jnp.zeros_like(sums_ref)

    def step(i, carry):
        for array in arrays:
            array.wait(i)
        slots_here = [i * MANY + s for s in range(MANY)]
        both = [dot(pairs_ref[slot], right_ref[list_ref[slot]]) for slot in slots_here]
        ds = []
        for slot, x in zip(slots_here, both):
            product = x[:, :size] + x[:, size:]
            d = shrink(t_ref[slot] - STEP * product) - theta_ref[slot]
            ds.append(jnp.where(slot < live_ref[0], d, 0.0))
        for slot, d in zip(slots_here, ds):
            d_ref[slot] = d
        if not last:
            tiles = [pairs_ref[slot] for slot in slots_here]
            add_products(slots_here, ds, tiles, list_ref, sums_ref)
        out.start(i)
        return carry

    lax.fori_loop(0, chunks, step, 0)
    if not last:
        write_sums(sums_ref, out_ref)
    for i in range(chunks):
        out.wait(i)


def shape(dims, dtype):
    return jax.ShapeDtypeStruct(dims, dtype)


def far(x):
    return pltpu.with_memory_space_constraint(x, pltpu.HBM)


def slot_blocks(*dims):
    return pl.BlockSpec((PER_STEP,) + dims, lambda i: (i,) + (0,) * len(dims))


def body(
    features,
    diag_inverse,
    precision_tiles,
    inverse_tiles,
    slot_rows,
    slot_columns,
    owned_columns,
    live_counts,
):
    row_count = lax.axis_size("row")
    col_count = lax.axis_size("col")
    r = lax.axis_index("row")
    c = lax.axis_index("col")
    blocks, samples, size = features.shape
    slots = precision_tiles.shape[2]
    columns = owned_columns.shape[2]
    per_source = slots // col_count
    group = size // row_count
    theta = precision_tiles[0, 0]
    tiles = inverse_tiles[0, 0]
    tile_shape = (slots, size, size)
    piece_shape = (row_count, columns, group, size)

    with jax.named_scope("slices"):
        mine = pl.pallas_call(
            functools.partial(slice_kernel, group),
            in_specs=[HBM],
            out_specs=VMEM,
            out_shape=shape((blocks, group, samples), BF),
            scratch_shapes=[
                pltpu.VMEM(features.shape, BF), pltpu.SemaphoreType.DMA((2,))
            ],
            compiler_params=PARAMS,
        )(far(features))
        slices = lax.all_gather(mine, "col", axis=0, tiled=True)

    with jax.named_scope("tables"):
        rows_here = lax.dynamic_index_in_dim(slot_rows, c, 1, keepdims=False)
        lists_here = lax.dynamic_index_in_dim(slot_columns, c, 1, keepdims=False)
        owned_here = lax.dynamic_index_in_dim(owned_columns, c, 1, keepdims=False) - c * blocks
        my_list = lax.dynamic_index_in_dim(lists_here, r, 0, keepdims=False)
        live = lax.dynamic_slice(live_counts, (r, c), (1, 1)).reshape(1)
        wanted = lax.dynamic_slice(
            slot_rows, (r, 0, c * per_source), (1, col_count, per_source)
        ).reshape(col_count, per_source) - c * blocks
        flat = owned_here.reshape(-1)
        same = (flat[:, None] == flat[None, :]).astype(F32)
        my_owned = lax.dynamic_index_in_dim(owned_here, r, 0, keepdims=False)
        col_diag = jnp.take(diag_inverse, my_owned, axis=0)

    tile_vmem = pltpu.VMEM(tile_shape, F32)
    tile_out = pltpu.HBM(tile_shape, F32)
    sums = pltpu.VMEM((columns, size, 2 * size), F32)
    chunks = slots // CHUNK

    def sems(*dims):
        return pltpu.SemaphoreType.DMA(dims)

    with jax.named_scope("split"):
        pairs = pl.pallas_call(
            split_kernel,
            grid=(slots // PER_STEP,),
            in_specs=[slot_blocks(size, size)],
            out_specs=slot_blocks(size, 2 * size),
            out_shape=pltpu.HBM((slots, size, 2 * size), BF),
        )(far(tiles))

    with jax.named_scope("blocks"):
        chips = col_count // CORES
        near = [0]
        far_chips = list(range(1, chips))
        near_count = CORES
        near_shape = (per_source, samples + size, size)
        swap_shape = (chips - 1, per_source, size, size)
        far_shape = (CORES * per_source, size, size)
        mine, wanted = lax.optimization_barrier((mine, wanted))
        own, other, swap = pl.pallas_call(
            near_gather_kernel,
            in_specs=[SMEM, HBM, HBM],
            out_specs=[HBM] * 3,
            out_shape=[
                pltpu.HBM(near_shape, BF), pltpu.HBM(near_shape, BF), pltpu.HBM(swap_shape, BF)
            ],
            scratch_shapes=[
                pltpu.VMEM((CORES,) + near_shape, BF),
                pltpu.VMEM(swap_shape, BF),
                sems(CORES, per_source, 2),
                sems(chips - 1, per_source),
                sems(CORES + 1),
            ],
            compiler_params=PARAMS,
        )(wanted, far(features), far(diag_inverse))
        to_other = [
            (i, i // CORES * CORES + (i + 1) % CORES) for i in range(col_count)
        ]
        swapped = lax.ppermute(swap, "col", to_other)
        got_blocks = [own, lax.ppermute(other, "col", to_other)]
        far_out = list(pl.pallas_call(
            far_gather_kernel,
            in_specs=[SMEM, HBM, HBM],
            out_specs=[HBM] * (chips - 1),
            out_shape=[pltpu.HBM(far_shape, BF)] * (chips - 1),
            scratch_shapes=[
                pltpu.VMEM((chips - 1,) + far_shape, BF),
                sems(chips - 1, per_source + 1),
                sems(chips - 1),
            ],
            compiler_params=PARAMS,
        )(wanted, far(diag_inverse), far(swapped)))

        def send(dz):
            return lax.ppermute(far_out[dz - 1], "col", [
                (h, (h // CORES - dz) % chips * CORES + h % CORES) for h in range(col_count)
            ])

        base, d, near_sums = pl.pallas_call(
            functools.partial(near_kernel, near, col_count),
            in_specs=[SMEM, SMEM, SMEM] + [HBM] * (3 + near_count),
            out_specs=[HBM] * 2 + [VMEM],
            out_shape=[tile_out, tile_out, pltpu.HBM((columns, size, 2 * size), F32)],
            scratch_shapes=[
                pltpu.VMEM((len(near) * CHUNK, samples, size), BF),
                pltpu.VMEM((columns, samples, size), BF),
                tile_vmem, tile_vmem, tile_vmem, tile_vmem,
                sems(near_count), sems(columns), sems(4, chunks),
            ],
            compiler_params=PARAMS,
        )(
            my_list, live, my_owned, far(features), far(theta), far(tiles),
            *[far(block) for block in got_blocks[:near_count]],
        )
        slices, pairs, got_blocks, base, d, near_sums, far_out = lax.optimization_barrier(
            (slices, pairs, got_blocks, base, d, near_sums, far_out)
        )

    far_slots = len(far_chips) * CHUNK
    with jax.named_scope("covariance"):
        partial = pl.pallas_call(
            functools.partial(covariance_kernel, far_chips, col_count),
            in_specs=[SMEM, SMEM, SMEM, HBM, HBM],
            out_specs=HBM,
            out_shape=pltpu.HBM((row_count, far_slots, group, size), F32),
            scratch_shapes=[
                pltpu.VMEM(slices.shape, BF),
                pltpu.VMEM(features.shape, BF),
                pltpu.VMEM((row_count, far_slots, group, size), F32),
                sems(2),
                sems(2),
                sems(row_count),
            ],
            compiler_params=PARAMS,
        )(rows_here, lists_here, owned_here, far(slices), far(features))
        covariance = lax.all_to_all(partial, "row", split_axis=0, concat_axis=0, tiled=True)

    with jax.named_scope("diag"):
        far_out, _ = lax.optimization_barrier((far_out, partial[0, 0]))
        soon = [1, chips - 1]
        sent = {dz: send(dz) for dz in soon}
        covariance, sent = lax.optimization_barrier((covariance, sent))
        sent.update({dz: send(dz) for dz in far_chips if dz not in soon})
        got_blocks = got_blocks + [sent[dz] for dz in far_chips]

    with jax.named_scope("first"):
        base, d, pieces = pl.pallas_call(
            functools.partial(first_kernel, far_chips, col_count),
            in_specs=[SMEM, SMEM, VMEM] + [HBM] * 5,
            out_specs=[HBM, HBM, VMEM],
            out_shape=[tile_out, tile_out, shape(piece_shape, F32)],
            scratch_shapes=[
                tile_vmem, tile_vmem, tile_vmem, tile_vmem, sums, sems(1), sems(4, chunks),
            ],
            input_output_aliases={6: 0, 7: 1},
            compiler_params=PARAMS,
        )(
            my_list, live, covariance, far(near_sums), far(theta), far(tiles), far(base), far(d)
        )

    def diagonal(half, base, d, col_diag, before=()):
        operands = [my_list, far(base), far(d), col_diag]
        operands += [far(block) for block in got_blocks] + [far(x) for x in before]
        with jax.named_scope("diagonal"):
            return pl.pallas_call(
                functools.partial(diagonal_kernel, half),
                in_specs=[SMEM, HBM, HBM, VMEM] + [HBM] * (len(operands) - 4),
                out_specs=HBM,
                out_shape=tile_out,
                scratch_shapes=[
                    tile_vmem, tile_vmem, pltpu.VMEM(tile_shape, BF), tile_vmem,
                    sems(col_count), sems(3, slots // MANY),
                ],
                input_output_aliases={len(operands) - 1: 0} if before else {},
                compiler_params=PARAMS,
            )(*operands)

    for sweep in range(1, SWEEPS):
        last = sweep == SWEEPS - 1
        with jax.named_scope("exchange"):
            flat_shape = (row_count * columns, group, size)
            got = lax.all_to_all(pieces, "row", split_axis=0, concat_axis=0, tiled=True)
            t = diagonal(0, base, d, col_diag)
            got, t = lax.optimization_barrier((got, t))
            summed = pl.pallas_call(
                sum_kernel,
                in_specs=[VMEM, VMEM],
                out_specs=VMEM,
                out_shape=shape(flat_shape, F32),
                compiler_params=PARAMS,
            )(same, got.reshape(flat_shape))
            q = lax.all_to_all(
                summed.reshape(piece_shape), "row", split_axis=0, concat_axis=0, tiled=True
            )
            d, t, _ = lax.optimization_barrier((d, t, summed[0]))
            t = diagonal(1, base, d, col_diag, (t,))
        with jax.named_scope("sweep"):
            result = pl.pallas_call(
                functools.partial(sweep_kernel, last),
                in_specs=[SMEM, SMEM, HBM, HBM, HBM, VMEM],
                out_specs=[HBM] if last else [HBM, VMEM],
                out_shape=[tile_out] if last else [tile_out, shape(piece_shape, F32)],
                scratch_shapes=[
                    tile_vmem, tile_vmem, pltpu.VMEM((slots, size, 2 * size), BF), tile_vmem,
                    pltpu.VMEM((columns, 2 * size, 2 * size), BF), sems(4, slots // MANY),
                ] + ([] if last else [sums]),
                compiler_params=PARAMS,
            )(my_list, live, far(t), far(theta), far(pairs), q)
            d = result[0]
            if not last:
                pieces = result[1]
    return d.reshape(precision_tiles.shape)


def solution(mesh):
    return jax.shard_map(
        body,
        mesh=mesh,
        in_specs=(
            P("col", None, None),
            P("col", None, None),
            P("row", "col", None, None, None),
            P("row", "col", None, None, None),
            P(),
            P(),
            P(),
            P(),
        ),
        out_specs=P("row", "col", None, None, None),
        check_vma=False,
    )
```
